32 devices in a mesh: lat: 8 (over z, y), depth: 4 (over x, core).
Axes of the slice: x: 2, y: 2, z: 4, core: 2. Of those that a mesh axis runs over, the one named last changes fastest.
Arguments:
- grade_field: float32 [64, 128, 2048], P('depth', 'lat'), may hold values from 0 to 1
- amplitude: float32 [64, 128, 2048], P('depth', 'lat'), may hold values from -6 to 6
- tf_table: int32 [4, 128], replicated, may hold values from 0 to 65535
- brick_mask: int32 [8, 16, 8], P('depth', 'lat'), may hold values 0 or 1
Outputs:
- frame: float32 [4, 128, 2048], P(None, 'lat', 'depth')
The draws below stay inside these ranges and needn't reach their ends.
All inputs are finite; a program needn't handle non-finite values. No bound on the sum of `brick_mask` on one device may be relied on, other than what follows from the above.
Results may differ from the reference program's by a relative error of at most 0.00073.
Values sent between devices are 32-bit elements; how exact they have to be, the bound alone decides.
No kernel may reach another device: no remote copies, remote signals or barrier semaphores. Data moves between devices by JAX's collectives and lax.ppermute only.
A program may use at most 128 MiB of HBM per device.

```python
import jax
import jax.numpy as jnp
from jax import lax

NB = 128
MZ = 8
MX = 8
MY = 256
NZ = 64
NX = 128
NY = 2048


def set_ends(values, own_key, least, top_value):
    place = [jax.random.randint(jax.random.fold_in(own_key, axis), (), 0, length) for axis, length in enumerate(values.shape)]
    widest = values.shape.index(max(values.shape))
    beside = place[:widest] + [(place[widest] + 1) % values.shape[widest]] + place[widest + 1:]
    return values.at[tuple(place)].set(least).at[tuple(beside)].set(top_value)


def steps_of(key, dims, split, smallest, largest):
    loudness, own = 1.0, jax.random.fold_in(key, 6)
    for dim, parts in split:
        steps = jnp.exp(jax.random.uniform(jax.random.fold_in(own, dim), (parts,), jnp.float32, smallest / len(split), largest / len(split)))
        loudness = loudness * jnp.repeat(steps, dims[dim] // parts).reshape([-1 if axis == dim else 1 for axis in range(len(dims))])
    return loudness


def noise(rng, shape, scale, limit, cuts=(), dtype=jnp.bfloat16):
    factor_of = steps_of(rng, shape, cuts, -0.22, 0.18) if cuts else 1.0
    array = jax.random.normal(rng, shape, jnp.float32) * scale * factor_of
    return jnp.minimum(jnp.maximum(array, -limit), limit).astype(dtype)


def setup_inputs(seed: int = 0) -> dict:
    seeds = jax.random.split(jax.random.key(seed), 5)
    return {
        "grade_field": jnp.clip(1.0 * jax.random.uniform(seeds[0], (NZ, NX, NY), jnp.float32) ** steps_of(seeds[0], (NZ, NX, NY), ((0, 4), (1, 8)), -0.2, 0.2), 0.0, 1.0),
        "amplitude": noise(seeds[1], (NZ, NX, NY), 1.0, 6.0, ((0, 4), (1, 8)), jnp.float32),
        "tf_table": set_ends(jax.random.randint(seeds[2], (4, NB), 0, 65536), jax.random.fold_in(seeds[2], 1), 0, 65535).astype(jnp.int32),
        "brick_mask": set_ends((jax.random.randint(seeds[3], (NZ // MZ, NX // MX, NY // MY), 0, 2) < 1).astype(jnp.int32), jax.random.fold_in(seeds[3], 1), 0, 1),
    }


def table_lookup(grade_flat, table_scaled, bin_count):
    bin_points = jnp.arange(bin_count).astype(jnp.float32)[:, None]
    position = grade_flat[None, :] * (bin_count - 1.0)
    hat_weights = jnp.maximum(0.0, 1.0 - jnp.abs(position - bin_points)).astype(jnp.bfloat16)
    return jnp.dot(table_scaled, hat_weights, preferred_element_type=jnp.float32)

def stencil(lower_two, lower_one, upper_one, upper_two):
    return (lower_two - 8.0 * lower_one + 8.0 * upper_one - upper_two) / 12.0

def reference(grade_field, amplitude, tf_table, brick_mask):
    table_scaled = (tf_table.astype(jnp.float32) / 65535.0).astype(jnp.bfloat16)
    stacked = jnp.stack([grade_field, amplitude])
    padded = jnp.pad(stacked, ((0, 0), (2, 2), (2, 2), (2, 2)))
    opacity_scale = 4.0 / NZ

    def one_slice(state_pair, level_index):
        color_sum, log_trans = state_pair
        window = lax.dynamic_slice_in_dim(padded, level_index, 5, 1)
        grad_z = stencil(window[:, 0, 2:-2, 2:-2], window[:, 1, 2:-2, 2:-2], window[:, 3, 2:-2, 2:-2], window[:, 4, 2:-2, 2:-2])
        middle = window[:, 2]
        grad_x = stencil(middle[:, 0:-4, 2:-2], middle[:, 1:-3, 2:-2], middle[:, 3:-1, 2:-2], middle[:, 4:, 2:-2])
        grad_y = stencil(middle[:, 2:-2, 0:-4], middle[:, 2:-2, 1:-3], middle[:, 2:-2, 3:-1], middle[:, 2:-2, 4:])
        classes = table_lookup(middle[0, 2:-2, 2:-2].reshape(-1), table_scaled, NB).reshape(4, NX, NY)
        block_row = lax.dynamic_index_in_dim(brick_mask, level_index // MZ, 0, keepdims=False)
        cover_mask = jnp.broadcast_to(block_row[:, None, :, None], (NX // MX, MX, NY // MY, MY)).reshape(NX, NY).astype(jnp.float32)
        edge_weight = 1.0 - 1.0 / jnp.sqrt(grad_x[1] * grad_x[1] + grad_y[1] * grad_y[1] + grad_z[1] * grad_z[1] + 1.0)
        opacity = opacity_scale * classes[3] * edge_weight * cover_mask
        normal_len = jnp.sqrt(grad_x[0] * grad_x[0] + grad_y[0] * grad_y[0] + grad_z[0] * grad_z[0] + 0.25)
        shading = 0.3 + 0.7 * jnp.abs(grad_z[0]) / normal_len
        colors = classes[0:3] * shading[None]
        color_sum = color_sum + (jnp.exp(log_trans) * opacity)[None] * colors
        log_trans = log_trans + jnp.log1p(-opacity)
        return ((color_sum, log_trans), None)
    start = (jnp.zeros((3, NX, NY), jnp.float32), jnp.zeros((NX, NY), jnp.float32))
    final_pair, unused = lax.scan(one_slice, start, jnp.arange(NZ).astype(jnp.int32))
    color_sum, log_trans = final_pair
    return jnp.concatenate([color_sum, (1.0 - jnp.exp(log_trans))[None]], 0)
```

```python
import functools

import jax
import jax.numpy as jnp
from jax import lax
from jax.experimental import pallas as pl
from jax.experimental.pallas import tpu as pltpu
from jax.sharding import PartitionSpec as P

MZ = 8
MX = 8
MY = 256
LANES = 128
SUB = 8
TOP = 8


def pack_kernel(grade_ref, amp_ref, up_ref, down_ref, front_ref, back_ref):
    slices, rows = grade_ref.shape[:2]
    for f, ref in enumerate((grade_ref, amp_ref)):
        for z in range(slices):
            at = 2 * (z % 4)
            up_ref[f, z // 4, at:at + 2, :] = ref[z, rows - 2:rows, :]
            down_ref[f, z // 4, at:at + 2, :] = ref[z, 0:2, :]
        front_ref[f] = ref[slices - 2:slices]
        back_ref[f] = ref[0:2]


def round_weight(w):
    return w.astype(jnp.bfloat16).astype(jnp.float32)


def march_kernel(scale, pieces, mask_ref, rank_ref, grade_hbm, amp_hbm, above_ref, below_ref, front_hbm,
                 back_hbm, table_ref, *rest):
    outs, (grid_g, grid_a, acc_ref, low_ref, high_ref, sems) = rest[:pieces], rest[pieces:]
    slices, rows, cols = grade_hbm.shape
    strips = cols // LANES
    copies = []
    for f, (src, grid) in enumerate(((grade_hbm, grid_g), (amp_hbm, grid_a))):
        for s in range(strips):
            lanes = pl.ds(s * LANES, LANES)
            body = pl.ds(TOP, rows)
            trio = (
                (src.at[:, :, lanes], grid.at[pl.ds(2, slices), s + 1, body, :]),
                (front_hbm.at[f, :, :, lanes], grid.at[pl.ds(0, 2), s + 1, body, :]),
                (back_hbm.at[f, :, :, lanes], grid.at[pl.ds(slices + 2, 2), s + 1, body, :]),
            )
            for k, (here, there) in enumerate(trio):
                copies.append(pltpu.make_async_copy(here, there, sems.at[f, s, k]))
    for copy in copies:
        copy.start()
    for f, grid in enumerate((grid_g, grid_a)):
        zero = jnp.zeros((rows, LANES), jnp.float32)
        for z in range(slices):
            grid[z + 2, 0, TOP:TOP + rows, :] = zero
            grid[z + 2, strips + 1, TOP:TOP + rows, :] = zero
            at = 2 * (z % 4)
            for s in range(strips):
                lanes = slice(s * LANES, (s + 1) * LANES)
                grid[z + 2, s + 1, TOP - 2:TOP, :] = above_ref[f, z // 4, at:at + 2, lanes]
                grid[z + 2, s + 1, TOP + rows:TOP + rows + 2, :] = below_ref[f, z // 4, at:at + 2, lanes]
    bins = table_ref.shape[1]
    table = (table_ref[...].astype(jnp.float32) / 65535.0).astype(jnp.bfloat16).astype(jnp.float32)
    row = lax.broadcasted_iota(jnp.int32, table.shape, 0)
    table = jnp.where(row == 3, table * scale, table)
    column = lax.broadcasted_iota(jnp.int32, table.shape, 1)
    following = jnp.where(column == bins - 1, 0.0, pltpu.roll(table, bins - 1, 1))
    for c in range(4):
        low_ref[c] = jnp.broadcast_to(table[c:c + 1, :], (SUB, bins))
        high_ref[c] = jnp.broadcast_to(following[c:c + 1, :], (SUB, bins))
    for copy in copies:
        copy.wait()
    lane = lax.broadcasted_iota(jnp.int32, (SUB, LANES), 1)
    per_block = MY // LANES
    piece_blocks = cols // pieces // MY

    def gather(ref, c, index):
        return jnp.take_along_axis(ref[c], index, axis=1)

    def stencil(m2, m1, p1, p2):
        return (m2 - p2) + 8.0 * (p1 - m1)

    def derivs(grid, z, s, r0):
        mid = grid[z, s, r0:r0 + SUB, :]
        left = grid[z, s - 1, r0:r0 + SUB, :]
        right = grid[z, s + 1, r0:r0 + SUB, :]
        dy = stencil(
            pltpu.roll(jnp.where(lane >= LANES - 2, left, mid), 2, 1),
            pltpu.roll(jnp.where(lane >= LANES - 1, left, mid), 1, 1),
            pltpu.roll(jnp.where(lane < 1, right, mid), LANES - 1, 1),
            pltpu.roll(jnp.where(lane < 2, right, mid), LANES - 2, 1),
        )
        dz = stencil(*(grid[z + k, s, r0:r0 + SUB, :] for k in (-2, -1, 1, 2)))
        dx = stencil(*(grid[z, s, r0 + k:r0 + k + SUB, :] for k in (-2, -1, 1, 2)))
        return mid, dx * dx + dy * dy + dz * dz, dz

    def block(cb, carry):
        owner = lax.bitwise_xor(cb // piece_blocks, rank_ref[0])
        lanes = pl.ds(pl.multiple_of(lax.rem(cb, piece_blocks) * MY, MY), MY)
        for rt in range(rows // MX):
            r0 = TOP + rt * MX
            for j in range(per_block):
                for c in range(3):
                    acc_ref[j, c] = jnp.zeros((SUB, LANES), jnp.float32)
                acc_ref[j, 3] = jnp.ones((SUB, LANES), jnp.float32)
            for zb in range(slices // MZ):
                @pl.when(mask_ref[zb, rt, cb] != 0)
                def _():
                    for j in range(per_block):
                        s = cb * per_block + j + 1
                        red, green, blue, trans = (acc_ref[j, c] for c in range(4))
                        for zi in range(MZ):
                            z = 2 + zb * MZ + zi
                            grade, g_sq, gz = derivs(grid_g, z, s, r0)
                            _, a_sq, _ = derivs(grid_a, z, s, r0)
                            edge = 1.0 - 12.0 * lax.rsqrt(a_sq + 144.0)
                            shade = 0.3 + 0.7 * (jnp.abs(gz) * lax.rsqrt(g_sq + 36.0))
                            position = grade * (bins - 1.0)
                            index = jnp.minimum(position.astype(jnp.int32), bins - 1)
                            w_low = 1.0 - (position - index.astype(jnp.float32))
                            w_high = round_weight(1.0 - w_low)
                            w_low = round_weight(w_low)
                            cls = [
                                w_low * gather(low_ref, c, index) + w_high * gather(high_ref, c, index)
                                for c in range(4)
                            ]
                            weight = trans * (cls[3] * edge)
                            trans = trans - weight
                            weight = weight * shade
                            red = red + weight * cls[0]
                            green = green + weight * cls[1]
                            blue = blue + weight * cls[2]
                        for c, value in enumerate((red, green, blue, trans)):
                            acc_ref[j, c] = value
            for k in range(pieces):
                @pl.when(owner == k)
                def _():
                    for c in range(4):
                        value = jnp.concatenate([acc_ref[j, c] for j in range(per_block)], axis=1)
                        outs[k][c, rt * SUB:(rt + 1) * SUB, lanes] = value
        return carry

    lax.fori_loop(0, cols // MY, block, 0)


def shift(x, axis, step):
    size = lax.axis_size(axis)
    return lax.ppermute(x, axis, [(i, i + step) for i in range(size) if 0 <= i + step < size])


def local(grade_field, amplitude, tf_table, brick_mask):
    slices, rows, cols = grade_field.shape
    pieces = lax.axis_size("depth")
    rank = lax.axis_index("depth")
    scale = 4.0 / (slices * pieces)
    strips = cols // LANES
    f32 = jnp.float32
    vmem = pl.BlockSpec(memory_space=pltpu.VMEM)
    smem = pl.BlockSpec(memory_space=pltpu.SMEM)
    hbm = pl.BlockSpec(memory_space=pl.ANY)
    big = pltpu.CompilerParams(vmem_limit_bytes=48 << 20)
    lat_halo = jax.ShapeDtypeStruct((2, slices // 4, SUB, cols), f32)
    depth_halo = jax.ShapeDtypeStruct((2, 2, rows, cols), f32)
    up, down, front, back = pl.pallas_call(
        pack_kernel,
        out_shape=(lat_halo, lat_halo, depth_halo, depth_halo),
        in_specs=[vmem, vmem],
        out_specs=[vmem] * 4,
        compiler_params=big,
        name="pack",
    )(grade_field, amplitude)
    above = shift(up, "lat", 1)
    below = shift(down, "lat", -1)
    front = shift(front, "depth", 1)
    back = shift(back, "depth", -1)
    piece = jax.ShapeDtypeStruct((4, rows, cols // pieces), f32)
    grid = pltpu.VMEM((slices + 4, strips + 2, TOP + rows + SUB, LANES), f32)
    parts = pl.pallas_call(
        functools.partial(march_kernel, scale, pieces),
        out_shape=(piece,) * pieces,
        in_specs=[smem, smem, hbm, hbm, vmem, vmem, hbm, hbm, vmem],
        out_specs=[vmem] * pieces,
        scratch_shapes=[
            grid,
            grid,
            pltpu.VMEM((MY // LANES, 4, SUB, LANES), f32),
            pltpu.VMEM((4, SUB, tf_table.shape[1]), f32),
            pltpu.VMEM((4, SUB, tf_table.shape[1]), f32),
            pltpu.SemaphoreType.DMA((2, strips, 3)),
        ],
        compiler_params=big,
        name="march",
    )(brick_mask, rank.reshape(1).astype(jnp.int32), grade_field, amplitude, above, below, front, back, tf_table)
    held = [parts[0]] + [
        lax.ppermute(parts[k], "depth", [(i, i ^ k) for i in range(pieces)]) for k in range(1, pieces)
    ]
    level = 0
    while len(held) > 1:
        first = (rank >> level) % 2 == 0
        merged = []
        for mine, other in zip(held[0::2], held[1::2]):
            ahead = jnp.where(first, mine, other)
            behind = jnp.where(first, other, mine)
            rgb = ahead[0:3] + ahead[3:4] * behind[0:3]
            merged.append(jnp.concatenate([rgb, ahead[3:4] * behind[3:4]], 0))
        held = merged
        level += 1
    return jnp.concatenate([held[0][0:3], 1.0 - held[0][3:4]], 0)


def solution(mesh):
    placed = (P("depth", "lat", None), P("depth", "lat", None), P(), P("depth", "lat", None))
    return jax.shard_map(
        local, mesh=mesh, in_specs=placed, out_specs=P(None, "lat", "depth"), check_vma=False
    )
```

```python
import functools

import jax
import jax.numpy as jnp
from jax import lax
from jax.experimental import pallas as pl
from jax.experimental.pallas import tpu as pltpu
from jax.sharding import PartitionSpec as P

MZ = 8
MX = 8
MY = 256
LANES = 128
SUB = 8
TOP = 8
TERMS = 9


def sublane(shape):
    return lax.broadcasted_iota(jnp.int32, shape, len(shape) - 2)


def pack_kernel(lat_ref, depth_ref, grade_hbm, amp_hbm, pair_ref, cross_ref, near_hbm, far_hbm, held, sems, depth_sems):
    slices, rows, cols = grade_hbm.shape
    fields = (grade_hbm, amp_hbm)
    loads = {}
    for k in range(4):
        for f, src in enumerate(fields):
            for q in range(4):
                z = k + 4 * q
                loads[f, z] = pltpu.make_async_copy(src.at[z], held.at[f, z], sems.at[f, z])
                loads[f, z].start()
    odd_depth = lax.rem(depth_ref[0], 2)
    last, first = (1 - odd_depth) * (slices - 2), odd_depth * (slices - 2)
    others = []
    for f, src in enumerate(fields):
        others.append(pltpu.make_async_copy(src.at[pl.ds(last, 2)], near_hbm.at[f], depth_sems.at[f, 0]))
        others.append(pltpu.make_async_copy(src.at[pl.ds(first, 2)], far_hbm.at[f], depth_sems.at[f, 1]))
    for copy in others:
        copy.start()
    sub = sublane((SUB, cols))
    odd_row = lax.rem(sub, 2) == 1
    is_even = jnp.broadcast_to(lax.rem(lat_ref[0], 2), (SUB, cols)) == 0
    for k in range(4):
        for f in range(2):
            for q in range(4):
                loads[f, k + 4 * q].wait()
            high = [held[f, k + 4 * q, rows - SUB:rows, :] for q in range(4)]
            low = [held[f, k + 4 * q, 0:SUB, :] for q in range(4)]
            raw = jnp.where(
                sub < 4,
                jnp.where(sub < 2, pltpu.roll(high[0], 2, 0), pltpu.roll(high[3], 4, 0)),
                jnp.where(sub < 6, pltpu.roll(high[2], 6, 0), high[1]),
            )
            above = jnp.where(odd_row, raw, raw - 8.0 * pltpu.roll(raw, SUB - 1, 0))
            raw = jnp.where(
                sub < 4,
                jnp.where(sub < 2, low[3], pltpu.roll(low[2], 2, 0)),
                jnp.where(sub < 6, pltpu.roll(low[1], 4, 0), pltpu.roll(low[0], 6, 0)),
            )
            below = jnp.where(odd_row, 8.0 * pltpu.roll(raw, 1, 0) - raw, -raw)
            pair_ref[f, k] = jnp.where(is_even, above, below)
            cross_ref[f, k] = jnp.where(is_even, below, above)
    for copy in others:
        copy.wait()


def round_weight(w):
    return w.astype(jnp.bfloat16).astype(jnp.float32)


def march_kernel(scale, pieces, mask_ref, depth_ref, grade_hbm, amp_hbm, near_hbm, far_hbm, table_ref, *rest):
    outs, kept_ref = rest[:pieces], rest[pieces]
    grid_g, grid_a, acc_ref, low_ref, high_ref, sems = rest[pieces + 1:]
    slices, rows, cols = grade_hbm.shape
    strips = cols // LANES
    fields = ((grade_hbm, grid_g), (amp_hbm, grid_a))
    body = pl.ds(TOP, rows)
    odd_depth = lax.rem(depth_ref[0], 2)
    near_at = (1 - odd_depth) * (slices + 2)
    far_at = odd_depth * (slices + 2)

    def copies(s):
        lanes = pl.ds(s * LANES, LANES) if isinstance(s, int) else pl.ds(pl.multiple_of(s * LANES, LANES), LANES)
        made = []
        for f, (src, grid) in enumerate(fields):
            trio = (
                (src.at[:, :, lanes], grid.at[pl.ds(2, slices), s + 1, body, :]),
                (near_hbm.at[f, :, :, lanes], grid.at[pl.ds(near_at, 2), s + 1, body, :]),
                (far_hbm.at[f, :, :, lanes], grid.at[pl.ds(far_at, 2), s + 1, body, :]),
            )
            made += [pltpu.make_async_copy(here, there, sems.at[f, s, k]) for k, (here, there) in enumerate(trio)]
        return made

    for s in range(strips):
        for copy in copies(s):
            copy.start()
    zero = jnp.zeros((SUB, LANES), jnp.float32)
    for _, grid in fields:
        for z in range(slices):
            for r in range(0, rows, SUB):
                grid[z + 2, 0, TOP + r:TOP + r + SUB, :] = zero
                grid[z + 2, strips + 1, TOP + r:TOP + r + SUB, :] = zero
            for s in range(strips):
                grid[z + 2, s + 1, 0:TOP, :] = zero
                grid[z + 2, s + 1, TOP + rows:TOP + rows + SUB, :] = zero
    bins = table_ref.shape[1]
    table = (table_ref[...].astype(jnp.float32) / 65535.0).astype(jnp.bfloat16).astype(jnp.float32)
    table = jnp.where(sublane(table.shape) == 3, table * scale, table)
    column = lax.broadcasted_iota(jnp.int32, table.shape, 1)
    following = jnp.where(column == bins - 1, 0.0, pltpu.roll(table, bins - 1, 1))
    for c in range(4):
        low_ref[c] = jnp.broadcast_to(table[c:c + 1, :], (SUB, bins))
        high_ref[c] = jnp.broadcast_to(following[c:c + 1, :], (SUB, bins))
    lane = lax.broadcasted_iota(jnp.int32, (SUB, LANES), 1)
    per_block = MY // LANES
    piece_blocks = cols // pieces // MY

    def gather(ref, c, index):
        return jnp.take_along_axis(ref[c], index, axis=1)

    def stencil(m2, m1, p1, p2):
        return (m2 - p2) + 8.0 * (p1 - m1)

    def derivs(grid, z, s, r0):
        mid = grid[z, s, r0:r0 + SUB, :]
        left = grid[z, s - 1, r0:r0 + SUB, :]
        right = grid[z, s + 1, r0:r0 + SUB, :]
        dy = stencil(
            pltpu.roll(jnp.where(lane >= LANES - 2, left, mid), 2, 1),
            pltpu.roll(jnp.where(lane >= LANES - 1, left, mid), 1, 1),
            pltpu.roll(jnp.where(lane < 1, right, mid), LANES - 1, 1),
            pltpu.roll(jnp.where(lane < 2, right, mid), LANES - 2, 1),
        )
        dz = stencil(*(grid[z + k, s, r0:r0 + SUB, :] for k in (-2, -1, 1, 2)))
        dx = stencil(*(grid[z, s, r0 + k:r0 + k + SUB, :] for k in (-2, -1, 1, 2)))
        return mid, dx, dy * dy + dz * dz, dz

    def block(cb, carry):
        @pl.when(cb == 0)
        def _():
            for copy in copies(0):
                copy.wait()

        for j in range(1, per_block + 1):
            @pl.when(cb * per_block + j < strips)
            def _():
                for copy in copies(cb * per_block + j):
                    copy.wait()

        owner = lax.bitwise_xor(cb // piece_blocks, depth_ref[0])
        lanes = pl.ds(pl.multiple_of(lax.rem(cb, piece_blocks) * MY, MY), MY)
        for rt in range(rows // MX):
            r0 = TOP + rt * MX
            edge_rows = slice(0, 2) if rt == 0 else slice(SUB - 2, SUB)
            for j in range(per_block):
                for c in range(3):
                    acc_ref[j, c] = zero
                acc_ref[j, 3] = zero + 1.0
            for zb in range(slices // MZ):
                at = ((0, 4), (6, 2))[rt][zb]

                @pl.when(mask_ref[zb, rt, cb] != 0)
                def _():
                    for j in range(per_block):
                        s = cb * per_block + j + 1
                        red, green, blue, trans = (acc_ref[j, c] for c in range(4))
                        for zi in range(MZ):
                            z = 2 + zb * MZ + zi
                            grade, g_x, g_yz, g_z = derivs(grid_g, z, s, r0)
                            _, a_x, a_yz, _ = derivs(grid_a, z, s, r0)
                            g_yz = g_yz + 36.0
                            a_yz = a_yz + 144.0
                            steep = 0.7 * jnp.abs(g_z)
                            position = grade * (bins - 1.0)
                            index = jnp.minimum(position.astype(jnp.int32), bins - 1)
                            w_low = 1.0 - (position - index.astype(jnp.float32))
                            w_high = round_weight(1.0 - w_low)
                            w_low = round_weight(w_low)
                            cls = [
                                w_low * gather(low_ref, c, index) + w_high * gather(high_ref, c, index)
                                for c in range(4)
                            ]
                            for n, term in enumerate((g_x, a_x, g_yz, a_yz, steep, *cls)):
                                kept_ref[zi, s - 1, n, at:at + 2, :] = term[edge_rows, :]
                            edge = 1.0 - 12.0 * lax.rsqrt(a_x * a_x + a_yz)
                            shade = 0.3 + steep * lax.rsqrt(g_x * g_x + g_yz)
                            weight = trans * (cls[3] * edge)
                            trans = trans - weight
                            weight = weight * shade
                            red = red + weight * cls[0]
                            green = green + weight * cls[1]
                            blue = blue + weight * cls[2]
                        for c, value in enumerate((red, green, blue, trans)):
                            acc_ref[j, c] = value
            for k in range(pieces):
                @pl.when(owner == k)
                def _():
                    for c in range(4):
                        for j in range(per_block):
                            part = pl.ds(pl.multiple_of(lax.rem(cb, piece_blocks) * MY + j * LANES, LANES), LANES)
                            outs[k][c, rt * SUB:(rt + 1) * SUB, part] = acc_ref[j, c]
        return carry

    lax.fori_loop(0, cols // MY, block, 0)


def edge_kernel(pieces, mask_ref, depth_ref, lat_ref, kept_ref, pair_ref, cross_ref, *outs):
    half = kept_ref.shape[0]
    strips = kept_ref.shape[1]
    sub = sublane((SUB, LANES))
    is_first = lax.rem((sub + 2) // 4, 2) == 0
    odd_lat = jnp.broadcast_to(lax.rem(lat_ref[0], 2), (SUB, LANES))
    from_pair = lax.rem(sub // 2, 2) != odd_lat
    piece_strips = strips // pieces
    packs = piece_strips // 2

    def halo(f, zi, lanes):
        pair, cross = pair_ref[f, zi % 4, :, lanes], cross_ref[f, zi % 4, :, lanes]
        if zi < 4:
            return jnp.where(from_pair, pair, cross)
        return pltpu.roll(jnp.where(from_pair, cross, pair), 2, 0)

    def strip(s):
        lanes = pl.ds(pl.multiple_of(s * LANES, LANES), LANES)
        cb = s // (MY // LANES)
        full = [[jnp.broadcast_to(mask_ref[zb, rt, cb], (SUB, LANES)) for rt in range(2)] for zb in range(2)]
        live = jnp.where(
            sub < 4, jnp.where(sub < 2, full[0][0], full[1][1]), jnp.where(sub < 6, full[1][0], full[0][1])
        ) != 0
        zero = jnp.zeros((SUB, LANES), jnp.float32)
        total = [zero, zero, zero]
        trans = zero + 1.0
        for zi in range(half):
            g_x, a_x, g_yz, a_yz, steep, red, green, blue, alpha = (kept_ref[zi, s, n] for n in range(TERMS))
            g_x = g_x + halo(0, zi, lanes)
            a_x = a_x + halo(1, zi, lanes)
            edge = 1.0 - 12.0 * lax.rsqrt(a_x * a_x + a_yz)
            shade = 0.3 + steep * lax.rsqrt(g_x * g_x + g_yz)
            weight = jnp.where(live, trans * (alpha * edge), 0.0)
            trans = trans - weight
            weight = weight * shade
            total = [t + jnp.where(live, weight * c, 0.0) for t, c in zip(total, (red, green, blue))]
        out = [t + trans * pltpu.roll(t, 4, 0) for t in total]
        return out + [trans * pltpu.roll(trans, 4, 0)]

    def piece(p, carry):
        results = [strip(p * piece_strips + j) for j in range(piece_strips)]
        owner = lax.bitwise_xor(p, depth_ref[0])
        for j in range(packs):
            packed = [
                jnp.where(is_first, one, pltpu.roll(two, 4, 0)) for one, two in zip(results[j], results[j + packs])
            ]
            for k in range(pieces):
                @pl.when(owner == k)
                def _():
                    for c in range(4):
                        outs[k][c, :, j * LANES:(j + 1) * LANES] = packed[c]
        return carry

    lax.fori_loop(0, pieces, piece, 0)


def fold(parts, rank):
    level = 0
    while len(parts) > 1:
        first = lax.rem(lax.shift_right_logical(rank, level), 2) == 0
        merged = []
        for mine, other in zip(parts[0::2], parts[1::2]):
            first_here = jnp.broadcast_to(first, mine[3].shape)
            clear = jnp.where(first_here, mine[3], other[3])
            merged.append(
                [jnp.where(first_here, m, o) + clear * jnp.where(first_here, o, m) for m, o in zip(mine[:3], other[:3])]
                + [mine[3] * other[3]]
            )
        parts = merged
        level += 1
    return parts[0][:3] + [1.0 - parts[0][3]]


def finish_kernel(pieces, depth_ref, *refs):
    inner, edges, out_ref = refs[:pieces], refs[pieces:2 * pieces], refs[-1]
    rows, cols = out_ref.shape[1:]
    rank = depth_ref[0]
    frame = fold([[ref[c] for c in range(4)] for ref in inner], rank)
    rim = fold([[ref[c] for c in range(4)] for ref in edges], rank)
    for c in range(4):
        packed = rim[c]
        wide = jnp.concatenate([packed, pltpu.roll(packed, 4, 0)], axis=1)
        sub = sublane(wide.shape)
        out_ref[c, 0:SUB, :] = jnp.where(sub < 2, wide, frame[c][0:SUB, :])
        out_ref[c, rows - SUB:rows, :] = jnp.where(sub >= SUB - 2, wide, frame[c][rows - SUB:rows, :])


def swap_near(x, axis):
    return lax.ppermute(x, axis, [(i, i ^ 1) for i in range(lax.axis_size(axis))])


def swap_far(x, axis):
    size = lax.axis_size(axis)
    return lax.ppermute(x, axis, [(i, j) for k in range(1, size - 1, 2) for i, j in ((k, k + 1), (k + 1, k))])


def local(grade_field, amplitude, tf_table, brick_mask):
    slices, rows, cols = grade_field.shape
    assert (slices, rows) == (2 * MZ, 2 * MX)
    pieces = lax.axis_size("depth")
    depth_rank = lax.axis_index("depth").astype(jnp.int32).reshape(1)
    lat_rank = lax.axis_index("lat").astype(jnp.int32).reshape(1)
    scale = 4.0 / (slices * pieces)
    strips = cols // LANES
    f32 = jnp.float32
    vmem = pl.BlockSpec(memory_space=pltpu.VMEM)
    smem = pl.BlockSpec(memory_space=pltpu.SMEM)
    hbm = pl.BlockSpec(memory_space=pltpu.MemorySpace.HBM)
    lat_halo = jax.ShapeDtypeStruct((2, slices // 4, SUB, cols), f32)
    depth_halo = jax.ShapeDtypeStruct((2, 2, rows, cols), f32)
    pair, cross, near, far = pl.pallas_call(
        pack_kernel,
        out_shape=(lat_halo, lat_halo, depth_halo, depth_halo),
        in_specs=[smem, smem, hbm, hbm],
        out_specs=[vmem, vmem, hbm, hbm],
        scratch_shapes=[
            pltpu.VMEM((2, slices, rows, cols), f32),
            pltpu.SemaphoreType.DMA((2, slices)),
            pltpu.SemaphoreType.DMA((2, 2)),
        ],
        compiler_params=pltpu.CompilerParams(vmem_limit_bytes=16 << 20),
        name="pack",
    )(lat_rank, depth_rank, grade_field, amplitude)
    pair = swap_near(pair, "lat")
    cross = swap_far(cross, "lat")
    near = swap_near(near, "depth")
    far = swap_far(far, "depth")
    piece = jax.ShapeDtypeStruct((4, rows, cols // pieces), f32)
    kept = jax.ShapeDtypeStruct((MZ, strips, TERMS, SUB, LANES), f32)
    grid = pltpu.VMEM((slices + 4, strips + 2, TOP + rows + SUB, LANES), f32)
    table = pltpu.VMEM((4, SUB, tf_table.shape[1]), f32)
    *parts, kept = pl.pallas_call(
        functools.partial(march_kernel, scale, pieces),
        out_shape=(piece,) * pieces + (kept,),
        in_specs=[smem, smem, hbm, hbm, hbm, hbm, vmem],
        out_specs=[vmem] * (pieces + 1),
        scratch_shapes=[
            grid,
            grid,
            pltpu.VMEM((MY // LANES, 4, SUB, LANES), f32),
            table,
            table,
            pltpu.SemaphoreType.DMA((2, strips, 3)),
        ],
        compiler_params=pltpu.CompilerParams(vmem_limit_bytes=24 << 20),
        name="march",
    )(brick_mask, depth_rank, grade_field, amplitude, near, far, tf_table)

    def exchange(parts):
        return [parts[0]] + [
            lax.ppermute(parts[k], "depth", [(i, i ^ k) for i in range(pieces)]) for k in range(1, pieces)
        ]

    inner = exchange(parts)
    rim = jax.ShapeDtypeStruct((4, SUB, cols // pieces // 2), f32)
    rims = pl.pallas_call(
        functools.partial(edge_kernel, pieces),
        out_shape=(rim,) * pieces,
        in_specs=[smem, smem, smem, vmem, vmem, vmem],
        out_specs=[vmem] * pieces,
        compiler_params=pltpu.CompilerParams(vmem_limit_bytes=16 << 20),
        name="edges",
    )(brick_mask, depth_rank, lat_rank, kept, pair, cross)
    edges = exchange(rims)
    return pl.pallas_call(
        functools.partial(finish_kernel, pieces),
        out_shape=piece,
        in_specs=[smem] + [vmem] * (2 * pieces),
        out_specs=vmem,
        compiler_params=pltpu.CompilerParams(vmem_limit_bytes=4 << 20),
        name="finish",
    )(depth_rank, *inner, *edges)


def solution(mesh):
    placed = (P("depth", "lat", None), P("depth", "lat", None), P(), P("depth", "lat", None))
    return jax.shard_map(
        local, mesh=mesh, in_specs=placed, out_specs=P(None, "lat", "depth"), check_vma=False
    )
```

```python
import functools

import jax
import jax.numpy as jnp
from jax import lax
from jax.experimental import pallas as pl
from jax.experimental.pallas import tpu as pltpu
from jax.sharding import PartitionSpec as P

MZ = 8
MX = 8
MY = 256
LANES = 128
SUB = 8
TOP = 8
TERMS = 9


def sublane(shape):
    return lax.broadcasted_iota(jnp.int32, shape, len(shape) - 2)


def rows_kernel(lat_ref, grade_hbm, amp_hbm, pair_hbm, cross_hbm, sems):
    slices, rows = grade_hbm.shape[:2]
    span = slices // 4
    even = lax.rem(lat_ref[0], 2) == 0

    def copies(above_dst, below_dst):
        made = []
        for f, src in enumerate((grade_hbm, amp_hbm)):
            for q in range(4):
                part = src.at[pl.ds(span * q, span)]
                above = above_dst.at[f, :, pl.ds((0, 6, 4, 2)[q], 2), :]
                below = below_dst.at[f, :, pl.ds((6, 4, 2, 0)[q], 2), :]
                made.append(pltpu.make_async_copy(part.at[:, pl.ds(rows - 2, 2), :], above, sems.at[f, q, 0]))
                made.append(pltpu.make_async_copy(part.at[:, pl.ds(0, 2), :], below, sems.at[f, q, 1]))
        for copy in made:
            copy.start()
        for copy in made:
            copy.wait()

    @pl.when(even)
    def _():
        copies(pair_hbm, cross_hbm)

    @pl.when(jnp.logical_not(even))
    def _():
        copies(cross_hbm, pair_hbm)


def slices_kernel(depth_ref, grade_hbm, amp_hbm, near_hbm, far_hbm, sems):
    slices = grade_hbm.shape[0]
    odd = lax.rem(depth_ref[0], 2)
    made = []
    for f, src in enumerate((grade_hbm, amp_hbm)):
        for n, (dst, at) in enumerate(((near_hbm, 1 - odd), (far_hbm, odd))):
            made.append(pltpu.make_async_copy(src.at[pl.ds(at * (slices - 2), 2)], dst.at[f], sems.at[f, n]))
    for copy in made:
        copy.start()
    for copy in made:
        copy.wait()


def round_weight(w):
    return w.astype(jnp.bfloat16).astype(jnp.float32)


def march_kernel(scale, pieces, mask_ref, depth_ref, grade_hbm, amp_hbm, near_hbm, far_hbm, table_ref, *rest):
    outs, kept_ref = rest[:pieces], rest[pieces]
    grid_g, grid_a, acc_ref, low_ref, high_ref, sems = rest[pieces + 1:]
    slices, rows, cols = grade_hbm.shape
    strips = cols // LANES
    fields = ((grade_hbm, grid_g), (amp_hbm, grid_a))
    body = pl.ds(TOP, rows)
    odd_depth = lax.rem(depth_ref[0], 2)
    near_at = (1 - odd_depth) * (slices + 2)
    far_at = odd_depth * (slices + 2)

    def copies(s):
        lanes = pl.ds(s * LANES, LANES) if isinstance(s, int) else pl.ds(pl.multiple_of(s * LANES, LANES), LANES)
        made = []
        for f, (src, grid) in enumerate(fields):
            trio = (
                (src.at[:, :, lanes], grid.at[pl.ds(2, slices), s + 1, body, :]),
                (near_hbm.at[f, :, :, lanes], grid.at[pl.ds(near_at, 2), s + 1, body, :]),
                (far_hbm.at[f, :, :, lanes], grid.at[pl.ds(far_at, 2), s + 1, body, :]),
            )
            made += [pltpu.make_async_copy(here, there, sems.at[f, s, k]) for k, (here, there) in enumerate(trio)]
        return made

    for s in range(strips):
        for copy in copies(s):
            copy.start()
    zero = jnp.zeros((SUB, LANES), jnp.float32)
    for _, grid in fields:
        for z in range(slices):
            for r in range(0, rows, SUB):
                grid[z + 2, 0, TOP + r:TOP + r + SUB, :] = zero
                grid[z + 2, strips + 1, TOP + r:TOP + r + SUB, :] = zero
            for s in range(strips):
                grid[z + 2, s + 1, 0:TOP, :] = zero
                grid[z + 2, s + 1, TOP + rows:TOP + rows + SUB, :] = zero
    bins = table_ref.shape[1]
    table = (table_ref[...].astype(jnp.float32) / 65535.0).astype(jnp.bfloat16).astype(jnp.float32)
    table = jnp.where(sublane(table.shape) == 3, table * scale, table)
    column = lax.broadcasted_iota(jnp.int32, table.shape, 1)
    following = jnp.where(column == bins - 1, 0.0, pltpu.roll(table, bins - 1, 1))
    for c in range(4):
        low_ref[c] = jnp.broadcast_to(table[c:c + 1, :], (SUB, bins))
        high_ref[c] = jnp.broadcast_to(following[c:c + 1, :], (SUB, bins))
    lane = lax.broadcasted_iota(jnp.int32, (SUB, LANES), 1)
    per_block = MY // LANES
    piece_blocks = cols // pieces // MY

    def gather(ref, c, index):
        return jnp.take_along_axis(ref[c], index, axis=1)

    def stencil(m2, m1, p1, p2):
        return (m2 - p2) + 8.0 * (p1 - m1)

    def derivs(grid, z, s, r0):
        mid = grid[z, s, r0:r0 + SUB, :]
        left = grid[z, s - 1, r0:r0 + SUB, :]
        right = grid[z, s + 1, r0:r0 + SUB, :]
        dy = stencil(
            pltpu.roll(jnp.where(lane >= LANES - 2, left, mid), 2, 1),
            pltpu.roll(jnp.where(lane >= LANES - 1, left, mid), 1, 1),
            pltpu.roll(jnp.where(lane < 1, right, mid), LANES - 1, 1),
            pltpu.roll(jnp.where(lane < 2, right, mid), LANES - 2, 1),
        )
        dz = stencil(*(grid[z + k, s, r0:r0 + SUB, :] for k in (-2, -1, 1, 2)))
        dx = stencil(*(grid[z, s, r0 + k:r0 + k + SUB, :] for k in (-2, -1, 1, 2)))
        return mid, dx, dy * dy + dz * dz, dz

    def block(cb, carry):
        @pl.when(cb == 0)
        def _():
            for copy in copies(0):
                copy.wait()

        for j in range(1, per_block + 1):
            @pl.when(cb * per_block + j < strips)
            def _():
                for copy in copies(cb * per_block + j):
                    copy.wait()

        owner = lax.bitwise_xor(cb // piece_blocks, depth_ref[0])
        lanes = pl.ds(pl.multiple_of(lax.rem(cb, piece_blocks) * MY, MY), MY)
        for rt in range(rows // MX):
            r0 = TOP + rt * MX
            edge_rows = slice(0, 2) if rt == 0 else slice(SUB - 2, SUB)
            for j in range(per_block):
                for c in range(3):
                    acc_ref[j, c] = zero
                acc_ref[j, 3] = zero + 1.0
            for zb in range(slices // MZ):
                at = ((0, 4), (6, 2))[rt][zb]

                @pl.when(mask_ref[zb, rt, cb] != 0)
                def _():
                    for j in range(per_block):
                        s = cb * per_block + j + 1
                        red, green, blue, trans = (acc_ref[j, c] for c in range(4))
                        for zi in range(MZ):
                            z = 2 + zb * MZ + zi
                            grade, g_x, g_yz, g_z = derivs(grid_g, z, s, r0)
                            _, a_x, a_yz, _ = derivs(grid_a, z, s, r0)
                            g_yz = g_yz + 36.0
                            a_yz = a_yz + 144.0
                            steep = 0.7 * jnp.abs(g_z)
                            position = grade * (bins - 1.0)
                            index = jnp.minimum(position.astype(jnp.int32), bins - 1)
                            w_low = 1.0 - (position - index.astype(jnp.float32))
                            w_high = round_weight(1.0 - w_low)
                            w_low = round_weight(w_low)
                            cls = [
                                w_low * gather(low_ref, c, index) + w_high * gather(high_ref, c, index)
                                for c in range(4)
                            ]
                            for n, term in enumerate((g_x, a_x, g_yz, a_yz, steep, *cls)):
                                kept_ref[zi, s - 1, n, at:at + 2, :] = term[edge_rows, :]
                            edge = 1.0 - 12.0 * lax.rsqrt(a_x * a_x + a_yz)
                            shade = 0.3 + steep * lax.rsqrt(g_x * g_x + g_yz)
                            weight = trans * (cls[3] * edge)
                            trans = trans - weight
                            weight = weight * shade
                            red = red + weight * cls[0]
                            green = green + weight * cls[1]
                            blue = blue + weight * cls[2]
                        for c, value in enumerate((red, green, blue, trans)):
                            acc_ref[j, c] = value
            for k in range(pieces):
                @pl.when(owner == k)
                def _():
                    for c in range(4):
                        for j in range(per_block):
                            part = pl.ds(pl.multiple_of(lax.rem(cb, piece_blocks) * MY + j * LANES, LANES), LANES)
                            outs[k][c, rt * SUB:(rt + 1) * SUB, part] = acc_ref[j, c]
        return carry

    lax.fori_loop(0, cols // MY, block, 0)


def edge_kernel(pieces, mask_ref, depth_ref, lat_ref, kept_ref, pair_ref, cross_ref, *outs):
    half = kept_ref.shape[0]
    strips = kept_ref.shape[1]
    sub = sublane((SUB, LANES))
    is_first = lax.rem((sub + 2) // 4, 2) == 0
    odd_lat = jnp.broadcast_to(lax.rem(lat_ref[0], 2), (SUB, LANES))
    from_pair = lax.rem(sub // 2, 2) != odd_lat
    piece_strips = strips // pieces
    packs = piece_strips // 2

    above = lax.rem(sub // 2, 2) == 0
    even_row = lax.rem(sub, 2) == 0

    def outside(raw, above):
        mate = jnp.where(even_row, pltpu.roll(raw, SUB - 1, 0), pltpu.roll(raw, 1, 0))
        mate = jnp.where(above == even_row, 8.0 * mate, 0.0)
        return jnp.where(above, raw - mate, mate - raw)

    def halo(f, zi, lanes):
        pair, cross = pair_ref[f, zi % 4, :, lanes], cross_ref[f, zi % 4, :, lanes]
        if zi < 4:
            return outside(jnp.where(from_pair, pair, cross), above)
        return outside(pltpu.roll(jnp.where(from_pair, cross, pair), 2, 0), above)

    def strip(s):
        lanes = pl.ds(pl.multiple_of(s * LANES, LANES), LANES)
        cb = s // (MY // LANES)
        full = [[jnp.broadcast_to(mask_ref[zb, rt, cb], (SUB, LANES)) for rt in range(2)] for zb in range(2)]
        live = jnp.where(
            sub < 4, jnp.where(sub < 2, full[0][0], full[1][1]), jnp.where(sub < 6, full[1][0], full[0][1])
        ) != 0
        zero = jnp.zeros((SUB, LANES), jnp.float32)
        total = [zero, zero, zero]
        trans = zero + 1.0
        for zi in range(half):
            g_x, a_x, g_yz, a_yz, steep, red, green, blue, alpha = (kept_ref[zi, s, n] for n in range(TERMS))
            g_x = g_x + halo(0, zi, lanes)
            a_x = a_x + halo(1, zi, lanes)
            edge = 1.0 - 12.0 * lax.rsqrt(a_x * a_x + a_yz)
            shade = 0.3 + steep * lax.rsqrt(g_x * g_x + g_yz)
            weight = jnp.where(live, trans * (alpha * edge), 0.0)
            trans = trans - weight
            weight = weight * shade
            total = [t + jnp.where(live, weight * c, 0.0) for t, c in zip(total, (red, green, blue))]
        out = [t + trans * pltpu.roll(t, 4, 0) for t in total]
        return out + [trans * pltpu.roll(trans, 4, 0)]

    def piece(p, carry):
        results = [strip(p * piece_strips + j) for j in range(piece_strips)]
        owner = lax.bitwise_xor(p, depth_ref[0])
        for j in range(packs):
            packed = [
                jnp.where(is_first, one, pltpu.roll(two, 4, 0)) for one, two in zip(results[j], results[j + packs])
            ]
            for k in range(pieces):
                @pl.when(owner == k)
                def _():
                    for c in range(4):
                        outs[k][c, :, j * LANES:(j + 1) * LANES] = packed[c]
        return carry

    lax.fori_loop(0, pieces, piece, 0)


def fold(parts, rank):
    level = 0
    while len(parts) > 1:
        first = lax.rem(lax.shift_right_logical(rank, level), 2) == 0
        merged = []
        for mine, other in zip(parts[0::2], parts[1::2]):
            first_here = jnp.broadcast_to(first, mine[3].shape)
            clear = jnp.where(first_here, mine[3], other[3])
            merged.append(
                [jnp.where(first_here, m, o) + clear * jnp.where(first_here, o, m) for m, o in zip(mine[:3], other[:3])]
                + [mine[3] * other[3]]
            )
        parts = merged
        level += 1
    return parts[0][:3] + [1.0 - parts[0][3]]


def finish_kernel(pieces, depth_ref, *refs):
    inner, edges, out_ref = refs[:pieces], refs[pieces:2 * pieces], refs[-1]
    rows, cols = out_ref.shape[1:]
    rank = depth_ref[0]
    frame = fold([[ref[c] for c in range(4)] for ref in inner], rank)
    rim = fold([[ref[c] for c in range(4)] for ref in edges], rank)
    for c in range(4):
        packed = rim[c]
        wide = jnp.concatenate([packed, pltpu.roll(packed, 4, 0)], axis=1)
        sub = sublane(wide.shape)
        out_ref[c, 0:SUB, :] = jnp.where(sub < 2, wide, frame[c][0:SUB, :])
        out_ref[c, rows - SUB:rows, :] = jnp.where(sub >= SUB - 2, wide, frame[c][rows - SUB:rows, :])


def swap_near(x, axis):
    return lax.ppermute(x, axis, [(i, i ^ 1) for i in range(lax.axis_size(axis))])


def swap_far(x, axis):
    size = lax.axis_size(axis)
    return lax.ppermute(x, axis, [(i, j) for k in range(1, size - 1, 2) for i, j in ((k, k + 1), (k + 1, k))])


def local(grade_field, amplitude, tf_table, brick_mask):
    slices, rows, cols = grade_field.shape
    assert (slices, rows) == (2 * MZ, 2 * MX)
    pieces = lax.axis_size("depth")
    depth_rank = lax.axis_index("depth").astype(jnp.int32).reshape(1)
    lat_rank = lax.axis_index("lat").astype(jnp.int32).reshape(1)
    scale = 4.0 / (slices * pieces)
    strips = cols // LANES
    f32 = jnp.float32
    vmem = pl.BlockSpec(memory_space=pltpu.VMEM)
    smem = pl.BlockSpec(memory_space=pltpu.SMEM)
    hbm = pl.BlockSpec(memory_space=pltpu.MemorySpace.HBM)
    lat_halo = jax.ShapeDtypeStruct((2, slices // 4, SUB, cols), f32)
    depth_halo = jax.ShapeDtypeStruct((2, 2, rows, cols), f32)
    hbm_only = pltpu.MemorySpace.HBM
    grade_field = pltpu.with_memory_space_constraint(grade_field, hbm_only)
    amplitude = pltpu.with_memory_space_constraint(amplitude, hbm_only)
    pair, cross = pl.pallas_call(
        rows_kernel,
        out_shape=(lat_halo, lat_halo),
        in_specs=[smem, hbm, hbm],
        out_specs=[hbm, hbm],
        scratch_shapes=[pltpu.SemaphoreType.DMA((2, 4, 2))],
        name="take_rows",
    )(lat_rank, grade_field, amplitude)
    near, far = pl.pallas_call(
        slices_kernel,
        out_shape=(depth_halo, depth_halo),
        in_specs=[smem, hbm, hbm],
        out_specs=[hbm, hbm],
        scratch_shapes=[pltpu.SemaphoreType.DMA((2, 2))],
        name="take_slices",
    )(depth_rank, grade_field, amplitude)
    pair = swap_near(pair, "lat")
    cross = swap_far(cross, "lat")
    near = swap_near(near, "depth")
    far = swap_far(far, "depth")
    piece = jax.ShapeDtypeStruct((4, rows, cols // pieces), f32)
    kept = jax.ShapeDtypeStruct((MZ, strips, TERMS, SUB, LANES), f32)
    grid = pltpu.VMEM((slices + 4, strips + 2, TOP + rows + SUB, LANES), f32)
    table = pltpu.VMEM((4, SUB, tf_table.shape[1]), f32)
    *parts, kept = pl.pallas_call(
        functools.partial(march_kernel, scale, pieces),
        out_shape=(piece,) * pieces + (kept,),
        in_specs=[smem, smem, hbm, hbm, hbm, hbm, vmem],
        out_specs=[vmem] * (pieces + 1),
        scratch_shapes=[
            grid,
            grid,
            pltpu.VMEM((MY // LANES, 4, SUB, LANES), f32),
            table,
            table,
            pltpu.SemaphoreType.DMA((2, strips, 3)),
        ],
        compiler_params=pltpu.CompilerParams(vmem_limit_bytes=24 << 20),
        name="march",
    )(brick_mask, depth_rank, grade_field, amplitude, near, far, tf_table)

    def exchange(parts):
        return [parts[0]] + [
            lax.ppermute(parts[k], "depth", [(i, i ^ k) for i in range(pieces)]) for k in range(1, pieces)
        ]

    inner = exchange(parts)
    rim = jax.ShapeDtypeStruct((4, SUB, cols // pieces // 2), f32)
    rims = pl.pallas_call(
        functools.partial(edge_kernel, pieces),
        out_shape=(rim,) * pieces,
        in_specs=[smem, smem, smem, vmem, vmem, vmem],
        out_specs=[vmem] * pieces,
        compiler_params=pltpu.CompilerParams(vmem_limit_bytes=16 << 20),
        name="edges",
    )(brick_mask, depth_rank, lat_rank, kept, pair, cross)
    edges = exchange(rims)
    return pl.pallas_call(
        functools.partial(finish_kernel, pieces),
        out_shape=piece,
        in_specs=[smem] + [vmem] * (2 * pieces),
        out_specs=vmem,
        compiler_params=pltpu.CompilerParams(vmem_limit_bytes=4 << 20),
        name="finish",
    )(depth_rank, *inner, *edges)


def solution(mesh):
    placed = (P("depth", "lat", None), P("depth", "lat", None), P(), P("depth", "lat", None))
    return jax.shard_map(
        local, mesh=mesh, in_specs=placed, out_specs=P(None, "lat", "depth"), check_vma=False
    )
```

```python
import functools

import jax
import jax.numpy as jnp
from jax import lax
from jax.experimental import pallas as pl
from jax.experimental.pallas import tpu as pltpu
from jax.sharding import PartitionSpec as P

MZ = 8
MX = 8
MY = 256
LANES = 128
SUB = 8
TOP = 8
TERMS = 9


def sublane(shape):
    return lax.broadcasted_iota(jnp.int32, shape, len(shape) - 2)


def take_kernel(lat_ref, depth_ref, grade_hbm, amp_hbm, pair_ref, cross_ref, near_ref, far_ref, sems, depth_sems):
    slices, rows = grade_hbm.shape[:2]
    span = slices // 4
    even = lax.rem(lat_ref[0], 2) == 0
    odd = lax.rem(depth_ref[0], 2)
    fields = (grade_hbm, amp_hbm)

    def copies(above_dst, below_dst):
        made = []
        for f, src in enumerate(fields):
            for q in range(4):
                part = src.at[pl.ds(span * q, span)]
                above = above_dst.at[f, :, pl.ds((0, 6, 4, 2)[q], 2), :]
                below = below_dst.at[f, :, pl.ds((6, 4, 2, 0)[q], 2), :]
                made.append(pltpu.make_async_copy(part.at[:, pl.ds(rows - 2, 2), :], above, sems.at[f, q, 0]))
                made.append(pltpu.make_async_copy(part.at[:, pl.ds(0, 2), :], below, sems.at[f, q, 1]))
        for f, src in enumerate(fields):
            for n, (dst, at) in enumerate(((near_ref, 1 - odd), (far_ref, odd))):
                here = src.at[pl.ds(at * (slices - 2), 2)]
                made.append(pltpu.make_async_copy(here, dst.at[f], depth_sems.at[f, n]))
        for copy in made:
            copy.start()
        for copy in made:
            copy.wait()

    @pl.when(even)
    def _():
        copies(pair_ref, cross_ref)

    @pl.when(jnp.logical_not(even))
    def _():
        copies(cross_ref, pair_ref)


def round_weight(w):
    return w.astype(jnp.bfloat16).astype(jnp.float32)


def march_kernel(scale, pieces, mask_ref, depth_ref, grade_hbm, amp_hbm, near_hbm, far_hbm, table_ref, *rest):
    outs, kept_ref = rest[:pieces], rest[pieces]
    grid_g, grid_a, acc_ref, low_ref, high_ref, sems = rest[pieces + 1:]
    slices, rows, cols = grade_hbm.shape
    strips = cols // LANES
    fields = ((grade_hbm, grid_g), (amp_hbm, grid_a))
    body = pl.ds(TOP, rows)
    odd_depth = lax.rem(depth_ref[0], 2)
    near_at = (1 - odd_depth) * (slices + 2)
    far_at = odd_depth * (slices + 2)

    def copies(s):
        lanes = pl.ds(s * LANES, LANES) if isinstance(s, int) else pl.ds(pl.multiple_of(s * LANES, LANES), LANES)
        made = []
        for f, (src, grid) in enumerate(fields):
            trio = (
                (src.at[:, :, lanes], grid.at[pl.ds(2, slices), s + 1, body, :]),
                (near_hbm.at[f, :, :, lanes], grid.at[pl.ds(near_at, 2), s + 1, body, :]),
                (far_hbm.at[f, :, :, lanes], grid.at[pl.ds(far_at, 2), s + 1, body, :]),
            )
            made += [pltpu.make_async_copy(here, there, sems.at[f, s, k]) for k, (here, there) in enumerate(trio)]
        return made

    for s in range(strips):
        for copy in copies(s):
            copy.start()
    zero = jnp.zeros((SUB, LANES), jnp.float32)
    for _, grid in fields:
        for z in range(slices):
            for r in range(0, rows, SUB):
                grid[z + 2, 0, TOP + r:TOP + r + SUB, :] = zero
                grid[z + 2, strips + 1, TOP + r:TOP + r + SUB, :] = zero
            for s in range(strips):
                grid[z + 2, s + 1, 0:TOP, :] = zero
                grid[z + 2, s + 1, TOP + rows:TOP + rows + SUB, :] = zero
    bins = table_ref.shape[1]
    table = (table_ref[...].astype(jnp.float32) / 65535.0).astype(jnp.bfloat16).astype(jnp.float32)
    table = jnp.where(sublane(table.shape) == 3, table * scale, table)
    column = lax.broadcasted_iota(jnp.int32, table.shape, 1)
    following = jnp.where(column == bins - 1, 0.0, pltpu.roll(table, bins - 1, 1))
    for c in range(4):
        low_ref[c] = jnp.broadcast_to(table[c:c + 1, :], (SUB, bins))
        high_ref[c] = jnp.broadcast_to(following[c:c + 1, :], (SUB, bins))
    lane = lax.broadcasted_iota(jnp.int32, (SUB, LANES), 1)
    per_block = MY // LANES
    piece_blocks = cols // pieces // MY

    def gather(ref, c, index):
        return jnp.take_along_axis(ref[c], index, axis=1)

    def stencil(m2, m1, p1, p2):
        return (m2 - p2) + 8.0 * (p1 - m1)

    def derivs(grid, z, s, r0):
        mid = grid[z, s, r0:r0 + SUB, :]
        left = grid[z, s - 1, r0:r0 + SUB, :]
        right = grid[z, s + 1, r0:r0 + SUB, :]
        dy = stencil(
            pltpu.roll(jnp.where(lane >= LANES - 2, left, mid), 2, 1),
            pltpu.roll(jnp.where(lane >= LANES - 1, left, mid), 1, 1),
            pltpu.roll(jnp.where(lane < 1, right, mid), LANES - 1, 1),
            pltpu.roll(jnp.where(lane < 2, right, mid), LANES - 2, 1),
        )
        dz = stencil(*(grid[z + k, s, r0:r0 + SUB, :] for k in (-2, -1, 1, 2)))
        dx = stencil(*(grid[z, s, r0 + k:r0 + k + SUB, :] for k in (-2, -1, 1, 2)))
        return mid, dx, dy * dy + dz * dz, dz

    def block(cb, carry):
        @pl.when(cb == 0)
        def _():
            for copy in copies(0):
                copy.wait()

        for j in range(1, per_block + 1):
            @pl.when(cb * per_block + j < strips)
            def _():
                for copy in copies(cb * per_block + j):
                    copy.wait()

        owner = lax.bitwise_xor(cb // piece_blocks, depth_ref[0])
        lanes = pl.ds(pl.multiple_of(lax.rem(cb, piece_blocks) * MY, MY), MY)
        for rt in range(rows // MX):
            r0 = TOP + rt * MX
            edge_rows = slice(0, 2) if rt == 0 else slice(SUB - 2, SUB)
            for j in range(per_block):
                for c in range(3):
                    acc_ref[j, c] = zero
                acc_ref[j, 3] = zero + 1.0
            for zb in range(slices // MZ):
                at = ((0, 4), (6, 2))[rt][zb]

                @pl.when(mask_ref[zb, rt, cb] != 0)
                def _():
                    for j in range(per_block):
                        s = cb * per_block + j + 1
                        red, green, blue, trans = (acc_ref[j, c] for c in range(4))
                        for zi in range(MZ):
                            z = 2 + zb * MZ + zi
                            grade, g_x, g_yz, g_z = derivs(grid_g, z, s, r0)
                            _, a_x, a_yz, _ = derivs(grid_a, z, s, r0)
                            g_yz = g_yz + 36.0
                            a_yz = a_yz + 144.0
                            steep = 0.7 * jnp.abs(g_z)
                            position = grade * (bins - 1.0)
                            index = jnp.minimum(position.astype(jnp.int32), bins - 1)
                            w_low = 1.0 - (position - index.astype(jnp.float32))
                            w_high = round_weight(1.0 - w_low)
                            w_low = round_weight(w_low)
                            cls = [
                                w_low * gather(low_ref, c, index) + w_high * gather(high_ref, c, index)
                                for c in range(4)
                            ]
                            for n, term in enumerate((g_x, a_x, g_yz, a_yz, steep, *cls)):
                                kept_ref[zi, s - 1, n, at:at + 2, :] = term[edge_rows, :]
                            edge = 1.0 - 12.0 * lax.rsqrt(a_x * a_x + a_yz)
                            shade = 0.3 + steep * lax.rsqrt(g_x * g_x + g_yz)
                            weight = trans * (cls[3] * edge)
                            trans = trans - weight
                            weight = weight * shade
                            red = red + weight * cls[0]
                            green = green + weight * cls[1]
                            blue = blue + weight * cls[2]
                        for c, value in enumerate((red, green, blue, trans)):
                            acc_ref[j, c] = value
            for k in range(pieces):
                @pl.when(owner == k)
                def _():
                    for c in range(4):
                        for j in range(per_block):
                            part = pl.ds(pl.multiple_of(lax.rem(cb, piece_blocks) * MY + j * LANES, LANES), LANES)
                            outs[k][c, rt * SUB:(rt + 1) * SUB, part] = acc_ref[j, c]
        return carry

    lax.fori_loop(0, cols // MY, block, 0)


def edge_kernel(pieces, mask_ref, depth_ref, lat_ref, kept_ref, pair_ref, cross_ref, *outs):
    half = kept_ref.shape[0]
    strips = kept_ref.shape[1]
    sub = sublane((SUB, LANES))
    is_first = lax.rem((sub + 2) // 4, 2) == 0
    odd_lat = jnp.broadcast_to(lax.rem(lat_ref[0], 2), (SUB, LANES))
    from_pair = lax.rem(sub // 2, 2) != odd_lat
    piece_strips = strips // pieces
    packs = piece_strips // 2

    above = lax.rem(sub // 2, 2) == 0
    even_row = lax.rem(sub, 2) == 0

    def outside(raw, above):
        mate = jnp.where(even_row, pltpu.roll(raw, SUB - 1, 0), pltpu.roll(raw, 1, 0))
        mate = jnp.where(above == even_row, 8.0 * mate, 0.0)
        return jnp.where(above, raw - mate, mate - raw)

    def halo(f, zi, lanes):
        pair, cross = pair_ref[f, zi % 4, :, lanes], cross_ref[f, zi % 4, :, lanes]
        if zi < 4:
            return outside(jnp.where(from_pair, pair, cross), above)
        return outside(pltpu.roll(jnp.where(from_pair, cross, pair), 2, 0), above)

    def strip(s):
        lanes = pl.ds(pl.multiple_of(s * LANES, LANES), LANES)
        cb = s // (MY // LANES)
        full = [[jnp.broadcast_to(mask_ref[zb, rt, cb], (SUB, LANES)) for rt in range(2)] for zb in range(2)]
        live = jnp.where(
            sub < 4, jnp.where(sub < 2, full[0][0], full[1][1]), jnp.where(sub < 6, full[1][0], full[0][1])
        ) != 0
        zero = jnp.zeros((SUB, LANES), jnp.float32)
        total = [zero, zero, zero]
        trans = zero + 1.0
        for zi in range(half):
            g_x, a_x, g_yz, a_yz, steep, red, green, blue, alpha = (kept_ref[zi, s, n] for n in range(TERMS))
            g_x = g_x + halo(0, zi, lanes)
            a_x = a_x + halo(1, zi, lanes)
            edge = 1.0 - 12.0 * lax.rsqrt(a_x * a_x + a_yz)
            shade = 0.3 + steep * lax.rsqrt(g_x * g_x + g_yz)
            weight = jnp.where(live, trans * (alpha * edge), 0.0)
            trans = trans - weight
            weight = weight * shade
            total = [t + jnp.where(live, weight * c, 0.0) for t, c in zip(total, (red, green, blue))]
        out = [t + trans * pltpu.roll(t, 4, 0) for t in total]
        return out + [trans * pltpu.roll(trans, 4, 0)]

    def piece(p, carry):
        results = [strip(p * piece_strips + j) for j in range(piece_strips)]
        owner = lax.bitwise_xor(p, depth_ref[0])
        for j in range(packs):
            packed = [
                jnp.where(is_first, one, pltpu.roll(two, 4, 0)) for one, two in zip(results[j], results[j + packs])
            ]
            for k in range(pieces):
                @pl.when(owner == k)
                def _():
                    for c in range(4):
                        outs[k][c, :, j * LANES:(j + 1) * LANES] = packed[c]
        return carry

    lax.fori_loop(0, pieces, piece, 0)


def fold(parts, rank):
    level = 0
    while len(parts) > 1:
        first = lax.rem(lax.shift_right_logical(rank, level), 2) == 0
        merged = []
        for mine, other in zip(parts[0::2], parts[1::2]):
            first_here = jnp.broadcast_to(first, mine[3].shape)
            clear = jnp.where(first_here, mine[3], other[3])
            merged.append(
                [jnp.where(first_here, m, o) + clear * jnp.where(first_here, o, m) for m, o in zip(mine[:3], other[:3])]
                + [mine[3] * other[3]]
            )
        parts = merged
        level += 1
    return parts[0][:3] + [1.0 - parts[0][3]]


def finish_kernel(pieces, depth_ref, *refs):
    inner, edges, out_ref = refs[:pieces], refs[pieces:2 * pieces], refs[-1]
    rows, cols = out_ref.shape[1:]
    rank = depth_ref[0]
    frame = fold([[ref[c] for c in range(4)] for ref in inner], rank)
    rim = fold([[ref[c] for c in range(4)] for ref in edges], rank)
    for c in range(4):
        packed = rim[c]
        wide = jnp.concatenate([packed, pltpu.roll(packed, 4, 0)], axis=1)
        sub = sublane(wide.shape)
        out_ref[c, 0:SUB, :] = jnp.where(sub < 2, wide, frame[c][0:SUB, :])
        out_ref[c, rows - SUB:rows, :] = jnp.where(sub >= SUB - 2, wide, frame[c][rows - SUB:rows, :])


def swap_near(x, axis):
    return lax.ppermute(x, axis, [(i, i ^ 1) for i in range(lax.axis_size(axis))])


def swap_far(x, axis):
    size = lax.axis_size(axis)
    return lax.ppermute(x, axis, [(i, j) for k in range(1, size - 1, 2) for i, j in ((k, k + 1), (k + 1, k))])


def local(grade_field, amplitude, tf_table, brick_mask):
    slices, rows, cols = grade_field.shape
    assert (slices, rows) == (2 * MZ, 2 * MX)
    pieces = lax.axis_size("depth")
    depth_rank = lax.axis_index("depth").astype(jnp.int32).reshape(1)
    lat_rank = lax.axis_index("lat").astype(jnp.int32).reshape(1)
    scale = 4.0 / (slices * pieces)
    strips = cols // LANES
    f32 = jnp.float32
    vmem = pl.BlockSpec(memory_space=pltpu.VMEM)
    smem = pl.BlockSpec(memory_space=pltpu.SMEM)
    hbm = pl.BlockSpec(memory_space=pltpu.MemorySpace.HBM)
    lat_halo = jax.ShapeDtypeStruct((2, slices // 4, SUB, cols), f32)
    depth_halo = jax.ShapeDtypeStruct((2, 2, rows, cols), f32)
    hbm_only = pltpu.MemorySpace.HBM
    grade_field = pltpu.with_memory_space_constraint(grade_field, hbm_only)
    amplitude = pltpu.with_memory_space_constraint(amplitude, hbm_only)
    pair, cross, near, far = pl.pallas_call(
        take_kernel,
        out_shape=(lat_halo, lat_halo, depth_halo, depth_halo),
        in_specs=[smem, smem, hbm, hbm],
        out_specs=[vmem] * 4,
        scratch_shapes=[pltpu.SemaphoreType.DMA((2, 4, 2)), pltpu.SemaphoreType.DMA((2, 2))],
        compiler_params=pltpu.CompilerParams(vmem_limit_bytes=8 << 20),
        name="take",
    )(lat_rank, depth_rank, grade_field, amplitude)
    pair = swap_near(pair, "lat")
    cross = swap_far(cross, "lat")
    near = swap_near(near, "depth")
    far = swap_far(far, "depth")
    piece = jax.ShapeDtypeStruct((4, rows, cols // pieces), f32)
    kept = jax.ShapeDtypeStruct((MZ, strips, TERMS, SUB, LANES), f32)
    grid = pltpu.VMEM((slices + 4, strips + 2, TOP + rows + SUB, LANES), f32)
    table = pltpu.VMEM((4, SUB, tf_table.shape[1]), f32)
    *parts, kept = pl.pallas_call(
        functools.partial(march_kernel, scale, pieces),
        out_shape=(piece,) * pieces + (kept,),
        in_specs=[smem, smem, hbm, hbm, hbm, hbm, vmem],
        out_specs=[vmem] * (pieces + 1),
        scratch_shapes=[
            grid,
            grid,
            pltpu.VMEM((MY // LANES, 4, SUB, LANES), f32),
            table,
            table,
            pltpu.SemaphoreType.DMA((2, strips, 3)),
        ],
        compiler_params=pltpu.CompilerParams(vmem_limit_bytes=24 << 20),
        name="march",
    )(brick_mask, depth_rank, grade_field, amplitude, near, far, tf_table)

    def exchange(parts):
        return [parts[0]] + [
            lax.ppermute(parts[k], "depth", [(i, i ^ k) for i in range(pieces)]) for k in range(1, pieces)
        ]

    inner = exchange(parts)
    rim = jax.ShapeDtypeStruct((4, SUB, cols // pieces // 2), f32)
    rims = pl.pallas_call(
        functools.partial(edge_kernel, pieces),
        out_shape=(rim,) * pieces,
        in_specs=[smem, smem, smem, vmem, vmem, vmem],
        out_specs=[vmem] * pieces,
        compiler_params=pltpu.CompilerParams(vmem_limit_bytes=16 << 20),
        name="edges",
    )(brick_mask, depth_rank, lat_rank, kept, pair, cross)
    edges = exchange(rims)
    return pl.pallas_call(
        functools.partial(finish_kernel, pieces),
        out_shape=piece,
        in_specs=[smem] + [vmem] * (2 * pieces),
        out_specs=vmem,
        compiler_params=pltpu.CompilerParams(vmem_limit_bytes=4 << 20),
        name="finish",
    )(depth_rank, *inner, *edges)


def solution(mesh):
    placed = (P("depth", "lat", None), P("depth", "lat", None), P(), P("depth", "lat", None))
    return jax.shard_map(
        local, mesh=mesh, in_specs=placed, out_specs=P(None, "lat", "depth"), check_vma=False
    )
```

```python
import functools

import jax
import jax.numpy as jnp
from jax import lax
from jax.experimental import pallas as pl
from jax.experimental.pallas import tpu as pltpu
from jax.sharding import PartitionSpec as P

MZ = 8
MX = 8
MY = 256
LANES = 128
SUB = 8
TERMS = 9


def sublane(shape):
    return lax.broadcasted_iota(jnp.int32, shape, len(shape) - 2)


def take_kernel(lat_ref, depth_ref, grade_hbm, amp_hbm, pair_ref, cross_ref, near_ref, far_ref, sems, depth_sems):
    slices, rows = grade_hbm.shape[:2]
    span = slices // 4
    even = lax.rem(lat_ref[0], 2) == 0
    odd = lax.rem(depth_ref[0], 2)
    fields = (grade_hbm, amp_hbm)

    def copies(above_dst, below_dst):
        made = []
        for f, src in enumerate(fields):
            for q in range(4):
                part = src.at[pl.ds(span * q, span)]
                above = above_dst.at[f, :, pl.ds((0, 6, 4, 2)[q], 2), :]
                below = below_dst.at[f, :, pl.ds((6, 4, 2, 0)[q], 2), :]
                made.append(pltpu.make_async_copy(part.at[:, pl.ds(rows - 2, 2), :], above, sems.at[f, q, 0]))
                made.append(pltpu.make_async_copy(part.at[:, pl.ds(0, 2), :], below, sems.at[f, q, 1]))
        for f, src in enumerate(fields):
            for n, (dst, at) in enumerate(((near_ref, 1 - odd), (far_ref, odd))):
                here = src.at[pl.ds(at * (slices - 2), 2)]
                made.append(pltpu.make_async_copy(here, dst.at[f], depth_sems.at[f, n]))
        for copy in made:
            copy.start()
        for copy in made:
            copy.wait()

    @pl.when(even)
    def _():
        copies(pair_ref, cross_ref)

    @pl.when(jnp.logical_not(even))
    def _():
        copies(cross_ref, pair_ref)


def round_weight(w):
    return w.astype(jnp.bfloat16).astype(jnp.float32)


def stencil(m2, m1, p1, p2):
    return (m2 - p2) + 8.0 * (p1 - m1)


def fill_tables(scale, table_ref, low_ref, high_ref):
    bins = table_ref.shape[1]
    table = (table_ref[...].astype(jnp.float32) / 65535.0).astype(jnp.bfloat16).astype(jnp.float32)
    table = jnp.where(sublane(table.shape) == 3, table * scale, table)
    column = lax.broadcasted_iota(jnp.int32, table.shape, 1)
    following = jnp.where(column == bins - 1, 0.0, pltpu.roll(table, bins - 1, 1))
    for c in range(4):
        low_ref[c] = jnp.broadcast_to(table[c:c + 1, :], (SUB, bins))
        high_ref[c] = jnp.broadcast_to(following[c:c + 1, :], (SUB, bins))


class Field:
    def __init__(self, ref, slices, strips, s):
        self.ref, self.strips = ref, strips
        self.per_slice = ref.shape[0] // slices
        self.s = s

    def load(self, z, rt, ds=0, k=0):
        start = pl.multiple_of((self.s + ds) * SUB, SUB) + (z * self.per_slice + rt * self.strips * SUB + k)
        return self.ref[pl.ds(start, SUB), :]

    def columns(self, z, rt, mid, lane):
        left = jnp.where(self.s > 0, self.load(z, rt, -jnp.minimum(self.s, 1)), 0.0)
        right = jnp.where(self.s < self.strips - 1, self.load(z, rt, jnp.minimum(self.strips - 1 - self.s, 1)), 0.0)
        return stencil(
            pltpu.roll(jnp.where(lane >= LANES - 2, left, mid), 2, 1),
            pltpu.roll(jnp.where(lane >= LANES - 1, left, mid), 1, 1),
            pltpu.roll(jnp.where(lane < 1, right, mid), LANES - 1, 1),
            pltpu.roll(jnp.where(lane < 2, right, mid), LANES - 2, 1),
        )

    def rows(self, z, rt, mid, sub, roll):
        def shifted(k):
            if k > 0:
                inside = sub < SUB - k
                if rt == 0:
                    return jnp.where(inside, self.load(z, 0, 0, k), self.load(z, 1, 0, k - SUB))
                return jnp.where(inside, pltpu.roll(mid, SUB - k, 0) if roll else self.load(z, 1, 0, k), 0.0)
            inside = sub >= -k
            if rt == 1:
                return jnp.where(inside, self.load(z, 1, 0, k), self.load(z, 0, 0, SUB + k))
            return jnp.where(inside, pltpu.roll(mid, -k, 0) if roll else self.load(z, 0, 0, k), 0.0)

        return stencil(*(shifted(k) for k in (-2, -1, 1, 2)))


def classify(grade, bins, low_ref, high_ref):
    position = grade * (bins - 1.0)
    index = jnp.minimum(position.astype(jnp.int32), bins - 1)
    w_low = 1.0 - (position - index.astype(jnp.float32))
    w_high = round_weight(1.0 - w_low)
    w_low = round_weight(w_low)

    def gather(ref, c):
        return jnp.take_along_axis(ref[c], index, axis=1)

    return [w_low * gather(low_ref, c) + w_high * gather(high_ref, c) for c in range(4)]


def step(state, terms):
    red, green, blue, trans = state
    g_x, a_x, g_yz, a_yz, steep, *cls = terms
    edge = 1.0 - 12.0 * lax.rsqrt(a_x * a_x + a_yz)
    shade = 0.3 + steep * lax.rsqrt(g_x * g_x + g_yz)
    weight = trans * (cls[3] * edge)
    trans = trans - weight
    weight = weight * shade
    return (red + weight * cls[0], green + weight * cls[1], blue + weight * cls[2], trans)


def cell_terms(fields, z, rt, along, roll, bins, low_ref, high_ref):
    lane = lax.broadcasted_iota(jnp.int32, (SUB, LANES), 1)
    sub = sublane((SUB, LANES))
    parts = []
    for field, near in zip(fields, along):
        mid = field.load(z, rt)
        dy = field.columns(z, rt, mid, lane)
        dz = stencil(*near)
        parts.append((mid, field.rows(z, rt, mid, sub, roll), dy * dy + dz * dz, dz))
    (grade, g_x, g_yz, g_z), (_, a_x, a_yz, _) = parts
    cls = classify(grade, bins, low_ref, high_ref)
    return (g_x, a_x, g_yz + 36.0, a_yz + 144.0, 0.7 * jnp.abs(g_z), *cls)


KEPT_AT = ((0, 4), (6, 2))


def keep(kept_ref, zi, s, rt, zb, terms):
    rows = slice(0, 2) if rt == 0 else slice(SUB - 2, SUB)
    at = KEPT_AT[rt][zb]
    for n, term in enumerate(terms):
        kept_ref[zi, s, n, at:at + 2, :] = term[rows, :]


def middle_kernel(scale, slices, strips, mask_ref, grade_ref, amp_ref, table_ref, mid_ref, kept_ref, low_ref, high_ref):
    bins = table_ref.shape[1]
    fill_tables(scale, table_ref, low_ref, high_ref)
    per_block = MY // LANES
    zero = jnp.zeros((SUB, LANES), jnp.float32)

    def block(cb, carry):
        for rt in range(2):
            for j in range(per_block):
                s = cb * per_block + j
                for c in range(3):
                    mid_ref[rt, s, c] = zero
                mid_ref[rt, s, 3] = zero + 1.0
            for zb in range(2):
                @pl.when(mask_ref[zb, rt, cb] != 0)
                def _():
                    for j in range(per_block):
                        s = cb * per_block + j
                        fields = [Field(ref, slices, strips, s) for ref in (grade_ref, amp_ref)]
                        state = tuple(mid_ref[rt, s, c] for c in range(4))
                        for zi in range(2 - 2 * zb, MZ - 2 * zb):
                            z = zb * MZ + zi
                            along = [[field.load(z + k, rt) for k in (-2, -1, 1, 2)] for field in fields]
                            terms = cell_terms(fields, z, rt, along, False, bins, low_ref, high_ref)
                            keep(kept_ref, zi, s, rt, zb, terms)
                            state = step(state, terms)
                        for c in range(4):
                            mid_ref[rt, s, c] = state[c]
        return carry

    lax.fori_loop(0, strips // per_block, block, 0)


def ends_kernel(scale, pieces, slices, strips, mask_ref, depth_ref, grade_ref, amp_ref, near_ref, far_ref, table_ref,
                mid_ref, *rest):
    outs, (kept_ref, acc_ref, low_ref, high_ref) = rest[:pieces], rest[pieces:]
    bins = table_ref.shape[1]
    fill_tables(scale, table_ref, low_ref, high_ref)
    per_block = MY // LANES
    piece_strips = strips // pieces
    piece_blocks = piece_strips // per_block
    zero = jnp.zeros((SUB, LANES), jnp.float32)
    odd = jnp.broadcast_to(lax.rem(depth_ref[0], 2), (SUB, LANES)) == 1

    def block(cb, carry):
        owner = lax.bitwise_xor(cb // piece_blocks, depth_ref[0])
        for rt in range(2):
            for zb in range(2):
                if zb == 0:
                    for j in range(per_block):
                        for c in range(3):
                            acc_ref[j, c] = zero
                        acc_ref[j, 3] = zero + 1.0
                else:
                    for j in range(per_block):
                        s = cb * per_block + j
                        trans = acc_ref[j, 3]
                        for c in range(3):
                            acc_ref[j, c] = acc_ref[j, c] + trans * mid_ref[rt, s, c]
                        acc_ref[j, 3] = trans * mid_ref[rt, s, 3]

                @pl.when(mask_ref[zb, rt, cb] != 0)
                def _():
                    for j in range(per_block):
                        s = cb * per_block + j
                        fields = [Field(ref, slices, strips, s) for ref in (grade_ref, amp_ref)]
                        halos = [[Field(ref, 4, strips, s) for ref in (near_ref, far_ref)]] * 2
                        state = tuple(acc_ref[j, c] for c in range(4))
                        for zi in (0, 1) if zb == 0 else (MZ - 2, MZ - 1):
                            z = zb * MZ + zi
                            along = []
                            for f in range(2):
                                near, far = halos[f]

                                def at(z):
                                    if 0 <= z < slices:
                                        return fields[f].load(z, rt)
                                    k = 2 * f + z % slices % 2
                                    one, two = near.load(k, rt), far.load(k, rt)
                                    return jnp.where(odd, one, two) if z < 0 else jnp.where(odd, two, one)

                                along.append([at(z + k) for k in (-2, -1, 1, 2)])
                            terms = cell_terms(fields, z, rt, along, True, bins, low_ref, high_ref)
                            keep(kept_ref, zi if zb == 0 else zi - 4, s, rt, zb, terms)
                            state = step(state, terms)
                        for c in range(4):
                            acc_ref[j, c] = state[c]
            for k in range(pieces):
                @pl.when(owner == k)
                def _():
                    for c in range(4):
                        for j in range(per_block):
                            part = lax.rem(cb, piece_blocks) * MY + j * LANES
                            lanes = pl.ds(pl.multiple_of(part, LANES), LANES)
                            outs[k][c, rt * SUB:(rt + 1) * SUB, lanes] = acc_ref[j, c]
        return carry

    lax.fori_loop(0, strips // per_block, block, 0)


def edge_kernel(pieces, mask_ref, depth_ref, lat_ref, kept_ref, ends_ref, pair_ref, cross_ref, *outs):
    half = kept_ref.shape[0]
    strips = kept_ref.shape[1]
    sub = sublane((SUB, LANES))
    is_first = lax.rem((sub + 2) // 4, 2) == 0
    odd_lat = jnp.broadcast_to(lax.rem(lat_ref[0], 2), (SUB, LANES))
    from_pair = lax.rem(sub // 2, 2) != odd_lat
    piece_strips = strips // pieces
    packs = piece_strips // 2

    above = lax.rem(sub // 2, 2) == 0
    even_row = lax.rem(sub, 2) == 0

    def outside(raw, above):
        mate = jnp.where(even_row, pltpu.roll(raw, SUB - 1, 0), pltpu.roll(raw, 1, 0))
        mate = jnp.where(above == even_row, 8.0 * mate, 0.0)
        return jnp.where(above, raw - mate, mate - raw)

    def halo(f, zi, lanes):
        pair, cross = pair_ref[f, zi % 4, :, lanes], cross_ref[f, zi % 4, :, lanes]
        if zi < 4:
            return outside(jnp.where(from_pair, pair, cross), above)
        return outside(pltpu.roll(jnp.where(from_pair, cross, pair), 2, 0), above)

    def strip(s):
        lanes = pl.ds(pl.multiple_of(s * LANES, LANES), LANES)
        cb = s // (MY // LANES)
        full = [[jnp.broadcast_to(mask_ref[zb, rt, cb], (SUB, LANES)) for rt in range(2)] for zb in range(2)]
        live = jnp.where(
            sub < 4, jnp.where(sub < 2, full[0][0], full[1][1]), jnp.where(sub < 6, full[1][0], full[0][1])
        ) != 0
        zero = jnp.zeros((SUB, LANES), jnp.float32)
        total = [zero, zero, zero]
        trans = zero + 1.0
        for zi in range(half):
            terms = [kept_ref[zi, s, n] for n in range(TERMS)]
            if zi < 2:
                terms = [jnp.where(is_first, ends_ref[zi, s, n], term) for n, term in enumerate(terms)]
            if zi >= half - 2:
                terms = [jnp.where(is_first, term, ends_ref[zi - half + 4, s, n]) for n, term in enumerate(terms)]
            g_x, a_x, g_yz, a_yz, steep, red, green, blue, alpha = terms
            g_x = g_x + halo(0, zi, lanes)
            a_x = a_x + halo(1, zi, lanes)
            edge = 1.0 - 12.0 * lax.rsqrt(a_x * a_x + a_yz)
            shade = 0.3 + steep * lax.rsqrt(g_x * g_x + g_yz)
            weight = jnp.where(live, trans * (alpha * edge), 0.0)
            trans = trans - weight
            weight = weight * shade
            total = [t + jnp.where(live, weight * c, 0.0) for t, c in zip(total, (red, green, blue))]
        out = [t + trans * pltpu.roll(t, 4, 0) for t in total]
        return out + [trans * pltpu.roll(trans, 4, 0)]

    def piece(p, carry):
        results = [strip(p * piece_strips + j) for j in range(piece_strips)]
        owner = lax.bitwise_xor(p, depth_ref[0])
        for j in range(packs):
            packed = [
                jnp.where(is_first, one, pltpu.roll(two, 4, 0)) for one, two in zip(results[j], results[j + packs])
            ]
            for k in range(pieces):
                @pl.when(owner == k)
                def _():
                    for c in range(4):
                        outs[k][c, :, j * LANES:(j + 1) * LANES] = packed[c]
        return carry

    lax.fori_loop(0, pieces, piece, 0)


def fold(parts, rank):
    level = 0
    while len(parts) > 1:
        first = lax.rem(lax.shift_right_logical(rank, level), 2) == 0
        merged = []
        for mine, other in zip(parts[0::2], parts[1::2]):
            first_here = jnp.broadcast_to(first, mine[3].shape)
            clear = jnp.where(first_here, mine[3], other[3])
            merged.append(
                [jnp.where(first_here, m, o) + clear * jnp.where(first_here, o, m) for m, o in zip(mine[:3], other[:3])]
                + [mine[3] * other[3]]
            )
        parts = merged
        level += 1
    return parts[0][:3] + [1.0 - parts[0][3]]


def finish_kernel(pieces, depth_ref, *refs):
    inner, edges, out_ref = refs[:pieces], refs[pieces:2 * pieces], refs[-1]
    rows, cols = out_ref.shape[1:]
    rank = depth_ref[0]
    frame = fold([[ref[c] for c in range(4)] for ref in inner], rank)
    rim = fold([[ref[c] for c in range(4)] for ref in edges], rank)
    for c in range(4):
        packed = rim[c]
        wide = jnp.concatenate([packed, pltpu.roll(packed, 4, 0)], axis=1)
        sub = sublane(wide.shape)
        out_ref[c, 0:SUB, :] = jnp.where(sub < 2, wide, frame[c][0:SUB, :])
        out_ref[c, rows - SUB:rows, :] = jnp.where(sub >= SUB - 2, wide, frame[c][rows - SUB:rows, :])


def swap_near(x, axis):
    return lax.ppermute(x, axis, [(i, i ^ 1) for i in range(lax.axis_size(axis))])


def swap_far(x, axis):
    size = lax.axis_size(axis)
    return lax.ppermute(x, axis, [(i, j) for k in range(1, size - 1, 2) for i, j in ((k, k + 1), (k + 1, k))])


def by_strips(array):
    rows, cols = array.shape[-2:]
    split = array.reshape(-1, rows // SUB, SUB, cols // LANES, LANES)
    return split.transpose(0, 1, 3, 2, 4).reshape(-1, LANES)


def local(grade_field, amplitude, tf_table, brick_mask):
    slices, rows, cols = grade_field.shape
    assert (slices, rows) == (2 * MZ, 2 * MX)
    pieces = lax.axis_size("depth")
    depth_rank = lax.axis_index("depth").astype(jnp.int32).reshape(1)
    lat_rank = lax.axis_index("lat").astype(jnp.int32).reshape(1)
    f32 = jnp.float32
    vmem = pl.BlockSpec(memory_space=pltpu.VMEM)
    smem = pl.BlockSpec(memory_space=pltpu.SMEM)
    hbm = pl.BlockSpec(memory_space=pltpu.MemorySpace.HBM)
    lat_halo = jax.ShapeDtypeStruct((2, slices // 4, SUB, cols), f32)
    depth_halo = jax.ShapeDtypeStruct((2, 2, rows, cols), f32)
    hbm_only = pltpu.MemorySpace.HBM
    fields = (grade_field, amplitude)
    grade_field = pltpu.with_memory_space_constraint(grade_field, hbm_only)
    amplitude = pltpu.with_memory_space_constraint(amplitude, hbm_only)
    pair, cross, near, far = pl.pallas_call(
        take_kernel,
        out_shape=(lat_halo, lat_halo, depth_halo, depth_halo),
        in_specs=[smem, smem, hbm, hbm],
        out_specs=[vmem] * 4,
        scratch_shapes=[pltpu.SemaphoreType.DMA((2, 4, 2)), pltpu.SemaphoreType.DMA((2, 2))],
        compiler_params=pltpu.CompilerParams(vmem_limit_bytes=8 << 20),
        name="take",
    )(lat_rank, depth_rank, grade_field, amplitude)
    pair = swap_near(pair, "lat")
    cross = swap_far(cross, "lat")
    near = swap_near(near, "depth")
    far = swap_far(far, "depth")
    piece = jax.ShapeDtypeStruct((4, rows, cols // pieces), f32)
    scale = 4.0 / (slices * pieces)
    strips = cols // LANES
    table = pltpu.VMEM((4, SUB, tf_table.shape[1]), f32)
    grade_strips, amp_strips = by_strips(fields[0]), by_strips(fields[1])
    mid, kept = pl.pallas_call(
        functools.partial(middle_kernel, scale, slices, strips),
        out_shape=(
            jax.ShapeDtypeStruct((2, strips, 4, SUB, LANES), f32),
            jax.ShapeDtypeStruct((MZ, strips, TERMS, SUB, LANES), f32),
        ),
        in_specs=[smem, vmem, vmem, vmem],
        out_specs=[vmem, vmem],
        scratch_shapes=[table, table],
        compiler_params=pltpu.CompilerParams(vmem_limit_bytes=8 << 20),
        name="middle",
    )(brick_mask, grade_strips, amp_strips, tf_table)
    *parts, kept_ends = pl.pallas_call(
        functools.partial(ends_kernel, scale, pieces, slices, strips),
        out_shape=(piece,) * pieces + (jax.ShapeDtypeStruct((4, strips, TERMS, SUB, LANES), f32),),
        in_specs=[smem, smem] + [vmem] * 6,
        out_specs=[vmem] * (pieces + 1),
        scratch_shapes=[pltpu.VMEM((MY // LANES, 4, SUB, LANES), f32), table, table],
        compiler_params=pltpu.CompilerParams(vmem_limit_bytes=8 << 20),
        name="ends",
    )(brick_mask, depth_rank, grade_strips, amp_strips, by_strips(near), by_strips(far), tf_table, mid)

    def exchange(parts):
        return [parts[0]] + [
            lax.ppermute(parts[k], "depth", [(i, i ^ k) for i in range(pieces)]) for k in range(1, pieces)
        ]

    inner = exchange(parts)
    rim = jax.ShapeDtypeStruct((4, SUB, cols // pieces // 2), f32)
    rims = pl.pallas_call(
        functools.partial(edge_kernel, pieces),
        out_shape=(rim,) * pieces,
        in_specs=[smem, smem, smem, vmem, vmem, vmem, vmem],
        out_specs=[vmem] * pieces,
        compiler_params=pltpu.CompilerParams(vmem_limit_bytes=4 << 20),
        name="edges",
    )(brick_mask, depth_rank, lat_rank, kept, kept_ends, pair, cross)
    edges = exchange(rims)
    return pl.pallas_call(
        functools.partial(finish_kernel, pieces),
        out_shape=piece,
        in_specs=[smem] + [vmem] * (2 * pieces),
        out_specs=vmem,
        compiler_params=pltpu.CompilerParams(vmem_limit_bytes=4 << 20),
        name="finish",
    )(depth_rank, *inner, *edges)


def solution(mesh):
    placed = (P("depth", "lat", None), P("depth", "lat", None), P(), P("depth", "lat", None))
    return jax.shard_map(
        local, mesh=mesh, in_specs=placed, out_specs=P(None, "lat", "depth"), check_vma=False
    )
```

```python
import functools

import jax
import jax.numpy as jnp
from jax import lax
from jax.experimental import pallas as pl
from jax.experimental.pallas import tpu as pltpu
from jax.sharding import PartitionSpec as P

MZ = 8
MX = 8
MY = 256
LANES = 128
SUB = 8
TERMS = 9


def sublane(shape):
    return lax.broadcasted_iota(jnp.int32, shape, len(shape) - 2)


def rows_kernel(lat_ref, grade_hbm, amp_hbm, pair_ref, cross_ref, sems):
    slices, rows = grade_hbm.shape[:2]
    span = slices // 4
    even = lax.rem(lat_ref[0], 2) == 0

    def copies(above_dst, below_dst):
        made = []
        for f, src in enumerate((grade_hbm, amp_hbm)):
            for q in range(4):
                part = src.at[pl.ds(span * q, span)]
                above = above_dst.at[f, :, pl.ds((0, 6, 4, 2)[q], 2), :]
                below = below_dst.at[f, :, pl.ds((6, 4, 2, 0)[q], 2), :]
                made.append(pltpu.make_async_copy(part.at[:, pl.ds(rows - 2, 2), :], above, sems.at[f, q, 0]))
                made.append(pltpu.make_async_copy(part.at[:, pl.ds(0, 2), :], below, sems.at[f, q, 1]))
        for copy in made:
            copy.start()
        for copy in made:
            copy.wait()

    @pl.when(even)
    def _():
        copies(pair_ref, cross_ref)

    @pl.when(jnp.logical_not(even))
    def _():
        copies(cross_ref, pair_ref)


def slices_kernel(depth_ref, grade_hbm, amp_hbm, after_ref, near_ref, far_ref, sems):
    del after_ref
    slices = grade_hbm.shape[0]
    odd = lax.rem(depth_ref[0], 2)
    made = []
    for f, src in enumerate((grade_hbm, amp_hbm)):
        for n, (dst, at) in enumerate(((near_ref, 1 - odd), (far_ref, odd))):
            made.append(pltpu.make_async_copy(src.at[pl.ds(at * (slices - 2), 2)], dst.at[f], sems.at[f, n]))
    for copy in made:
        copy.start()
    for copy in made:
        copy.wait()


def round_weight(w):
    return w.astype(jnp.bfloat16).astype(jnp.float32)


def stencil(m2, m1, p1, p2):
    return (m2 - p2) + 8.0 * (p1 - m1)


def fill_tables(scale, table_ref, low_ref, high_ref):
    bins = table_ref.shape[1]
    table = (table_ref[...].astype(jnp.float32) / 65535.0).astype(jnp.bfloat16).astype(jnp.float32)
    table = jnp.where(sublane(table.shape) == 3, table * scale, table)
    column = lax.broadcasted_iota(jnp.int32, table.shape, 1)
    following = jnp.where(column == bins - 1, 0.0, pltpu.roll(table, bins - 1, 1))
    for c in range(4):
        low_ref[c] = jnp.broadcast_to(table[c:c + 1, :], (SUB, bins))
        high_ref[c] = jnp.broadcast_to(following[c:c + 1, :], (SUB, bins))


class Field:
    def __init__(self, ref, slices, strips, s):
        self.ref, self.strips = ref, strips
        self.per_slice = ref.shape[0] // slices
        self.s = s

    def load(self, z, rt, ds=0, k=0):
        start = pl.multiple_of((self.s + ds) * SUB, SUB) + (z * self.per_slice + rt * self.strips * SUB + k)
        return self.ref[pl.ds(start, SUB), :]

    def columns(self, z, rt, mid, lane):
        left = jnp.where(self.s > 0, self.load(z, rt, -jnp.minimum(self.s, 1)), 0.0)
        right = jnp.where(self.s < self.strips - 1, self.load(z, rt, jnp.minimum(self.strips - 1 - self.s, 1)), 0.0)
        return stencil(
            pltpu.roll(jnp.where(lane >= LANES - 2, left, mid), 2, 1),
            pltpu.roll(jnp.where(lane >= LANES - 1, left, mid), 1, 1),
            pltpu.roll(jnp.where(lane < 1, right, mid), LANES - 1, 1),
            pltpu.roll(jnp.where(lane < 2, right, mid), LANES - 2, 1),
        )

    def rows(self, z, rt, mid, sub, roll):
        def shifted(k):
            if k > 0:
                inside = sub < SUB - k
                if rt == 0:
                    return jnp.where(inside, self.load(z, 0, 0, k), self.load(z, 1, 0, k - SUB))
                return jnp.where(inside, pltpu.roll(mid, SUB - k, 0) if roll else self.load(z, 1, 0, k), 0.0)
            inside = sub >= -k
            if rt == 1:
                return jnp.where(inside, self.load(z, 1, 0, k), self.load(z, 0, 0, SUB + k))
            return jnp.where(inside, pltpu.roll(mid, -k, 0) if roll else self.load(z, 0, 0, k), 0.0)

        return stencil(*(shifted(k) for k in (-2, -1, 1, 2)))


def classify(grade, bins, low_ref, high_ref):
    position = grade * (bins - 1.0)
    index = jnp.minimum(position.astype(jnp.int32), bins - 1)
    w_low = 1.0 - (position - index.astype(jnp.float32))
    w_high = round_weight(1.0 - w_low)
    w_low = round_weight(w_low)

    def gather(ref, c):
        return jnp.take_along_axis(ref[c], index, axis=1)

    return [w_low * gather(low_ref, c) + w_high * gather(high_ref, c) for c in range(4)]


def step(state, terms):
    red, green, blue, trans = state
    g_x, a_x, g_yz, a_yz, steep, *cls = terms
    edge = 1.0 - 12.0 * lax.rsqrt(a_x * a_x + a_yz)
    shade = 0.3 + steep * lax.rsqrt(g_x * g_x + g_yz)
    weight = trans * (cls[3] * edge)
    trans = trans - weight
    weight = weight * shade
    return (red + weight * cls[0], green + weight * cls[1], blue + weight * cls[2], trans)


def cell_terms(fields, z, rt, along, roll, bins, low_ref, high_ref):
    lane = lax.broadcasted_iota(jnp.int32, (SUB, LANES), 1)
    sub = sublane((SUB, LANES))
    parts = []
    for field, near in zip(fields, along):
        mid = field.load(z, rt)
        dy = field.columns(z, rt, mid, lane)
        dz = stencil(*near)
        parts.append((mid, field.rows(z, rt, mid, sub, roll), dy * dy + dz * dz, dz))
    (grade, g_x, g_yz, g_z), (_, a_x, a_yz, _) = parts
    cls = classify(grade, bins, low_ref, high_ref)
    return (g_x, a_x, g_yz + 36.0, a_yz + 144.0, 0.7 * jnp.abs(g_z), *cls)


KEPT_AT = ((0, 4), (6, 2))


def keep(kept_ref, zi, s, rt, zb, terms):
    rows = slice(0, 2) if rt == 0 else slice(SUB - 2, SUB)
    at = KEPT_AT[rt][zb]
    for n, term in enumerate(terms):
        kept_ref[zi, s, n, at:at + 2, :] = term[rows, :]


def middle_kernel(scale, slices, strips, mask_ref, grade_ref, amp_ref, table_ref, mid_ref, kept_ref, low_ref, high_ref):
    bins = table_ref.shape[1]
    fill_tables(scale, table_ref, low_ref, high_ref)
    per_block = MY // LANES
    zero = jnp.zeros((SUB, LANES), jnp.float32)

    def block(cb, carry):
        for rt in range(2):
            for j in range(per_block):
                s = cb * per_block + j
                for c in range(3):
                    mid_ref[rt, s, c] = zero
                mid_ref[rt, s, 3] = zero + 1.0
            for zb in range(2):
                @pl.when(mask_ref[zb, rt, cb] != 0)
                def _():
                    for j in range(per_block):
                        s = cb * per_block + j
                        fields = [Field(ref, slices, strips, s) for ref in (grade_ref, amp_ref)]
                        state = tuple(mid_ref[rt, s, c] for c in range(4))
                        for zi in range(2 - 2 * zb, MZ - 2 * zb):
                            z = zb * MZ + zi
                            along = [[field.load(z + k, rt) for k in (-2, -1, 1, 2)] for field in fields]
                            terms = cell_terms(fields, z, rt, along, False, bins, low_ref, high_ref)
                            keep(kept_ref, zi, s, rt, zb, terms)
                            state = step(state, terms)
                        for c in range(4):
                            mid_ref[rt, s, c] = state[c]
        return carry

    lax.fori_loop(0, strips // per_block, block, 0)


def ends_kernel(scale, pieces, slices, strips, mask_ref, depth_ref, grade_ref, amp_ref, near_ref, far_ref, table_ref,
                mid_ref, *rest):
    outs, (kept_ref, acc_ref, low_ref, high_ref) = rest[:pieces], rest[pieces:]
    bins = table_ref.shape[1]
    fill_tables(scale, table_ref, low_ref, high_ref)
    per_block = MY // LANES
    piece_strips = strips // pieces
    piece_blocks = piece_strips // per_block
    zero = jnp.zeros((SUB, LANES), jnp.float32)
    odd = jnp.broadcast_to(lax.rem(depth_ref[0], 2), (SUB, LANES)) == 1

    def block(cb, carry):
        owner = lax.bitwise_xor(cb // piece_blocks, depth_ref[0])
        for rt in range(2):
            for zb in range(2):
                if zb == 0:
                    for j in range(per_block):
                        for c in range(3):
                            acc_ref[j, c] = zero
                        acc_ref[j, 3] = zero + 1.0
                else:
                    for j in range(per_block):
                        s = cb * per_block + j
                        trans = acc_ref[j, 3]
                        for c in range(3):
                            acc_ref[j, c] = acc_ref[j, c] + trans * mid_ref[rt, s, c]
                        acc_ref[j, 3] = trans * mid_ref[rt, s, 3]

                @pl.when(mask_ref[zb, rt, cb] != 0)
                def _():
                    for j in range(per_block):
                        s = cb * per_block + j
                        fields = [Field(ref, slices, strips, s) for ref in (grade_ref, amp_ref)]
                        halos = [[Field(ref, 4, strips, s) for ref in (near_ref, far_ref)]] * 2
                        state = tuple(acc_ref[j, c] for c in range(4))
                        for zi in (0, 1) if zb == 0 else (MZ - 2, MZ - 1):
                            z = zb * MZ + zi
                            along = []
                            for f in range(2):
                                near, far = halos[f]

                                def at(z):
                                    if 0 <= z < slices:
                                        return fields[f].load(z, rt)
                                    k = 2 * f + z % slices % 2
                                    one, two = near.load(k, rt), far.load(k, rt)
                                    return jnp.where(odd, one, two) if z < 0 else jnp.where(odd, two, one)

                                along.append([at(z + k) for k in (-2, -1, 1, 2)])
                            terms = cell_terms(fields, z, rt, along, True, bins, low_ref, high_ref)
                            keep(kept_ref, zi if zb == 0 else zi - 4, s, rt, zb, terms)
                            state = step(state, terms)
                        for c in range(4):
                            acc_ref[j, c] = state[c]
            for k in range(pieces):
                @pl.when(owner == k)
                def _():
                    for c in range(4):
                        for j in range(per_block):
                            part = lax.rem(cb, piece_blocks) * MY + j * LANES
                            lanes = pl.ds(pl.multiple_of(part, LANES), LANES)
                            outs[k][c, rt * SUB:(rt + 1) * SUB, lanes] = acc_ref[j, c]
        return carry

    lax.fori_loop(0, strips // per_block, block, 0)


def edge_kernel(pieces, mask_ref, depth_ref, lat_ref, kept_ref, ends_ref, pair_ref, cross_ref, *outs):
    half = kept_ref.shape[0]
    strips = kept_ref.shape[1]
    sub = sublane((SUB, LANES))
    is_first = lax.rem((sub + 2) // 4, 2) == 0
    odd_lat = jnp.broadcast_to(lax.rem(lat_ref[0], 2), (SUB, LANES))
    from_pair = lax.rem(sub // 2, 2) != odd_lat
    piece_strips = strips // pieces
    packs = piece_strips // 2

    above = lax.rem(sub // 2, 2) == 0
    even_row = lax.rem(sub, 2) == 0

    def outside(raw, above):
        mate = jnp.where(even_row, pltpu.roll(raw, SUB - 1, 0), pltpu.roll(raw, 1, 0))
        mate = jnp.where(above == even_row, 8.0 * mate, 0.0)
        return jnp.where(above, raw - mate, mate - raw)

    def halo(f, zi, lanes):
        pair, cross = pair_ref[f, zi % 4, :, lanes], cross_ref[f, zi % 4, :, lanes]
        if zi < 4:
            return outside(jnp.where(from_pair, pair, cross), above)
        return outside(pltpu.roll(jnp.where(from_pair, cross, pair), 2, 0), above)

    def strip(s):
        lanes = pl.ds(pl.multiple_of(s * LANES, LANES), LANES)
        cb = s // (MY // LANES)
        full = [[jnp.broadcast_to(mask_ref[zb, rt, cb], (SUB, LANES)) for rt in range(2)] for zb in range(2)]
        live = jnp.where(
            sub < 4, jnp.where(sub < 2, full[0][0], full[1][1]), jnp.where(sub < 6, full[1][0], full[0][1])
        ) != 0
        zero = jnp.zeros((SUB, LANES), jnp.float32)
        total = [zero, zero, zero]
        trans = zero + 1.0
        for zi in range(half):
            terms = [kept_ref[zi, s, n] for n in range(TERMS)]
            if zi < 2:
                terms = [jnp.where(is_first, ends_ref[zi, s, n], term) for n, term in enumerate(terms)]
            if zi >= half - 2:
                terms = [jnp.where(is_first, term, ends_ref[zi - half + 4, s, n]) for n, term in enumerate(terms)]
            g_x, a_x, g_yz, a_yz, steep, red, green, blue, alpha = terms
            g_x = g_x + halo(0, zi, lanes)
            a_x = a_x + halo(1, zi, lanes)
            edge = 1.0 - 12.0 * lax.rsqrt(a_x * a_x + a_yz)
            shade = 0.3 + steep * lax.rsqrt(g_x * g_x + g_yz)
            weight = jnp.where(live, trans * (alpha * edge), 0.0)
            trans = trans - weight
            weight = weight * shade
            total = [t + jnp.where(live, weight * c, 0.0) for t, c in zip(total, (red, green, blue))]
        out = [t + trans * pltpu.roll(t, 4, 0) for t in total]
        return out + [trans * pltpu.roll(trans, 4, 0)]

    def piece(p, carry):
        results = [strip(p * piece_strips + j) for j in range(piece_strips)]
        owner = lax.bitwise_xor(p, depth_ref[0])
        for j in range(packs):
            packed = [
                jnp.where(is_first, one, pltpu.roll(two, 4, 0)) for one, two in zip(results[j], results[j + packs])
            ]
            for k in range(pieces):
                @pl.when(owner == k)
                def _():
                    for c in range(4):
                        outs[k][c, :, j * LANES:(j + 1) * LANES] = packed[c]
        return carry

    lax.fori_loop(0, pieces, piece, 0)


def fold(parts, rank):
    level = 0
    while len(parts) > 1:
        first = lax.rem(lax.shift_right_logical(rank, level), 2) == 0
        merged = []
        for mine, other in zip(parts[0::2], parts[1::2]):
            first_here = jnp.broadcast_to(first, mine[3].shape)
            clear = jnp.where(first_here, mine[3], other[3])
            merged.append(
                [jnp.where(first_here, m, o) + clear * jnp.where(first_here, o, m) for m, o in zip(mine[:3], other[:3])]
                + [mine[3] * other[3]]
            )
        parts = merged
        level += 1
    return parts[0][:3] + [1.0 - parts[0][3]]


def finish_kernel(pieces, depth_ref, *refs):
    inner, edges, out_ref = refs[:pieces], refs[pieces:2 * pieces], refs[-1]
    rows, cols = out_ref.shape[1:]
    rank = depth_ref[0]
    frame = fold([[ref[c] for c in range(4)] for ref in inner], rank)
    rim = fold([[ref[c] for c in range(4)] for ref in edges], rank)
    for c in range(4):
        packed = rim[c]
        wide = jnp.concatenate([packed, pltpu.roll(packed, 4, 0)], axis=1)
        sub = sublane(wide.shape)
        out_ref[c, 0:SUB, :] = jnp.where(sub < 2, wide, frame[c][0:SUB, :])
        out_ref[c, rows - SUB:rows, :] = jnp.where(sub >= SUB - 2, wide, frame[c][rows - SUB:rows, :])


def swap_near(x, axis):
    return lax.ppermute(x, axis, [(i, i ^ 1) for i in range(lax.axis_size(axis))])


def swap_far(x, axis):
    size = lax.axis_size(axis)
    return lax.ppermute(x, axis, [(i, j) for k in range(1, size - 1, 2) for i, j in ((k, k + 1), (k + 1, k))])


def by_strips(array):
    rows, cols = array.shape[-2:]
    split = array.reshape(-1, rows // SUB, SUB, cols // LANES, LANES)
    return split.transpose(0, 1, 3, 2, 4).reshape(-1, LANES)


def local(grade_field, amplitude, tf_table, brick_mask):
    slices, rows, cols = grade_field.shape
    assert (slices, rows) == (2 * MZ, 2 * MX)
    pieces = lax.axis_size("depth")
    depth_rank = lax.axis_index("depth").astype(jnp.int32).reshape(1)
    lat_rank = lax.axis_index("lat").astype(jnp.int32).reshape(1)
    f32 = jnp.float32
    vmem = pl.BlockSpec(memory_space=pltpu.VMEM)
    smem = pl.BlockSpec(memory_space=pltpu.SMEM)
    hbm = pl.BlockSpec(memory_space=pltpu.MemorySpace.HBM)
    lat_halo = jax.ShapeDtypeStruct((2, slices // 4, SUB, cols), f32)
    depth_halo = jax.ShapeDtypeStruct((2, 2, rows, cols), f32)
    hbm_only = pltpu.MemorySpace.HBM
    fields = (grade_field, amplitude)
    grade_field = pltpu.with_memory_space_constraint(grade_field, hbm_only)
    amplitude = pltpu.with_memory_space_constraint(amplitude, hbm_only)
    small = pltpu.CompilerParams(vmem_limit_bytes=4 << 20)
    pair, cross = pl.pallas_call(
        rows_kernel,
        out_shape=(lat_halo, lat_halo),
        in_specs=[smem, hbm, hbm],
        out_specs=[vmem, vmem],
        scratch_shapes=[pltpu.SemaphoreType.DMA((2, 4, 2))],
        compiler_params=small,
        name="take_rows",
    )(lat_rank, grade_field, amplitude)
    near, far = pl.pallas_call(
        slices_kernel,
        out_shape=(depth_halo, depth_halo),
        in_specs=[smem, hbm, hbm, pl.BlockSpec(memory_space=pl.ANY)],
        out_specs=[vmem, vmem],
        scratch_shapes=[pltpu.SemaphoreType.DMA((2, 2))],
        compiler_params=small,
        name="take_slices",
    )(depth_rank, grade_field, amplitude, pair)
    pair = swap_near(pair, "lat")
    cross = swap_far(cross, "lat")
    near = swap_near(near, "depth")
    far = swap_far(far, "depth")
    piece = jax.ShapeDtypeStruct((4, rows, cols // pieces), f32)
    scale = 4.0 / (slices * pieces)
    strips = cols // LANES
    table = pltpu.VMEM((4, SUB, tf_table.shape[1]), f32)
    grade_strips, amp_strips = by_strips(fields[0]), by_strips(fields[1])
    mid, kept = pl.pallas_call(
        functools.partial(middle_kernel, scale, slices, strips),
        out_shape=(
            jax.ShapeDtypeStruct((2, strips, 4, SUB, LANES), f32),
            jax.ShapeDtypeStruct((MZ, strips, TERMS, SUB, LANES), f32),
        ),
        in_specs=[smem, vmem, vmem, vmem],
        out_specs=[vmem, vmem],
        scratch_shapes=[table, table],
        compiler_params=pltpu.CompilerParams(vmem_limit_bytes=8 << 20),
        cost_estimate=pl.CostEstimate(flops=10**10, bytes_accessed=10**8, transcendentals=0),
        name="middle",
    )(brick_mask, grade_strips, amp_strips, tf_table)
    *parts, kept_ends = pl.pallas_call(
        functools.partial(ends_kernel, scale, pieces, slices, strips),
        out_shape=(piece,) * pieces + (jax.ShapeDtypeStruct((4, strips, TERMS, SUB, LANES), f32),),
        in_specs=[smem, smem] + [vmem] * 6,
        out_specs=[vmem] * (pieces + 1),
        scratch_shapes=[pltpu.VMEM((MY // LANES, 4, SUB, LANES), f32), table, table],
        compiler_params=pltpu.CompilerParams(vmem_limit_bytes=8 << 20),
        name="ends",
    )(brick_mask, depth_rank, grade_strips, amp_strips, by_strips(near), by_strips(far), tf_table, mid)

    def exchange(parts):
        return [parts[0]] + [
            lax.ppermute(parts[k], "depth", [(i, i ^ k) for i in range(pieces)]) for k in range(1, pieces)
        ]

    inner = exchange(parts)
    rim = jax.ShapeDtypeStruct((4, SUB, cols // pieces // 2), f32)
    rims = pl.pallas_call(
        functools.partial(edge_kernel, pieces),
        out_shape=(rim,) * pieces,
        in_specs=[smem, smem, smem, vmem, vmem, vmem, vmem],
        out_specs=[vmem] * pieces,
        compiler_params=pltpu.CompilerParams(vmem_limit_bytes=4 << 20),
        name="edges",
    )(brick_mask, depth_rank, lat_rank, kept, kept_ends, pair, cross)
    edges = exchange(rims)
    return pl.pallas_call(
        functools.partial(finish_kernel, pieces),
        out_shape=piece,
        in_specs=[smem] + [vmem] * (2 * pieces),
        out_specs=vmem,
        compiler_params=pltpu.CompilerParams(vmem_limit_bytes=4 << 20),
        name="finish",
    )(depth_rank, *inner, *edges)


def solution(mesh):
    placed = (P("depth", "lat", None), P("depth", "lat", None), P(), P("depth", "lat", None))
    return jax.shard_map(
        local, mesh=mesh, in_specs=placed, out_specs=P(None, "lat", "depth"), check_vma=False
    )
```

```python
import functools

import jax
import jax.numpy as jnp
from jax import lax
from jax.experimental import pallas as pl
from jax.experimental.pallas import tpu as pltpu
from jax.sharding import PartitionSpec as P

MZ = 8
MX = 8
MY = 256
LANES = 128
SUB = 8
TERMS = 9


def sublane(shape):
    return lax.broadcasted_iota(jnp.int32, shape, len(shape) - 2)


def rows_kernel(last_parity, lat_ref, grade_hbm, amp_hbm, *refs):
    out_ref, sems = refs[-2:]
    slices, rows = grade_hbm.shape[:2]
    span = slices // 4

    def copies(first, places):
        made = []
        for f, src in enumerate((grade_hbm, amp_hbm)):
            for q in range(4):
                here = src.at[pl.ds(span * q, span), pl.ds(first, 2), :]
                made.append(pltpu.make_async_copy(here, out_ref.at[f, :, pl.ds(places[q], 2), :], sems.at[f, q]))
        for copy in made:
            copy.start()
        for copy in made:
            copy.wait()

    last = lax.rem(lat_ref[0], 2) == last_parity

    @pl.when(last)
    def _():
        copies(rows - 2, (0, 6, 4, 2))

    @pl.when(jnp.logical_not(last))
    def _():
        copies(0, (6, 4, 2, 0))


def slices_kernel(depth_ref, grade_hbm, amp_hbm, after_ref, near_ref, far_ref, sems):
    del after_ref
    slices = grade_hbm.shape[0]
    odd = lax.rem(depth_ref[0], 2)
    made = []
    for f, src in enumerate((grade_hbm, amp_hbm)):
        for n, (dst, at) in enumerate(((near_ref, 1 - odd), (far_ref, odd))):
            made.append(pltpu.make_async_copy(src.at[pl.ds(at * (slices - 2), 2)], dst.at[f], sems.at[f, n]))
    for copy in made:
        copy.start()
    for copy in made:
        copy.wait()


def round_weight(w):
    return w.astype(jnp.bfloat16).astype(jnp.float32)


def stencil(m2, m1, p1, p2):
    return (m2 - p2) + 8.0 * (p1 - m1)


def fill_tables(scale, table_ref, low_ref, high_ref):
    bins = table_ref.shape[1]
    table = (table_ref[...].astype(jnp.float32) / 65535.0).astype(jnp.bfloat16).astype(jnp.float32)
    table = jnp.where(sublane(table.shape) == 3, table * scale, table)
    column = lax.broadcasted_iota(jnp.int32, table.shape, 1)
    following = jnp.where(column == bins - 1, 0.0, pltpu.roll(table, bins - 1, 1))
    for c in range(4):
        low_ref[c] = jnp.broadcast_to(table[c:c + 1, :], (SUB, bins))
        high_ref[c] = jnp.broadcast_to(following[c:c + 1, :], (SUB, bins))


class Field:
    def __init__(self, ref, slices, strips, s):
        self.ref, self.strips = ref, strips
        self.per_slice = ref.shape[0] // slices
        self.s = s

    def load(self, z, rt, ds=0, k=0):
        start = pl.multiple_of((self.s + ds) * SUB, SUB) + (z * self.per_slice + rt * self.strips * SUB + k)
        return self.ref[pl.ds(start, SUB), :]

    def columns(self, z, rt, mid, lane):
        left = jnp.where(self.s > 0, self.load(z, rt, -jnp.minimum(self.s, 1)), 0.0)
        right = jnp.where(self.s < self.strips - 1, self.load(z, rt, jnp.minimum(self.strips - 1 - self.s, 1)), 0.0)
        return stencil(
            pltpu.roll(jnp.where(lane >= LANES - 2, left, mid), 2, 1),
            pltpu.roll(jnp.where(lane >= LANES - 1, left, mid), 1, 1),
            pltpu.roll(jnp.where(lane < 1, right, mid), LANES - 1, 1),
            pltpu.roll(jnp.where(lane < 2, right, mid), LANES - 2, 1),
        )

    def rows(self, z, rt, mid, sub, roll):
        def shifted(k):
            if k > 0:
                inside = sub < SUB - k
                if rt == 0:
                    return jnp.where(inside, self.load(z, 0, 0, k), self.load(z, 1, 0, k - SUB))
                return jnp.where(inside, pltpu.roll(mid, SUB - k, 0) if roll else self.load(z, 1, 0, k), 0.0)
            inside = sub >= -k
            if rt == 1:
                return jnp.where(inside, self.load(z, 1, 0, k), self.load(z, 0, 0, SUB + k))
            return jnp.where(inside, pltpu.roll(mid, -k, 0) if roll else self.load(z, 0, 0, k), 0.0)

        return stencil(*(shifted(k) for k in (-2, -1, 1, 2)))


def classify(grade, bins, low_ref, high_ref):
    position = grade * (bins - 1.0)
    index = jnp.minimum(position.astype(jnp.int32), bins - 1)
    w_low = 1.0 - (position - index.astype(jnp.float32))
    w_high = round_weight(1.0 - w_low)
    w_low = round_weight(w_low)

    def gather(ref, c):
        return jnp.take_along_axis(ref[c], index, axis=1)

    return [w_low * gather(low_ref, c) + w_high * gather(high_ref, c) for c in range(4)]


def step(state, terms):
    red, green, blue, trans = state
    g_x, a_x, g_yz, a_yz, steep, *cls = terms
    edge = 1.0 - 12.0 * lax.rsqrt(a_x * a_x + a_yz)
    shade = 0.3 + steep * lax.rsqrt(g_x * g_x + g_yz)
    weight = trans * (cls[3] * edge)
    trans = trans - weight
    weight = weight * shade
    return (red + weight * cls[0], green + weight * cls[1], blue + weight * cls[2], trans)


def cell_terms(fields, z, rt, along, roll, bins, low_ref, high_ref):
    lane = lax.broadcasted_iota(jnp.int32, (SUB, LANES), 1)
    sub = sublane((SUB, LANES))
    parts = []
    for field, near in zip(fields, along):
        mid = field.load(z, rt)
        dy = field.columns(z, rt, mid, lane)
        dz = stencil(*near)
        parts.append((mid, field.rows(z, rt, mid, sub, roll), dy * dy + dz * dz, dz))
    (grade, g_x, g_yz, g_z), (_, a_x, a_yz, _) = parts
    cls = classify(grade, bins, low_ref, high_ref)
    return (g_x, a_x, g_yz + 36.0, a_yz + 144.0, 0.7 * jnp.abs(g_z), *cls)


KEPT_AT = ((0, 4), (6, 2))


def keep(kept_ref, zi, s, rt, zb, terms):
    rows = slice(0, 2) if rt == 0 else slice(SUB - 2, SUB)
    at = KEPT_AT[rt][zb]
    for n, term in enumerate(terms):
        kept_ref[zi, s, n, at:at + 2, :] = term[rows, :]


def middle_kernel(scale, slices, strips, mask_ref, grade_ref, amp_ref, table_ref, mid_ref, kept_ref, low_ref, high_ref):
    bins = table_ref.shape[1]
    fill_tables(scale, table_ref, low_ref, high_ref)
    per_block = MY // LANES
    zero = jnp.zeros((SUB, LANES), jnp.float32)

    def block(cb, carry):
        for rt in range(2):
            for j in range(per_block):
                s = cb * per_block + j
                for c in range(3):
                    mid_ref[rt, s, c] = zero
                mid_ref[rt, s, 3] = zero + 1.0
            for zb in range(2):
                @pl.when(mask_ref[zb, rt, cb] != 0)
                def _():
                    for j in range(per_block):
                        s = cb * per_block + j
                        fields = [Field(ref, slices, strips, s) for ref in (grade_ref, amp_ref)]
                        state = tuple(mid_ref[rt, s, c] for c in range(4))
                        for zi in range(2 - 2 * zb, MZ - 2 * zb):
                            z = zb * MZ + zi
                            along = [[field.load(z + k, rt) for k in (-2, -1, 1, 2)] for field in fields]
                            terms = cell_terms(fields, z, rt, along, False, bins, low_ref, high_ref)
                            keep(kept_ref, zi, s, rt, zb, terms)
                            state = step(state, terms)
                        for c in range(4):
                            mid_ref[rt, s, c] = state[c]
        return carry

    lax.fori_loop(0, strips // per_block, block, 0)


def ends_kernel(scale, pieces, slices, strips, mask_ref, depth_ref, grade_ref, amp_ref, near_ref, far_ref, table_ref,
                mid_ref, *rest):
    outs, (kept_ref, acc_ref, low_ref, high_ref) = rest[:pieces], rest[pieces:]
    bins = table_ref.shape[1]
    fill_tables(scale, table_ref, low_ref, high_ref)
    per_block = MY // LANES
    piece_strips = strips // pieces
    piece_blocks = piece_strips // per_block
    zero = jnp.zeros((SUB, LANES), jnp.float32)
    odd = jnp.broadcast_to(lax.rem(depth_ref[0], 2), (SUB, LANES)) == 1

    def block(cb, carry):
        owner = lax.bitwise_xor(cb // piece_blocks, depth_ref[0])
        for rt in range(2):
            for zb in range(2):
                if zb == 0:
                    for j in range(per_block):
                        for c in range(3):
                            acc_ref[j, c] = zero
                        acc_ref[j, 3] = zero + 1.0
                else:
                    for j in range(per_block):
                        s = cb * per_block + j
                        trans = acc_ref[j, 3]
                        for c in range(3):
                            acc_ref[j, c] = acc_ref[j, c] + trans * mid_ref[rt, s, c]
                        acc_ref[j, 3] = trans * mid_ref[rt, s, 3]

                @pl.when(mask_ref[zb, rt, cb] != 0)
                def _():
                    for j in range(per_block):
                        s = cb * per_block + j
                        fields = [Field(ref, slices, strips, s) for ref in (grade_ref, amp_ref)]
                        halos = [[Field(ref, 4, strips, s) for ref in (near_ref, far_ref)]] * 2
                        state = tuple(acc_ref[j, c] for c in range(4))
                        for zi in (0, 1) if zb == 0 else (MZ - 2, MZ - 1):
                            z = zb * MZ + zi
                            along = []
                            for f in range(2):
                                near, far = halos[f]

                                def at(z):
                                    if 0 <= z < slices:
                                        return fields[f].load(z, rt)
                                    k = 2 * f + z % slices % 2
                                    one, two = near.load(k, rt), far.load(k, rt)
                                    return jnp.where(odd, one, two) if z < 0 else jnp.where(odd, two, one)

                                along.append([at(z + k) for k in (-2, -1, 1, 2)])
                            terms = cell_terms(fields, z, rt, along, True, bins, low_ref, high_ref)
                            keep(kept_ref, zi if zb == 0 else zi - 4, s, rt, zb, terms)
                            state = step(state, terms)
                        for c in range(4):
                            acc_ref[j, c] = state[c]
            for k in range(pieces):
                @pl.when(owner == k)
                def _():
                    for c in range(4):
                        for j in range(per_block):
                            part = lax.rem(cb, piece_blocks) * MY + j * LANES
                            lanes = pl.ds(pl.multiple_of(part, LANES), LANES)
                            outs[k][c, rt * SUB:(rt + 1) * SUB, lanes] = acc_ref[j, c]
        return carry

    lax.fori_loop(0, strips // per_block, block, 0)


def edge_kernel(pieces, mask_ref, depth_ref, lat_ref, kept_ref, ends_ref, pair_ref, cross_ref, *outs):
    half = kept_ref.shape[0]
    strips = kept_ref.shape[1]
    sub = sublane((SUB, LANES))
    is_first = lax.rem((sub + 2) // 4, 2) == 0
    odd_lat = jnp.broadcast_to(lax.rem(lat_ref[0], 2), (SUB, LANES))
    from_pair = lax.rem(sub // 2, 2) != odd_lat
    piece_strips = strips // pieces
    packs = piece_strips // 2

    above = lax.rem(sub // 2, 2) == 0
    even_row = lax.rem(sub, 2) == 0

    def outside(raw, above):
        mate = jnp.where(even_row, pltpu.roll(raw, SUB - 1, 0), pltpu.roll(raw, 1, 0))
        mate = jnp.where(above == even_row, 8.0 * mate, 0.0)
        return jnp.where(above, raw - mate, mate - raw)

    def halo(f, zi, lanes):
        pair, cross = pair_ref[f, zi % 4, :, lanes], cross_ref[f, zi % 4, :, lanes]
        if zi < 4:
            return outside(jnp.where(from_pair, pair, cross), above)
        return outside(pltpu.roll(jnp.where(from_pair, cross, pair), 2, 0), above)

    def strip(s):
        lanes = pl.ds(pl.multiple_of(s * LANES, LANES), LANES)
        cb = s // (MY // LANES)
        full = [[jnp.broadcast_to(mask_ref[zb, rt, cb], (SUB, LANES)) for rt in range(2)] for zb in range(2)]
        live = jnp.where(
            sub < 4, jnp.where(sub < 2, full[0][0], full[1][1]), jnp.where(sub < 6, full[1][0], full[0][1])
        ) != 0
        zero = jnp.zeros((SUB, LANES), jnp.float32)
        total = [zero, zero, zero]
        trans = zero + 1.0
        for zi in range(half):
            terms = [kept_ref[zi, s, n] for n in range(TERMS)]
            if zi < 2:
                terms = [jnp.where(is_first, ends_ref[zi, s, n], term) for n, term in enumerate(terms)]
            if zi >= half - 2:
                terms = [jnp.where(is_first, term, ends_ref[zi - half + 4, s, n]) for n, term in enumerate(terms)]
            g_x, a_x, g_yz, a_yz, steep, red, green, blue, alpha = terms
            g_x = g_x + halo(0, zi, lanes)
            a_x = a_x + halo(1, zi, lanes)
            edge = 1.0 - 12.0 * lax.rsqrt(a_x * a_x + a_yz)
            shade = 0.3 + steep * lax.rsqrt(g_x * g_x + g_yz)
            weight = jnp.where(live, trans * (alpha * edge), 0.0)
            trans = trans - weight
            weight = weight * shade
            total = [t + jnp.where(live, weight * c, 0.0) for t, c in zip(total, (red, green, blue))]
        out = [t + trans * pltpu.roll(t, 4, 0) for t in total]
        return out + [trans * pltpu.roll(trans, 4, 0)]

    def piece(p, carry):
        results = [strip(p * piece_strips + j) for j in range(piece_strips)]
        owner = lax.bitwise_xor(p, depth_ref[0])
        for j in range(packs):
            packed = [
                jnp.where(is_first, one, pltpu.roll(two, 4, 0)) for one, two in zip(results[j], results[j + packs])
            ]
            for k in range(pieces):
                @pl.when(owner == k)
                def _():
                    for c in range(4):
                        outs[k][c, :, j * LANES:(j + 1) * LANES] = packed[c]
        return carry

    lax.fori_loop(0, pieces, piece, 0)


def fold(parts, rank):
    level = 0
    while len(parts) > 1:
        first = lax.rem(lax.shift_right_logical(rank, level), 2) == 0
        merged = []
        for mine, other in zip(parts[0::2], parts[1::2]):
            first_here = jnp.broadcast_to(first, mine[3].shape)
            clear = jnp.where(first_here, mine[3], other[3])
            merged.append(
                [jnp.where(first_here, m, o) + clear * jnp.where(first_here, o, m) for m, o in zip(mine[:3], other[:3])]
                + [mine[3] * other[3]]
            )
        parts = merged
        level += 1
    return parts[0][:3] + [1.0 - parts[0][3]]


def finish_kernel(pieces, depth_ref, *refs):
    inner, edges, out_ref = refs[:pieces], refs[pieces:2 * pieces], refs[-1]
    rows, cols = out_ref.shape[1:]
    rank = depth_ref[0]
    frame = fold([[ref[c] for c in range(4)] for ref in inner], rank)
    rim = fold([[ref[c] for c in range(4)] for ref in edges], rank)
    for c in range(4):
        packed = rim[c]
        wide = jnp.concatenate([packed, pltpu.roll(packed, 4, 0)], axis=1)
        sub = sublane(wide.shape)
        out_ref[c, 0:SUB, :] = jnp.where(sub < 2, wide, frame[c][0:SUB, :])
        out_ref[c, rows - SUB:rows, :] = jnp.where(sub >= SUB - 2, wide, frame[c][rows - SUB:rows, :])


def swap_near(x, axis):
    return lax.ppermute(x, axis, [(i, i ^ 1) for i in range(lax.axis_size(axis))])


def swap_far(x, axis):
    size = lax.axis_size(axis)
    return lax.ppermute(x, axis, [(i, j) for k in range(1, size - 1, 2) for i, j in ((k, k + 1), (k + 1, k))])


def by_strips(array):
    rows, cols = array.shape[-2:]
    split = array.reshape(-1, rows // SUB, SUB, cols // LANES, LANES)
    return split.transpose(0, 1, 3, 2, 4).reshape(-1, LANES)


def local(grade_field, amplitude, tf_table, brick_mask):
    slices, rows, cols = grade_field.shape
    assert (slices, rows) == (2 * MZ, 2 * MX)
    pieces = lax.axis_size("depth")
    depth_rank = lax.axis_index("depth").astype(jnp.int32).reshape(1)
    lat_rank = lax.axis_index("lat").astype(jnp.int32).reshape(1)
    f32 = jnp.float32
    vmem = pl.BlockSpec(memory_space=pltpu.VMEM)
    smem = pl.BlockSpec(memory_space=pltpu.SMEM)
    hbm = pl.BlockSpec(memory_space=pltpu.MemorySpace.HBM)
    lat_halo = jax.ShapeDtypeStruct((2, slices // 4, SUB, cols), f32)
    depth_halo = jax.ShapeDtypeStruct((2, 2, rows, cols), f32)
    hbm_only = pltpu.MemorySpace.HBM
    fields = (grade_field, amplitude)
    grade_field = pltpu.with_memory_space_constraint(grade_field, hbm_only)
    amplitude = pltpu.with_memory_space_constraint(amplitude, hbm_only)
    small = pltpu.CompilerParams(vmem_limit_bytes=4 << 20)
    after = pl.BlockSpec(memory_space=pl.ANY)

    def take_rows(last_parity, *earlier):
        return pl.pallas_call(
            functools.partial(rows_kernel, last_parity),
            out_shape=lat_halo,
            in_specs=[smem, hbm, hbm] + [after] * len(earlier),
            out_specs=vmem,
            scratch_shapes=[pltpu.SemaphoreType.DMA((2, 4))],
            compiler_params=small,
            name="take_rows",
        )(lat_rank, grade_field, amplitude, *earlier)

    pair = take_rows(0)
    cross = take_rows(1, pair)
    near, far = pl.pallas_call(
        slices_kernel,
        out_shape=(depth_halo, depth_halo),
        in_specs=[smem, hbm, hbm, after],
        out_specs=[vmem, vmem],
        scratch_shapes=[pltpu.SemaphoreType.DMA((2, 2))],
        compiler_params=small,
        name="take_slices",
    )(depth_rank, grade_field, amplitude, cross)
    pair = swap_near(pair, "lat")
    cross = swap_far(cross, "lat")
    near = swap_near(near, "depth")
    far = swap_far(far, "depth")
    piece = jax.ShapeDtypeStruct((4, rows, cols // pieces), f32)
    scale = 4.0 / (slices * pieces)
    strips = cols // LANES
    table = pltpu.VMEM((4, SUB, tf_table.shape[1]), f32)
    grade_strips, amp_strips = by_strips(fields[0]), by_strips(fields[1])
    mid, kept = pl.pallas_call(
        functools.partial(middle_kernel, scale, slices, strips),
        out_shape=(
            jax.ShapeDtypeStruct((2, strips, 4, SUB, LANES), f32),
            jax.ShapeDtypeStruct((MZ, strips, TERMS, SUB, LANES), f32),
        ),
        in_specs=[smem, vmem, vmem, vmem],
        out_specs=[vmem, vmem],
        scratch_shapes=[table, table],
        compiler_params=pltpu.CompilerParams(vmem_limit_bytes=8 << 20),
        cost_estimate=pl.CostEstimate(flops=10**10, bytes_accessed=10**8, transcendentals=0),
        name="middle",
    )(brick_mask, grade_strips, amp_strips, tf_table)
    *parts, kept_ends = pl.pallas_call(
        functools.partial(ends_kernel, scale, pieces, slices, strips),
        out_shape=(piece,) * pieces + (jax.ShapeDtypeStruct((4, strips, TERMS, SUB, LANES), f32),),
        in_specs=[smem, smem] + [vmem] * 6,
        out_specs=[vmem] * (pieces + 1),
        scratch_shapes=[pltpu.VMEM((MY // LANES, 4, SUB, LANES), f32), table, table],
        compiler_params=pltpu.CompilerParams(vmem_limit_bytes=8 << 20),
        name="ends",
    )(brick_mask, depth_rank, grade_strips, amp_strips, by_strips(near), by_strips(far), tf_table, mid)

    def exchange(parts):
        return [parts[0]] + [
            lax.ppermute(parts[k], "depth", [(i, i ^ k) for i in range(pieces)]) for k in range(1, pieces)
        ]

    inner = exchange(parts)
    rim = jax.ShapeDtypeStruct((4, SUB, cols // pieces // 2), f32)
    rims = pl.pallas_call(
        functools.partial(edge_kernel, pieces),
        out_shape=(rim,) * pieces,
        in_specs=[smem, smem, smem, vmem, vmem, vmem, vmem],
        out_specs=[vmem] * pieces,
        compiler_params=pltpu.CompilerParams(vmem_limit_bytes=4 << 20),
        name="edges",
    )(brick_mask, depth_rank, lat_rank, kept, kept_ends, pair, cross)
    edges = exchange(rims)
    return pl.pallas_call(
        functools.partial(finish_kernel, pieces),
        out_shape=piece,
        in_specs=[smem] + [vmem] * (2 * pieces),
        out_specs=vmem,
        compiler_params=pltpu.CompilerParams(vmem_limit_bytes=4 << 20),
        name="finish",
    )(depth_rank, *inner, *edges)


def solution(mesh):
    placed = (P("depth", "lat", None), P("depth", "lat", None), P(), P("depth", "lat", None))
    return jax.shard_map(
        local, mesh=mesh, in_specs=placed, out_specs=P(None, "lat", "depth"), check_vma=False
    )
```

```python
import functools

import jax
import jax.numpy as jnp
from jax import lax
from jax.experimental import pallas as pl
from jax.experimental.pallas import tpu as pltpu
from jax.sharding import PartitionSpec as P

MZ = 8
MX = 8
MY = 256
LANES = 128
SUB = 8
TERMS = 9


def sublane(shape):
    return lax.broadcasted_iota(jnp.int32, shape, len(shape) - 2)


def rows_kernel(last_parity, lat_ref, grade_hbm, amp_hbm, *refs):
    out_ref, sems = refs[-2:]
    slices, rows = grade_hbm.shape[:2]
    span = slices // 4

    def copies(first, places):
        made = []
        for f, src in enumerate((grade_hbm, amp_hbm)):
            for q in range(4):
                here = src.at[pl.ds(span * q, span), pl.ds(first, 2), :]
                made.append(pltpu.make_async_copy(here, out_ref.at[f, :, pl.ds(places[q], 2), :], sems.at[f, q]))
        for copy in made:
            copy.start()
        for copy in made:
            copy.wait()

    last = lax.rem(lat_ref[0], 2) == last_parity

    @pl.when(last)
    def _():
        copies(rows - 2, (0, 6, 4, 2))

    @pl.when(jnp.logical_not(last))
    def _():
        copies(0, (6, 4, 2, 0))


def slices_kernel(depth_ref, grade_hbm, amp_hbm, after_ref, near_ref, far_ref, sems):
    del after_ref
    slices = grade_hbm.shape[0]
    odd = lax.rem(depth_ref[0], 2)
    made = []
    for f, src in enumerate((grade_hbm, amp_hbm)):
        for n, (dst, at) in enumerate(((near_ref, 1 - odd), (far_ref, odd))):
            made.append(pltpu.make_async_copy(src.at[pl.ds(at * (slices - 2), 2)], dst.at[f], sems.at[f, n]))
    for copy in made:
        copy.start()
    for copy in made:
        copy.wait()


def round_weight(w):
    return w.astype(jnp.bfloat16).astype(jnp.float32)


def stencil(m2, m1, p1, p2):
    return (m2 - p2) + 8.0 * (p1 - m1)


def fill_tables(scale, table_ref, low_ref, high_ref):
    bins = table_ref.shape[1]
    table = (table_ref[...].astype(jnp.float32) / 65535.0).astype(jnp.bfloat16).astype(jnp.float32)
    table = jnp.where(sublane(table.shape) == 3, table * scale, table)
    column = lax.broadcasted_iota(jnp.int32, table.shape, 1)
    following = jnp.where(column == bins - 1, 0.0, pltpu.roll(table, bins - 1, 1))
    for c in range(4):
        low_ref[c] = jnp.broadcast_to(table[c:c + 1, :], (SUB, bins))
        high_ref[c] = jnp.broadcast_to(following[c:c + 1, :], (SUB, bins))


class Field:
    def __init__(self, ref, slices, strips, s):
        self.ref, self.strips = ref, strips
        self.per_slice = ref.shape[0] // slices
        self.s = s

    def load(self, z, rt, ds=0, k=0):
        start = pl.multiple_of((self.s + ds) * SUB, SUB) + (z * self.per_slice + rt * self.strips * SUB + k)
        return self.ref[pl.ds(start, SUB), :]

    def columns(self, z, rt, mid, lane):
        left = jnp.where(self.s > 0, self.load(z, rt, -jnp.minimum(self.s, 1)), 0.0)
        right = jnp.where(self.s < self.strips - 1, self.load(z, rt, jnp.minimum(self.strips - 1 - self.s, 1)), 0.0)
        return stencil(
            pltpu.roll(jnp.where(lane >= LANES - 2, left, mid), 2, 1),
            pltpu.roll(jnp.where(lane >= LANES - 1, left, mid), 1, 1),
            pltpu.roll(jnp.where(lane < 1, right, mid), LANES - 1, 1),
            pltpu.roll(jnp.where(lane < 2, right, mid), LANES - 2, 1),
        )

    def rows(self, z, rt, mid, sub, roll):
        def shifted(k):
            if k > 0:
                inside = sub < SUB - k
                if rt == 0:
                    return jnp.where(inside, self.load(z, 0, 0, k), self.load(z, 1, 0, k - SUB))
                return jnp.where(inside, pltpu.roll(mid, SUB - k, 0) if roll else self.load(z, 1, 0, k), 0.0)
            inside = sub >= -k
            if rt == 1:
                return jnp.where(inside, self.load(z, 1, 0, k), self.load(z, 0, 0, SUB + k))
            return jnp.where(inside, pltpu.roll(mid, -k, 0) if roll else self.load(z, 0, 0, k), 0.0)

        return stencil(*(shifted(k) for k in (-2, -1, 1, 2)))


def classify(grade, bins, low_ref, high_ref):
    position = grade * (bins - 1.0)
    index = jnp.minimum(position.astype(jnp.int32), bins - 1)
    w_low = 1.0 - (position - index.astype(jnp.float32))
    w_high = round_weight(1.0 - w_low)
    w_low = round_weight(w_low)

    def gather(ref, c):
        return jnp.take_along_axis(ref[c], index, axis=1)

    return [w_low * gather(low_ref, c) + w_high * gather(high_ref, c) for c in range(4)]


def step(state, terms):
    red, green, blue, trans = state
    g_x, a_x, g_yz, a_yz, steep, *cls = terms
    edge = 1.0 - 12.0 * lax.rsqrt(a_x * a_x + a_yz)
    shade = 0.3 + steep * lax.rsqrt(g_x * g_x + g_yz)
    weight = trans * (cls[3] * edge)
    trans = trans - weight
    weight = weight * shade
    return (red + weight * cls[0], green + weight * cls[1], blue + weight * cls[2], trans)


def cell_terms(fields, z, rt, along, roll, bins, low_ref, high_ref):
    lane = lax.broadcasted_iota(jnp.int32, (SUB, LANES), 1)
    sub = sublane((SUB, LANES))
    parts = []
    for field, near in zip(fields, along):
        mid = field.load(z, rt)
        dy = field.columns(z, rt, mid, lane)
        dz = stencil(*near)
        parts.append((mid, field.rows(z, rt, mid, sub, roll), dy * dy + dz * dz, dz))
    (grade, g_x, g_yz, g_z), (_, a_x, a_yz, _) = parts
    cls = classify(grade, bins, low_ref, high_ref)
    return (g_x, a_x, g_yz + 36.0, a_yz + 144.0, 0.7 * jnp.abs(g_z), *cls)


KEPT_AT = ((0, 4), (6, 2))


def keep(kept_ref, zi, s, rt, zb, terms):
    rows = slice(0, 2) if rt == 0 else slice(SUB - 2, SUB)
    at = KEPT_AT[rt][zb]
    for n, term in enumerate(terms):
        kept_ref[zi, s, n, at:at + 2, :] = term[rows, :]


def middle_kernel(scale, slices, strips, mask_ref, grade_ref, amp_ref, table_ref, mid_ref, kept_ref, low_ref, high_ref):
    bins = table_ref.shape[1]
    fill_tables(scale, table_ref, low_ref, high_ref)
    per_block = MY // LANES
    zero = jnp.zeros((SUB, LANES), jnp.float32)

    def block(cb, carry):
        for rt in range(2):
            for j in range(per_block):
                s = cb * per_block + j
                for c in range(3):
                    mid_ref[rt, s, c] = zero
                mid_ref[rt, s, 3] = zero + 1.0
            for zb in range(2):
                @pl.when(mask_ref[zb, rt, cb] != 0)
                def _():
                    for j in range(per_block):
                        s = cb * per_block + j
                        fields = [Field(ref, slices, strips, s) for ref in (grade_ref, amp_ref)]
                        state = tuple(mid_ref[rt, s, c] for c in range(4))
                        for zi in range(2 - 2 * zb, MZ - 2 * zb):
                            z = zb * MZ + zi
                            along = [[field.load(z + k, rt) for k in (-2, -1, 1, 2)] for field in fields]
                            terms = cell_terms(fields, z, rt, along, False, bins, low_ref, high_ref)
                            keep(kept_ref, zi, s, rt, zb, terms)
                            state = step(state, terms)
                        for c in range(4):
                            mid_ref[rt, s, c] = state[c]
        return carry

    lax.fori_loop(0, strips // per_block, block, 0)


def ends_kernel(scale, pieces, slices, strips, mask_ref, depth_ref, grade_ref, amp_ref, near_ref, far_ref, table_ref,
                mid_ref, *rest):
    outs, (kept_ref, acc_ref, low_ref, high_ref) = rest[:2], rest[2:]
    bins = table_ref.shape[1]
    fill_tables(scale, table_ref, low_ref, high_ref)
    per_block = MY // LANES
    piece_strips = strips // pieces
    piece_blocks = piece_strips // per_block
    zero = jnp.zeros((SUB, LANES), jnp.float32)
    odd = jnp.broadcast_to(lax.rem(depth_ref[0], 2), (SUB, LANES)) == 1

    def block(cb, carry):
        owner = lax.bitwise_xor(cb // piece_blocks, depth_ref[0])
        for rt in range(2):
            for zb in range(2):
                if zb == 0:
                    for j in range(per_block):
                        for c in range(3):
                            acc_ref[j, c] = zero
                        acc_ref[j, 3] = zero + 1.0
                else:
                    for j in range(per_block):
                        s = cb * per_block + j
                        trans = acc_ref[j, 3]
                        for c in range(3):
                            acc_ref[j, c] = acc_ref[j, c] + trans * mid_ref[rt, s, c]
                        acc_ref[j, 3] = trans * mid_ref[rt, s, 3]

                @pl.when(mask_ref[zb, rt, cb] != 0)
                def _():
                    for j in range(per_block):
                        s = cb * per_block + j
                        fields = [Field(ref, slices, strips, s) for ref in (grade_ref, amp_ref)]
                        halos = [[Field(ref, 4, strips, s) for ref in (near_ref, far_ref)]] * 2
                        state = tuple(acc_ref[j, c] for c in range(4))
                        for zi in (0, 1) if zb == 0 else (MZ - 2, MZ - 1):
                            z = zb * MZ + zi
                            along = []
                            for f in range(2):
                                near, far = halos[f]

                                def at(z):
                                    if 0 <= z < slices:
                                        return fields[f].load(z, rt)
                                    k = 2 * f + z % slices % 2
                                    one, two = near.load(k, rt), far.load(k, rt)
                                    return jnp.where(odd, one, two) if z < 0 else jnp.where(odd, two, one)

                                along.append([at(z + k) for k in (-2, -1, 1, 2)])
                            terms = cell_terms(fields, z, rt, along, True, bins, low_ref, high_ref)
                            keep(kept_ref, zi if zb == 0 else zi - 4, s, rt, zb, terms)
                            state = step(state, terms)
                        for c in range(4):
                            acc_ref[j, c] = state[c]
            for k, out in enumerate(outs):
                @pl.when(lax.rem(owner, 2) == k)
                def _():
                    for c in range(4):
                        for j in range(per_block):
                            part = lax.rem(cb, piece_blocks) * MY + j * LANES
                            lanes = pl.ds(pl.multiple_of(part, LANES), LANES)
                            out[owner // 2, c, rt * SUB:(rt + 1) * SUB, lanes] = acc_ref[j, c]
        return carry

    lax.fori_loop(0, strips // per_block, block, 0)


def edge_kernel(pieces, first, mask_ref, depth_ref, lat_ref, kept_ref, ends_ref, pair_ref, cross_ref, *refs):
    out_ref = refs[-1]
    half = kept_ref.shape[0]
    strips = kept_ref.shape[1]
    sub = sublane((SUB, LANES))
    is_first = lax.rem((sub + 2) // 4, 2) == 0
    odd_lat = jnp.broadcast_to(lax.rem(lat_ref[0], 2), (SUB, LANES))
    from_pair = lax.rem(sub // 2, 2) != odd_lat
    piece_strips = strips // pieces
    packs = piece_strips // 2

    above = lax.rem(sub // 2, 2) == 0
    even_row = lax.rem(sub, 2) == 0

    def outside(raw, above):
        mate = jnp.where(even_row, pltpu.roll(raw, SUB - 1, 0), pltpu.roll(raw, 1, 0))
        mate = jnp.where(above == even_row, 8.0 * mate, 0.0)
        return jnp.where(above, raw - mate, mate - raw)

    def halo(f, zi, lanes):
        pair, cross = pair_ref[f, zi % 4, :, lanes], cross_ref[f, zi % 4, :, lanes]
        if zi < 4:
            return outside(jnp.where(from_pair, pair, cross), above)
        return outside(pltpu.roll(jnp.where(from_pair, cross, pair), 2, 0), above)

    def strip(s):
        lanes = pl.ds(pl.multiple_of(s * LANES, LANES), LANES)
        cb = s // (MY // LANES)
        full = [[jnp.broadcast_to(mask_ref[zb, rt, cb], (SUB, LANES)) for rt in range(2)] for zb in range(2)]
        live = jnp.where(
            sub < 4, jnp.where(sub < 2, full[0][0], full[1][1]), jnp.where(sub < 6, full[1][0], full[0][1])
        ) != 0
        zero = jnp.zeros((SUB, LANES), jnp.float32)
        total = [zero, zero, zero]
        trans = zero + 1.0
        for zi in range(half):
            terms = [kept_ref[zi, s, n] for n in range(TERMS)]
            if zi < 2:
                terms = [jnp.where(is_first, ends_ref[zi, s, n], term) for n, term in enumerate(terms)]
            if zi >= half - 2:
                terms = [jnp.where(is_first, term, ends_ref[zi - half + 4, s, n]) for n, term in enumerate(terms)]
            g_x, a_x, g_yz, a_yz, steep, red, green, blue, alpha = terms
            g_x = g_x + halo(0, zi, lanes)
            a_x = a_x + halo(1, zi, lanes)
            edge = 1.0 - 12.0 * lax.rsqrt(a_x * a_x + a_yz)
            shade = 0.3 + steep * lax.rsqrt(g_x * g_x + g_yz)
            weight = jnp.where(live, trans * (alpha * edge), 0.0)
            trans = trans - weight
            weight = weight * shade
            total = [t + jnp.where(live, weight * c, 0.0) for t, c in zip(total, (red, green, blue))]
        out = [t + trans * pltpu.roll(t, 4, 0) for t in total]
        return out + [trans * pltpu.roll(trans, 4, 0)]

    def piece(n, carry):
        p = lax.bitwise_xor(first + n, depth_ref[0])
        results = [strip(p * piece_strips + j) for j in range(piece_strips)]
        for j in range(packs):
            packed = [
                jnp.where(is_first, one, pltpu.roll(two, 4, 0)) for one, two in zip(results[j], results[j + packs])
            ]
            for c in range(4):
                out_ref[n, c, :, j * LANES:(j + 1) * LANES] = packed[c]
        return carry

    lax.fori_loop(0, pieces // 2, piece, 0)


def merge(mine, other, rank, level):
    ahead = jnp.broadcast_to(lax.rem(lax.shift_right_logical(rank, level), 2), mine[3].shape) == 0
    clear = jnp.where(ahead, mine[3], other[3])
    return [
        jnp.where(ahead, m, o) + clear * jnp.where(ahead, o, m) for m, o in zip(mine[:3], other[:3])
    ] + [mine[3] * other[3]]


def channels(ref):
    return [ref[c] for c in range(4)]


def merge_kernel(depth_ref, stay_ref, got_ref, own_ref, away_ref):
    for n, out_ref in enumerate((own_ref, away_ref)):
        for c, value in enumerate(merge(channels(stay_ref.at[n]), channels(got_ref.at[n]), depth_ref[0], 0)):
            out_ref[c] = value


def finish_kernel(depth_ref, own_ref, got_ref, home_ref, beside_ref, across_ref, corner_ref, out_ref):
    rows = out_ref.shape[1]
    rank = depth_ref[0]
    frame = merge(channels(own_ref), channels(got_ref), rank, 1)
    near = merge(channels(home_ref.at[0]), channels(beside_ref.at[1]), rank, 0)
    far = merge(channels(across_ref.at[0]), channels(corner_ref.at[1]), rank, 0)
    rim = merge(near, far, rank, 1)
    for c in range(4):
        inner, packed = frame[c], rim[c]
        if c == 3:
            inner, packed = 1.0 - inner, 1.0 - packed
        wide = jnp.concatenate([packed, pltpu.roll(packed, 4, 0)], axis=1)
        sub = sublane(wide.shape)
        out_ref[c, 0:SUB, :] = jnp.where(sub < 2, wide, inner[0:SUB, :])
        out_ref[c, rows - SUB:rows, :] = jnp.where(sub >= SUB - 2, wide, inner[rows - SUB:rows, :])


def swap_near(x, axis):
    return lax.ppermute(x, axis, [(i, i ^ 1) for i in range(lax.axis_size(axis))])


def swap_far(x, axis):
    size = lax.axis_size(axis)
    return lax.ppermute(x, axis, [(i, j) for k in range(1, size - 1, 2) for i, j in ((k, k + 1), (k + 1, k))])


def by_strips(array):
    rows, cols = array.shape[-2:]
    split = array.reshape(-1, rows // SUB, SUB, cols // LANES, LANES)
    return split.transpose(0, 1, 3, 2, 4).reshape(-1, LANES)


def local(grade_field, amplitude, tf_table, brick_mask):
    slices, rows, cols = grade_field.shape
    pieces = lax.axis_size("depth")
    assert (slices, rows, pieces) == (2 * MZ, 2 * MX, 4)
    depth_rank = lax.axis_index("depth").astype(jnp.int32).reshape(1)
    lat_rank = lax.axis_index("lat").astype(jnp.int32).reshape(1)
    f32 = jnp.float32
    vmem = pl.BlockSpec(memory_space=pltpu.VMEM)
    smem = pl.BlockSpec(memory_space=pltpu.SMEM)
    hbm = pl.BlockSpec(memory_space=pltpu.MemorySpace.HBM)
    lat_halo = jax.ShapeDtypeStruct((2, slices // 4, SUB, cols), f32)
    depth_halo = jax.ShapeDtypeStruct((2, 2, rows, cols), f32)
    hbm_only = pltpu.MemorySpace.HBM
    fields = (grade_field, amplitude)
    grade_field = pltpu.with_memory_space_constraint(grade_field, hbm_only)
    amplitude = pltpu.with_memory_space_constraint(amplitude, hbm_only)
    small = pltpu.CompilerParams(vmem_limit_bytes=4 << 20)
    after = pl.BlockSpec(memory_space=pl.ANY)

    def take_rows(last_parity, *earlier):
        return pl.pallas_call(
            functools.partial(rows_kernel, last_parity),
            out_shape=lat_halo,
            in_specs=[smem, hbm, hbm] + [after] * len(earlier),
            out_specs=vmem,
            scratch_shapes=[pltpu.SemaphoreType.DMA((2, 4))],
            compiler_params=small,
            name="take_rows",
        )(lat_rank, grade_field, amplitude, *earlier)

    pair = take_rows(0)
    near, far = pl.pallas_call(
        slices_kernel,
        out_shape=(depth_halo, depth_halo),
        in_specs=[smem, hbm, hbm, after],
        out_specs=[vmem, vmem],
        scratch_shapes=[pltpu.SemaphoreType.DMA((2, 2))],
        compiler_params=small,
        name="take_slices",
    )(depth_rank, grade_field, amplitude, pair)
    cross = take_rows(1, far)
    pair = swap_near(pair, "lat")
    cross = swap_far(cross, "lat")
    near = swap_near(near, "depth")
    far = swap_far(far, "depth")
    piece = jax.ShapeDtypeStruct((4, rows, cols // pieces), f32)
    half = jax.ShapeDtypeStruct((2, *piece.shape), f32)
    scale = 4.0 / (slices * pieces)
    strips = cols // LANES
    table = pltpu.VMEM((4, SUB, tf_table.shape[1]), f32)
    grade_strips, amp_strips = by_strips(fields[0]), by_strips(fields[1])
    mid, kept = pl.pallas_call(
        functools.partial(middle_kernel, scale, slices, strips),
        out_shape=(
            jax.ShapeDtypeStruct((2, strips, 4, SUB, LANES), f32),
            jax.ShapeDtypeStruct((MZ, strips, TERMS, SUB, LANES), f32),
        ),
        in_specs=[smem, vmem, vmem, vmem],
        out_specs=[vmem, vmem],
        scratch_shapes=[table, table],
        compiler_params=pltpu.CompilerParams(vmem_limit_bytes=8 << 20),
        cost_estimate=pl.CostEstimate(flops=10**10, bytes_accessed=10**8, transcendentals=0),
        name="middle",
    )(brick_mask, grade_strips, amp_strips, tf_table)
    stay, go, kept_ends = pl.pallas_call(
        functools.partial(ends_kernel, scale, pieces, slices, strips),
        out_shape=(half, half, jax.ShapeDtypeStruct((4, strips, TERMS, SUB, LANES), f32)),
        in_specs=[smem, smem] + [vmem] * 6,
        out_specs=[vmem] * 3,
        scratch_shapes=[pltpu.VMEM((MY // LANES, 4, SUB, LANES), f32), table, table],
        compiler_params=pltpu.CompilerParams(vmem_limit_bytes=8 << 20),
        name="ends",
    )(brick_mask, depth_rank, grade_strips, amp_strips, by_strips(near), by_strips(far), tf_table, mid)

    def swap_across(x):
        return lax.ppermute(x, "depth", [(i, i ^ 2) for i in range(pieces)])

    own, away_inner = pl.pallas_call(
        merge_kernel,
        out_shape=(piece, piece),
        in_specs=[smem, vmem, vmem],
        out_specs=[vmem, vmem],
        compiler_params=small,
        name="merge",
    )(depth_rank, stay, swap_near(go, "depth"))
    got = swap_across(away_inner)
    rims = jax.ShapeDtypeStruct((2, 4, SUB, cols // pieces // 2), f32)

    def edges_of(first, *earlier):
        return pl.pallas_call(
            functools.partial(edge_kernel, pieces, first),
            out_shape=rims,
            in_specs=[smem, smem, smem, vmem, vmem, vmem, vmem] + [after] * len(earlier),
            out_specs=vmem,
            compiler_params=small,
            name="edges",
        )(brick_mask, depth_rank, lat_rank, kept, kept_ends, pair, cross, *earlier)

    away = edges_of(2, away_inner)
    home = edges_of(0, away)
    across = swap_across(away)
    edges = (home, swap_near(home, "depth"), across, swap_near(across, "depth"))
    return pl.pallas_call(
        finish_kernel,
        out_shape=piece,
        in_specs=[smem] + [vmem] * 6,
        out_specs=vmem,
        compiler_params=small,
        name="finish",
    )(depth_rank, own, got, *edges)


def solution(mesh):
    placed = (P("depth", "lat", None), P("depth", "lat", None), P(), P("depth", "lat", None))
    return jax.shard_map(
        local, mesh=mesh, in_specs=placed, out_specs=P(None, "lat", "depth"), check_vma=False
    )
```

```python
import functools

import jax
import jax.numpy as jnp
from jax import lax
from jax.experimental import pallas as pl
from jax.experimental.pallas import tpu as pltpu
from jax.sharding import PartitionSpec as P

MZ = 8
MX = 8
MY = 256
LANES = 128
SUB = 8
TERMS = 9


def sublane(shape):
    return lax.broadcasted_iota(jnp.int32, shape, len(shape) - 2)


def take_kernel(lat_ref, depth_ref, grade_hbm, amp_hbm, pair_ref, cross_ref, near_ref, far_ref, sems, depth_sems):
    slices, rows = grade_hbm.shape[:2]
    span = slices // 4
    odd = lax.rem(depth_ref[0], 2)
    fields = (grade_hbm, amp_hbm)

    def copies(above_dst, below_dst):
        made = []
        for f, src in enumerate(fields):
            for q in range(4):
                part = pl.ds(span * q, span)
                above = above_dst.at[f, :, pl.ds((0, 6, 4, 2)[q], 2), :]
                below = below_dst.at[f, :, pl.ds((6, 4, 2, 0)[q], 2), :]
                made.append(pltpu.make_async_copy(src.at[part, pl.ds(rows - 2, 2), :], above, sems.at[f, q, 0]))
                made.append(pltpu.make_async_copy(src.at[part, pl.ds(0, 2), :], below, sems.at[f, q, 1]))
        for f, src in enumerate(fields):
            for n, (dst, at) in enumerate(((near_ref, 1 - odd), (far_ref, odd))):
                here = src.at[pl.ds(at * (slices - 2), 2)]
                made.append(pltpu.make_async_copy(here, dst.at[f], depth_sems.at[f, n]))
        for copy in made:
            copy.start()
        for copy in made:
            copy.wait()

    even = lax.rem(lat_ref[0], 2) == 0

    @pl.when(even)
    def _():
        copies(pair_ref, cross_ref)

    @pl.when(jnp.logical_not(even))
    def _():
        copies(cross_ref, pair_ref)


def pass_on_kernel(*refs):
    del refs


def pass_on(x, *earlier):
    spec = pl.BlockSpec(memory_space=pl.ANY)
    return pl.pallas_call(
        pass_on_kernel,
        out_shape=jax.ShapeDtypeStruct(x.shape, x.dtype),
        in_specs=[spec] * (1 + len(earlier)),
        out_specs=spec,
        input_output_aliases={0: 0},
        compiler_params=pltpu.CompilerParams(vmem_limit_bytes=1 << 20),
        name="pass_on",
    )(x, *earlier)


def round_weight(w):
    return w.astype(jnp.bfloat16).astype(jnp.float32)


def stencil(m2, m1, p1, p2):
    return (m2 - p2) + 8.0 * (p1 - m1)


def fill_tables(scale, table_ref, low_ref, high_ref):
    bins = table_ref.shape[1]
    table = (table_ref[...].astype(jnp.float32) / 65535.0).astype(jnp.bfloat16).astype(jnp.float32)
    table = jnp.where(sublane(table.shape) == 3, table * scale, table)
    column = lax.broadcasted_iota(jnp.int32, table.shape, 1)
    following = jnp.where(column == bins - 1, 0.0, pltpu.roll(table, bins - 1, 1))
    for c in range(4):
        low_ref[c] = jnp.broadcast_to(table[c:c + 1, :], (SUB, bins))
        high_ref[c] = jnp.broadcast_to(following[c:c + 1, :], (SUB, bins))


class Field:
    def __init__(self, ref, slices, strips, s):
        self.ref, self.strips = ref, strips
        self.per_slice = ref.shape[0] // slices
        self.s = s

    def load(self, z, rt, ds=0, k=0):
        start = pl.multiple_of((self.s + ds) * SUB, SUB) + (z * self.per_slice + rt * self.strips * SUB + k)
        return self.ref[pl.ds(start, SUB), :]

    def columns(self, z, rt, mid, lane):
        left = jnp.where(self.s > 0, self.load(z, rt, -jnp.minimum(self.s, 1)), 0.0)
        right = jnp.where(self.s < self.strips - 1, self.load(z, rt, jnp.minimum(self.strips - 1 - self.s, 1)), 0.0)
        return stencil(
            pltpu.roll(jnp.where(lane >= LANES - 2, left, mid), 2, 1),
            pltpu.roll(jnp.where(lane >= LANES - 1, left, mid), 1, 1),
            pltpu.roll(jnp.where(lane < 1, right, mid), LANES - 1, 1),
            pltpu.roll(jnp.where(lane < 2, right, mid), LANES - 2, 1),
        )

    def rows(self, z, rt, mid, sub, roll):
        def shifted(k):
            if k > 0:
                inside = sub < SUB - k
                if rt == 0:
                    return jnp.where(inside, self.load(z, 0, 0, k), self.load(z, 1, 0, k - SUB))
                return jnp.where(inside, pltpu.roll(mid, SUB - k, 0) if roll else self.load(z, 1, 0, k), 0.0)
            inside = sub >= -k
            if rt == 1:
                return jnp.where(inside, self.load(z, 1, 0, k), self.load(z, 0, 0, SUB + k))
            return jnp.where(inside, pltpu.roll(mid, -k, 0) if roll else self.load(z, 0, 0, k), 0.0)

        return stencil(*(shifted(k) for k in (-2, -1, 1, 2)))


def classify(grade, bins, low_ref, high_ref):
    position = grade * (bins - 1.0)
    index = jnp.minimum(position.astype(jnp.int32), bins - 1)
    w_low = 1.0 - (position - index.astype(jnp.float32))
    w_high = round_weight(1.0 - w_low)
    w_low = round_weight(w_low)

    def gather(ref, c):
        return jnp.take_along_axis(ref[c], index, axis=1)

    return [w_low * gather(low_ref, c) + w_high * gather(high_ref, c) for c in range(4)]


def step(state, terms):
    red, green, blue, trans = state
    g_x, a_x, g_yz, a_yz, steep, *cls = terms
    edge = 1.0 - 12.0 * lax.rsqrt(a_x * a_x + a_yz)
    shade = 0.3 + steep * lax.rsqrt(g_x * g_x + g_yz)
    weight = trans * (cls[3] * edge)
    trans = trans - weight
    weight = weight * shade
    return (red + weight * cls[0], green + weight * cls[1], blue + weight * cls[2], trans)


def cell_terms(fields, z, rt, along, roll, bins, low_ref, high_ref):
    lane = lax.broadcasted_iota(jnp.int32, (SUB, LANES), 1)
    sub = sublane((SUB, LANES))
    parts = []
    for field, near in zip(fields, along):
        mid = field.load(z, rt)
        dy = field.columns(z, rt, mid, lane)
        dz = stencil(*near)
        parts.append((mid, field.rows(z, rt, mid, sub, roll), dy * dy + dz * dz, dz))
    (grade, g_x, g_yz, g_z), (_, a_x, a_yz, _) = parts
    cls = classify(grade, bins, low_ref, high_ref)
    return (g_x, a_x, g_yz + 36.0, a_yz + 144.0, 0.7 * jnp.abs(g_z), *cls)


KEPT_AT = ((0, 4), (6, 2))


def keep(kept_ref, zi, s, rt, zb, terms):
    rows = slice(0, 2) if rt == 0 else slice(SUB - 2, SUB)
    at = KEPT_AT[rt][zb]
    for n, term in enumerate(terms):
        kept_ref[zi, s, n, at:at + 2, :] = term[rows, :]


def middle_kernel(scale, slices, strips, mask_ref, grade_ref, amp_ref, table_ref, mid_ref, kept_ref, low_ref, high_ref):
    bins = table_ref.shape[1]
    fill_tables(scale, table_ref, low_ref, high_ref)
    per_block = MY // LANES
    zero = jnp.zeros((SUB, LANES), jnp.float32)

    def block(cb, carry):
        for rt in range(2):
            for j in range(per_block):
                s = cb * per_block + j
                for c in range(3):
                    mid_ref[rt, s, c] = zero
                mid_ref[rt, s, 3] = zero + 1.0

            def march(halves):
                for j in range(per_block):
                    s = cb * per_block + j
                    fields = [Field(ref, slices, strips, s) for ref in (grade_ref, amp_ref)]
                    state = (zero, zero, zero, zero + 1.0)
                    for zb in halves:
                        for zi in range(2 - 2 * zb, MZ - 2 * zb):
                            z = zb * MZ + zi
                            along = [[field.load(z + k, rt) for k in (-2, -1, 1, 2)] for field in fields]
                            terms = cell_terms(fields, z, rt, along, False, bins, low_ref, high_ref)
                            keep(kept_ref, zi, s, rt, zb, terms)
                            state = step(state, terms)
                    for c in range(4):
                        mid_ref[rt, s, c] = state[c]

            front, back = mask_ref[0, rt, cb] != 0, mask_ref[1, rt, cb] != 0
            pl.when(front & back)(functools.partial(march, (0, 1)))
            pl.when(front & ~back)(functools.partial(march, (0,)))
            pl.when(~front & back)(functools.partial(march, (1,)))
        return carry

    lax.fori_loop(0, strips // per_block, block, 0)


def ends_kernel(scale, pieces, slices, strips, mask_ref, depth_ref, grade_ref, amp_ref, near_ref, far_ref, table_ref,
                mid_ref, *rest):
    outs, (kept_ref, acc_ref, low_ref, high_ref) = rest[:2], rest[2:]
    bins = table_ref.shape[1]
    fill_tables(scale, table_ref, low_ref, high_ref)
    per_block = MY // LANES
    piece_strips = strips // pieces
    piece_blocks = piece_strips // per_block
    zero = jnp.zeros((SUB, LANES), jnp.float32)
    odd = jnp.broadcast_to(lax.rem(depth_ref[0], 2), (SUB, LANES)) == 1

    def block(cb, carry):
        owner = lax.bitwise_xor(cb // piece_blocks, depth_ref[0])
        full = [[mask_ref[zb, rt, cb] for rt in range(2)] for zb in range(2)]

        def march():
            for rt in range(2):
                for j in range(per_block):
                    s = cb * per_block + j
                    fields = [Field(ref, slices, strips, s) for ref in (grade_ref, amp_ref)]
                    near, far = (Field(ref, 4, strips, s) for ref in (near_ref, far_ref))
                    state = (zero, zero, zero, zero + 1.0)
                    for zb in range(2):
                        cover = jnp.broadcast_to(full[zb][rt], (SUB, LANES)).astype(jnp.float32)
                        if zb == 1:
                            red, green, blue, trans = state
                            state = tuple(
                                value + trans * mid_ref[rt, s, c] for c, value in enumerate((red, green, blue))
                            ) + (trans * mid_ref[rt, s, 3],)
                        for zi in (0, 1) if zb == 0 else (MZ - 2, MZ - 1):
                            z = zb * MZ + zi
                            along = []
                            for f in range(2):

                                def at(z):
                                    if 0 <= z < slices:
                                        return fields[f].load(z, rt)
                                    k = 2 * f + z % slices % 2
                                    one, two = near.load(k, rt), far.load(k, rt)
                                    return jnp.where(odd, one, two) if z < 0 else jnp.where(odd, two, one)

                                along.append([at(z + k) for k in (-2, -1, 1, 2)])
                            terms = cell_terms(fields, z, rt, along, True, bins, low_ref, high_ref)
                            keep(kept_ref, zi if zb == 0 else zi - 4, s, rt, zb, terms)
                            state = step(state, (*terms[:-1], terms[-1] * cover))
                    for c in range(4):
                        acc_ref[rt, j, c] = state[c]

        some = (full[0][0] | full[0][1] | full[1][0] | full[1][1]) != 0
        pl.when(some)(march)

        @pl.when(jnp.logical_not(some))
        def _():
            for rt in range(2):
                for j in range(per_block):
                    for c in range(4):
                        acc_ref[rt, j, c] = zero if c < 3 else zero + 1.0

        for k, out in enumerate(outs):
            @pl.when(lax.rem(owner, 2) == k)
            def _():
                for rt in range(2):
                    for c in range(4):
                        for j in range(per_block):
                            part = lax.rem(cb, piece_blocks) * MY + j * LANES
                            lanes = pl.ds(pl.multiple_of(part, LANES), LANES)
                            out[owner // 2, c, rt * SUB:(rt + 1) * SUB, lanes] = acc_ref[rt, j, c]
        return carry

    lax.fori_loop(0, strips // per_block, block, 0)


def edge_kernel(pieces, first, mask_ref, depth_ref, lat_ref, kept_ref, ends_ref, pair_ref, cross_ref, *refs):
    out_ref = refs[-1]
    half = kept_ref.shape[0]
    strips = kept_ref.shape[1]
    sub = sublane((SUB, LANES))
    is_first = lax.rem((sub + 2) // 4, 2) == 0
    odd_lat = jnp.broadcast_to(lax.rem(lat_ref[0], 2), (SUB, LANES))
    from_pair = lax.rem(sub // 2, 2) != odd_lat
    piece_strips = strips // pieces
    packs = piece_strips // 2

    above = lax.rem(sub // 2, 2) == 0
    even_row = lax.rem(sub, 2) == 0

    def outside(raw, above):
        mate = jnp.where(even_row, pltpu.roll(raw, SUB - 1, 0), pltpu.roll(raw, 1, 0))
        mate = jnp.where(above == even_row, 8.0 * mate, 0.0)
        return jnp.where(above, raw - mate, mate - raw)

    def halo(f, zi, lanes):
        pair, cross = pair_ref[f, zi % 4, :, lanes], cross_ref[f, zi % 4, :, lanes]
        if zi < 4:
            return outside(jnp.where(from_pair, pair, cross), above)
        return outside(pltpu.roll(jnp.where(from_pair, cross, pair), 2, 0), above)

    def strip(s):
        lanes = pl.ds(pl.multiple_of(s * LANES, LANES), LANES)
        cb = s // (MY // LANES)
        full = [[jnp.broadcast_to(mask_ref[zb, rt, cb], (SUB, LANES)) for rt in range(2)] for zb in range(2)]
        live = jnp.where(
            sub < 4, jnp.where(sub < 2, full[0][0], full[1][1]), jnp.where(sub < 6, full[1][0], full[0][1])
        ) != 0
        zero = jnp.zeros((SUB, LANES), jnp.float32)
        total = [zero, zero, zero]
        trans = zero + 1.0
        for zi in range(half):
            terms = [kept_ref[zi, s, n] for n in range(TERMS)]
            if zi < 2:
                terms = [jnp.where(is_first, ends_ref[zi, s, n], term) for n, term in enumerate(terms)]
            if zi >= half - 2:
                terms = [jnp.where(is_first, term, ends_ref[zi - half + 4, s, n]) for n, term in enumerate(terms)]
            g_x, a_x, g_yz, a_yz, steep, red, green, blue, alpha = terms
            g_x = g_x + halo(0, zi, lanes)
            a_x = a_x + halo(1, zi, lanes)
            edge = 1.0 - 12.0 * lax.rsqrt(a_x * a_x + a_yz)
            shade = 0.3 + steep * lax.rsqrt(g_x * g_x + g_yz)
            weight = jnp.where(live, trans * (alpha * edge), 0.0)
            trans = trans - weight
            weight = weight * shade
            total = [t + jnp.where(live, weight * c, 0.0) for t, c in zip(total, (red, green, blue))]
        out = [t + trans * pltpu.roll(t, 4, 0) for t in total]
        return out + [trans * pltpu.roll(trans, 4, 0)]

    def piece(n, carry):
        p = lax.bitwise_xor(first + n, depth_ref[0])
        results = [strip(p * piece_strips + j) for j in range(piece_strips)]
        for j in range(packs):
            packed = [
                jnp.where(is_first, one, pltpu.roll(two, 4, 0)) for one, two in zip(results[j], results[j + packs])
            ]
            for c in range(4):
                out_ref[n, c, :, j * LANES:(j + 1) * LANES] = packed[c]
        return carry

    lax.fori_loop(0, pieces // 2, piece, 0)


def merge(mine, other, rank, level):
    ahead = jnp.broadcast_to(lax.rem(lax.shift_right_logical(rank, level), 2), mine[3].shape) == 0
    clear = jnp.where(ahead, mine[3], other[3])
    return [
        jnp.where(ahead, m, o) + clear * jnp.where(ahead, o, m) for m, o in zip(mine[:3], other[:3])
    ] + [mine[3] * other[3]]


def channels(ref):
    return [ref[c] for c in range(4)]


def merge_kernel(depth_ref, stay_ref, got_ref, own_ref, away_ref):
    for n, out_ref in enumerate((own_ref, away_ref)):
        for c, value in enumerate(merge(channels(stay_ref.at[n]), channels(got_ref.at[n]), depth_ref[0], 0)):
            out_ref[c] = value


def finish_kernel(depth_ref, own_ref, got_ref, home_ref, beside_ref, across_ref, corner_ref, out_ref):
    rows = out_ref.shape[1]
    rank = depth_ref[0]
    frame = merge(channels(own_ref), channels(got_ref), rank, 1)
    near = merge(channels(home_ref.at[0]), channels(beside_ref.at[1]), rank, 0)
    far = merge(channels(across_ref.at[0]), channels(corner_ref.at[1]), rank, 0)
    rim = merge(near, far, rank, 1)
    for c in range(4):
        inner, packed = frame[c], rim[c]
        if c == 3:
            inner, packed = 1.0 - inner, 1.0 - packed
        wide = jnp.concatenate([packed, pltpu.roll(packed, 4, 0)], axis=1)
        sub = sublane(wide.shape)
        out_ref[c, 0:SUB, :] = jnp.where(sub < 2, wide, inner[0:SUB, :])
        out_ref[c, rows - SUB:rows, :] = jnp.where(sub >= SUB - 2, wide, inner[rows - SUB:rows, :])


def swap_near(x, axis):
    return lax.ppermute(x, axis, [(i, i ^ 1) for i in range(lax.axis_size(axis))])


def swap_far(x, axis):
    size = lax.axis_size(axis)
    return lax.ppermute(x, axis, [(i, j) for k in range(1, size - 1, 2) for i, j in ((k, k + 1), (k + 1, k))])


def by_strips(array):
    rows, cols = array.shape[-2:]
    split = array.reshape(-1, rows // SUB, SUB, cols // LANES, LANES)
    return split.transpose(0, 1, 3, 2, 4).reshape(-1, LANES)


def local(grade_field, amplitude, tf_table, brick_mask):
    slices, rows, cols = grade_field.shape
    pieces = lax.axis_size("depth")
    assert (slices, rows, pieces) == (2 * MZ, 2 * MX, 4)
    depth_rank = lax.axis_index("depth").astype(jnp.int32).reshape(1)
    lat_rank = lax.axis_index("lat").astype(jnp.int32).reshape(1)
    f32 = jnp.float32
    vmem = pl.BlockSpec(memory_space=pltpu.VMEM)
    smem = pl.BlockSpec(memory_space=pltpu.SMEM)
    hbm = pl.BlockSpec(memory_space=pltpu.MemorySpace.HBM)
    lat_halo = jax.ShapeDtypeStruct((2, slices // 4, SUB, cols), f32)
    depth_halo = jax.ShapeDtypeStruct((2, 2, rows, cols), f32)
    hbm_only = pltpu.MemorySpace.HBM
    fields = (grade_field, amplitude)
    grade_field = pltpu.with_memory_space_constraint(grade_field, hbm_only)
    amplitude = pltpu.with_memory_space_constraint(amplitude, hbm_only)
    small = pltpu.CompilerParams(vmem_limit_bytes=4 << 20)
    after = pl.BlockSpec(memory_space=pl.ANY)
    pair, cross, near, far = pl.pallas_call(
        take_kernel,
        out_shape=(lat_halo, lat_halo, depth_halo, depth_halo),
        in_specs=[smem, smem, hbm, hbm],
        out_specs=[vmem] * 4,
        scratch_shapes=[pltpu.SemaphoreType.DMA((2, 4, 2)), pltpu.SemaphoreType.DMA((2, 2))],
        compiler_params=pltpu.CompilerParams(vmem_limit_bytes=8 << 20),
        name="take",
    )(lat_rank, depth_rank, grade_field, amplitude)
    far = pass_on(far, pair)
    cross = pass_on(cross, far)
    near = pass_on(near, cross)
    pair = swap_near(pair, "lat")
    cross = swap_far(cross, "lat")
    near = swap_near(near, "depth")
    far = swap_far(far, "depth")
    piece = jax.ShapeDtypeStruct((4, rows, cols // pieces), f32)
    half = jax.ShapeDtypeStruct((2, *piece.shape), f32)
    scale = 4.0 / (slices * pieces)
    strips = cols // LANES
    table = pltpu.VMEM((4, SUB, tf_table.shape[1]), f32)
    grade_strips, amp_strips = by_strips(fields[0]), by_strips(fields[1])
    mid, kept = pl.pallas_call(
        functools.partial(middle_kernel, scale, slices, strips),
        out_shape=(
            jax.ShapeDtypeStruct((2, strips, 4, SUB, LANES), f32),
            jax.ShapeDtypeStruct((MZ, strips, TERMS, SUB, LANES), f32),
        ),
        in_specs=[smem, vmem, vmem, vmem],
        out_specs=[vmem, vmem],
        scratch_shapes=[table, table],
        compiler_params=pltpu.CompilerParams(vmem_limit_bytes=8 << 20),
        cost_estimate=pl.CostEstimate(flops=10**10, bytes_accessed=10**8, transcendentals=0),
        name="middle",
    )(brick_mask, grade_strips, amp_strips, tf_table)
    stay, go, kept_ends = pl.pallas_call(
        functools.partial(ends_kernel, scale, pieces, slices, strips),
        out_shape=(half, half, jax.ShapeDtypeStruct((4, strips, TERMS, SUB, LANES), f32)),
        in_specs=[smem, smem] + [vmem] * 6,
        out_specs=[vmem] * 3,
        scratch_shapes=[pltpu.VMEM((2, MY // LANES, 4, SUB, LANES), f32), table, table],
        compiler_params=pltpu.CompilerParams(vmem_limit_bytes=8 << 20),
        name="ends",
    )(brick_mask, depth_rank, grade_strips, amp_strips, by_strips(near), by_strips(far), tf_table, mid)

    def swap_across(x):
        return lax.ppermute(x, "depth", [(i, i ^ 2) for i in range(pieces)])

    own, away_inner = pl.pallas_call(
        merge_kernel,
        out_shape=(piece, piece),
        in_specs=[smem, vmem, vmem],
        out_specs=[vmem, vmem],
        compiler_params=small,
        name="merge",
    )(depth_rank, stay, swap_near(go, "depth"))
    got = swap_across(away_inner)
    rims = jax.ShapeDtypeStruct((2, 4, SUB, cols // pieces // 2), f32)

    def edges_of(first, *earlier):
        return pl.pallas_call(
            functools.partial(edge_kernel, pieces, first),
            out_shape=rims,
            in_specs=[smem, smem, smem, vmem, vmem, vmem, vmem] + [after] * len(earlier),
            out_specs=vmem,
            compiler_params=small,
            name="edges",
        )(brick_mask, depth_rank, lat_rank, kept, kept_ends, pair, cross, *earlier)

    away = edges_of(2, away_inner)
    home = edges_of(0, away)
    across = swap_across(away)
    edges = (home, swap_near(home, "depth"), across, swap_near(across, "depth"))
    return pl.pallas_call(
        finish_kernel,
        out_shape=piece,
        in_specs=[smem] + [vmem] * 6,
        out_specs=vmem,
        compiler_params=small,
        name="finish",
    )(depth_rank, own, got, *edges)


def solution(mesh):
    placed = (P("depth", "lat", None), P("depth", "lat", None), P(), P("depth", "lat", None))
    return jax.shard_map(
        local, mesh=mesh, in_specs=placed, out_specs=P(None, "lat", "depth"), check_vma=False
    )
```

```python
import functools

import jax
import jax.numpy as jnp
from jax import lax
from jax.experimental import pallas as pl
from jax.experimental.pallas import tpu as pltpu
from jax.sharding import PartitionSpec as P

MZ = 8
MX = 8
MY = 256
LANES = 128
SUB = 8
TERMS = 9


def sublane(shape):
    return lax.broadcasted_iota(jnp.int32, shape, len(shape) - 2)


PLACES = ((6, 4, 2, 0), (0, 6, 4, 2))


def row_copies(fields, out_ref, sems, last):
    slices, rows = fields[0].shape[:2]
    span = slices // 4
    made = []
    for f, src in enumerate(fields):
        for q in range(4):
            here = src.at[pl.ds(span * q, span), pl.ds(rows - 2 if last else 0, 2), :]
            made.append(pltpu.make_async_copy(here, out_ref.at[f, :, pl.ds(PLACES[last][q], 2), :], sems.at[f, q]))
    return made


def start_and_wait(copies):
    for copy in copies:
        copy.start()
    for copy in copies:
        copy.wait()


def pair_kernel(lat_ref, grade_hbm, amp_hbm, pair_ref, sems):
    odd = lax.rem(lat_ref[0], 2)
    for last in (0, 1):
        @pl.when(odd == 1 - last)
        def _():
            start_and_wait(row_copies((grade_hbm, amp_hbm), pair_ref, sems, last))


def rest_kernel(lat_ref, depth_ref, grade_hbm, amp_hbm, after_ref, cross_ref, near_ref, far_ref, sems, depth_sems):
    del after_ref
    slices = grade_hbm.shape[0]
    fields = (grade_hbm, amp_hbm)
    odd = lax.rem(depth_ref[0], 2)
    parallel = []
    for f, src in enumerate(fields):
        for n, (dst, at) in enumerate(((near_ref, 1 - odd), (far_ref, odd))):
            here = src.at[pl.ds(at * (slices - 2), 2)]
            parallel.append(pltpu.make_async_copy(here, dst.at[f], depth_sems.at[f, n]))
    odd_lat = lax.rem(lat_ref[0], 2)
    for last in (0, 1):
        @pl.when(odd_lat == last)
        def _():
            start_and_wait(row_copies(fields, cross_ref, sems, last) + parallel)


def pass_on_kernel(*refs):
    del refs


def pass_on(x, *earlier):
    spec = pl.BlockSpec(memory_space=pl.ANY)
    return pl.pallas_call(
        pass_on_kernel,
        out_shape=jax.ShapeDtypeStruct(x.shape, x.dtype),
        in_specs=[spec] * (1 + len(earlier)),
        out_specs=spec,
        input_output_aliases={0: 0},
        compiler_params=pltpu.CompilerParams(vmem_limit_bytes=1 << 20),
        name="pass_on",
    )(x, *earlier)


def round_weight(w):
    return w.astype(jnp.bfloat16).astype(jnp.float32)


def stencil(m2, m1, p1, p2):
    return (m2 - p2) + 8.0 * (p1 - m1)


def fill_tables(scale, table_ref, low_ref, high_ref):
    bins = table_ref.shape[1]
    table = (table_ref[...].astype(jnp.float32) / 65535.0).astype(jnp.bfloat16).astype(jnp.float32)
    table = jnp.where(sublane(table.shape) == 3, table * scale, table)
    column = lax.broadcasted_iota(jnp.int32, table.shape, 1)
    following = jnp.where(column == bins - 1, 0.0, pltpu.roll(table, bins - 1, 1))
    for c in range(4):
        low_ref[c] = jnp.broadcast_to(table[c:c + 1, :], (SUB, bins))
        high_ref[c] = jnp.broadcast_to(following[c:c + 1, :], (SUB, bins))


class Field:
    def __init__(self, ref, slices, strips, s):
        self.ref, self.strips = ref, strips
        self.per_slice = ref.shape[0] // slices
        self.s = s

    def load(self, z, rt, ds=0, k=0):
        start = pl.multiple_of((self.s + ds) * SUB, SUB) + (z * self.per_slice + rt * self.strips * SUB + k)
        return self.ref[pl.ds(start, SUB), :]

    def columns(self, z, rt, mid, lane):
        left = jnp.where(self.s > 0, self.load(z, rt, -jnp.minimum(self.s, 1)), 0.0)
        right = jnp.where(self.s < self.strips - 1, self.load(z, rt, jnp.minimum(self.strips - 1 - self.s, 1)), 0.0)
        return stencil(
            pltpu.roll(jnp.where(lane >= LANES - 2, left, mid), 2, 1),
            pltpu.roll(jnp.where(lane >= LANES - 1, left, mid), 1, 1),
            pltpu.roll(jnp.where(lane < 1, right, mid), LANES - 1, 1),
            pltpu.roll(jnp.where(lane < 2, right, mid), LANES - 2, 1),
        )

    def rows(self, z, rt, mid, sub, roll):
        def shifted(k):
            if k > 0:
                inside = sub < SUB - k
                if rt == 0:
                    return jnp.where(inside, self.load(z, 0, 0, k), self.load(z, 1, 0, k - SUB))
                return jnp.where(inside, pltpu.roll(mid, SUB - k, 0) if roll else self.load(z, 1, 0, k), 0.0)
            inside = sub >= -k
            if rt == 1:
                return jnp.where(inside, self.load(z, 1, 0, k), self.load(z, 0, 0, SUB + k))
            return jnp.where(inside, pltpu.roll(mid, -k, 0) if roll else self.load(z, 0, 0, k), 0.0)

        return stencil(*(shifted(k) for k in (-2, -1, 1, 2)))


def classify(grade, bins, low_ref, high_ref):
    position = grade * (bins - 1.0)
    index = jnp.minimum(position.astype(jnp.int32), bins - 1)
    w_low = 1.0 - (position - index.astype(jnp.float32))
    w_high = round_weight(1.0 - w_low)
    w_low = round_weight(w_low)

    def gather(ref, c):
        return jnp.take_along_axis(ref[c], index, axis=1)

    return [w_low * gather(low_ref, c) + w_high * gather(high_ref, c) for c in range(4)]


def step(state, terms):
    red, green, blue, trans = state
    g_x, a_x, g_yz, a_yz, steep, *cls = terms
    edge = 1.0 - 12.0 * lax.rsqrt(a_x * a_x + a_yz)
    shade = 0.3 + steep * lax.rsqrt(g_x * g_x + g_yz)
    weight = trans * (cls[3] * edge)
    trans = trans - weight
    weight = weight * shade
    return (red + weight * cls[0], green + weight * cls[1], blue + weight * cls[2], trans)


def cell_terms(fields, z, rt, along, roll, bins, low_ref, high_ref):
    lane = lax.broadcasted_iota(jnp.int32, (SUB, LANES), 1)
    sub = sublane((SUB, LANES))
    parts = []
    for field, near in zip(fields, along):
        mid = field.load(z, rt)
        dy = field.columns(z, rt, mid, lane)
        dz = stencil(*near)
        parts.append((mid, field.rows(z, rt, mid, sub, roll), dy * dy + dz * dz, dz))
    (grade, g_x, g_yz, g_z), (_, a_x, a_yz, _) = parts
    cls = classify(grade, bins, low_ref, high_ref)
    return (g_x, a_x, g_yz + 36.0, a_yz + 144.0, 0.7 * jnp.abs(g_z), *cls)


KEPT_AT = ((0, 4), (6, 2))


def keep(kept_ref, zi, s, rt, zb, terms):
    rows = slice(0, 2) if rt == 0 else slice(SUB - 2, SUB)
    at = KEPT_AT[rt][zb]
    for n, term in enumerate(terms):
        kept_ref[zi, s, n, at:at + 2, :] = term[rows, :]


BLANK = (0.0, 0.0, 36.0, 144.0, 0.0, 0.0, 0.0, 0.0, 0.0)


def blank(kept_ref, zi, s, rt, zb):
    at = KEPT_AT[rt][zb]
    for n, value in enumerate(BLANK):
        kept_ref[zi, s, n, at:at + 2, :] = jnp.full((2, LANES), value, jnp.float32)


def middle_kernel(scale, slices, strips, mask_ref, grade_ref, amp_ref, table_ref, mid_ref, kept_ref, low_ref, high_ref):
    bins = table_ref.shape[1]
    fill_tables(scale, table_ref, low_ref, high_ref)
    per_block = MY // LANES
    zero = jnp.zeros((SUB, LANES), jnp.float32)

    def block(cb, carry):
        for rt in range(2):
            def march(halves):
                for j in range(per_block):
                    s = cb * per_block + j
                    fields = [Field(ref, slices, strips, s) for ref in (grade_ref, amp_ref)]
                    state = (zero, zero, zero, zero + 1.0)
                    for zb in halves:
                        for zi in range(2 - 2 * zb, MZ - 2 * zb):
                            z = zb * MZ + zi
                            along = [[field.load(z + k, rt) for k in (-2, -1, 1, 2)] for field in fields]
                            terms = cell_terms(fields, z, rt, along, False, bins, low_ref, high_ref)
                            keep(kept_ref, zi, s, rt, zb, terms)
                            state = step(state, terms)
                    for zb in {0, 1} - set(halves):
                        for zi in range(2 - 2 * zb, MZ - 2 * zb):
                            blank(kept_ref, zi, s, rt, zb)
                    for c in range(4):
                        mid_ref[rt, s, c] = state[c]

            front, back = mask_ref[0, rt, cb] != 0, mask_ref[1, rt, cb] != 0
            pl.when(front & back)(functools.partial(march, (0, 1)))
            pl.when(front & ~back)(functools.partial(march, (0,)))
            pl.when(~front & back)(functools.partial(march, (1,)))
            pl.when(~front & ~back)(functools.partial(march, ()))
        return carry

    lax.fori_loop(0, strips // per_block, block, 0)


def ends_kernel(scale, pieces, slices, strips, mask_ref, depth_ref, grade_ref, amp_ref, near_ref, far_ref, table_ref,
                mid_ref, middle_kept_ref, *rest):
    outs, (kept_ref, acc_ref, low_ref, high_ref) = rest[:2], rest[2:]
    bins = table_ref.shape[1]
    fill_tables(scale, table_ref, low_ref, high_ref)
    per_block = MY // LANES
    piece_strips = strips // pieces
    piece_blocks = piece_strips // per_block
    zero = jnp.zeros((SUB, LANES), jnp.float32)
    odd = jnp.broadcast_to(lax.rem(depth_ref[0], 2), (SUB, LANES)) == 1

    def block(cb, carry):
        owner = lax.bitwise_xor(cb // piece_blocks, depth_ref[0])
        full = [[mask_ref[zb, rt, cb] for rt in range(2)] for zb in range(2)]

        def march():
            for j in range(per_block):
                s = cb * per_block + j
                for n in range(TERMS):
                    for k, zi in enumerate((0, 1, MZ - 2, MZ - 1)):
                        kept_ref[k, s, n] = middle_kept_ref[zi, s, n]
            for rt in range(2):
                for j in range(per_block):
                    s = cb * per_block + j
                    fields = [Field(ref, slices, strips, s) for ref in (grade_ref, amp_ref)]
                    near, far = (Field(ref, 4, strips, s) for ref in (near_ref, far_ref))
                    state = (zero, zero, zero, zero + 1.0)
                    for zb in range(2):
                        cover = jnp.broadcast_to(full[zb][rt], (SUB, LANES)).astype(jnp.float32)
                        if zb == 1:
                            red, green, blue, trans = state
                            state = tuple(
                                value + trans * mid_ref[rt, s, c] for c, value in enumerate((red, green, blue))
                            ) + (trans * mid_ref[rt, s, 3],)
                        for zi in (0, 1) if zb == 0 else (MZ - 2, MZ - 1):
                            z = zb * MZ + zi
                            along = []
                            for f in range(2):

                                def at(z):
                                    if 0 <= z < slices:
                                        return fields[f].load(z, rt)
                                    k = 2 * f + z % slices % 2
                                    one, two = near.load(k, rt), far.load(k, rt)
                                    return jnp.where(odd, one, two) if z < 0 else jnp.where(odd, two, one)

                                along.append([at(z + k) for k in (-2, -1, 1, 2)])
                            terms = cell_terms(fields, z, rt, along, True, bins, low_ref, high_ref)
                            terms = (*terms[:-1], terms[-1] * cover)
                            keep(kept_ref, zi if zb == 0 else zi - 4, s, rt, zb, terms)
                            state = step(state, terms)
                    for c in range(4):
                        acc_ref[rt, j, c] = state[c]

        some = (full[0][0] | full[0][1] | full[1][0] | full[1][1]) != 0
        pl.when(some)(march)

        @pl.when(jnp.logical_not(some))
        def _():
            for j in range(per_block):
                for n, value in enumerate(BLANK):
                    for k in range(4):
                        kept_ref[k, cb * per_block + j, n] = jnp.full((SUB, LANES), value, jnp.float32)
            for rt in range(2):
                for j in range(per_block):
                    for c in range(4):
                        acc_ref[rt, j, c] = zero if c < 3 else zero + 1.0

        for k, out in enumerate(outs):
            @pl.when(lax.rem(owner, 2) == k)
            def _():
                for rt in range(2):
                    for c in range(4):
                        for j in range(per_block):
                            part = lax.rem(cb, piece_blocks) * MY + j * LANES
                            lanes = pl.ds(pl.multiple_of(part, LANES), LANES)
                            out[owner // 2, c, rt * SUB:(rt + 1) * SUB, lanes] = acc_ref[rt, j, c]
        return carry

    lax.fori_loop(0, strips // per_block, block, 0)


def edge_kernel(pieces, first, depth_ref, lat_ref, kept_ref, ends_ref, pair_ref, cross_ref, *refs):
    out_ref = refs[-1]
    half = kept_ref.shape[0]
    strips = kept_ref.shape[1]
    sub = sublane((SUB, LANES))
    is_first = lax.rem((sub + 2) // 4, 2) == 0
    odd_lat = jnp.broadcast_to(lax.rem(lat_ref[0], 2), (SUB, LANES))
    from_pair = lax.rem(sub // 2, 2) != odd_lat
    piece_strips = strips // pieces
    packs = piece_strips // 2

    above = lax.rem(sub // 2, 2) == 0
    even_row = lax.rem(sub, 2) == 0

    own_factor = jnp.where(above, 1.0, -1.0)
    mate_factor = jnp.where(above == even_row, -8.0 * own_factor, 0.0)

    def outside(raw):
        mate = jnp.where(even_row, pltpu.roll(raw, SUB - 1, 0), pltpu.roll(raw, 1, 0))
        return own_factor * raw + mate_factor * mate

    def halo(f, zi, lanes):
        pair, cross = pair_ref[f, zi % 4, :, lanes], cross_ref[f, zi % 4, :, lanes]
        if zi < 4:
            return outside(jnp.where(from_pair, pair, cross))
        return outside(pltpu.roll(jnp.where(from_pair, cross, pair), 2, 0))

    def strip(s):
        lanes = pl.ds(pl.multiple_of(s * LANES, LANES), LANES)
        zero = jnp.zeros((SUB, LANES), jnp.float32)
        state = (zero, zero, zero, zero + 1.0)
        for zi in range(half):
            held, at = (kept_ref, zi) if 2 <= zi < half - 2 else (ends_ref, zi % (half - 4))
            g_x, a_x, *others = (held[at, s, n] for n in range(TERMS))
            state = step(state, (g_x + halo(0, zi, lanes), a_x + halo(1, zi, lanes), *others))
        *total, trans = state
        out = [t + trans * pltpu.roll(t, 4, 0) for t in total]
        return out + [trans * pltpu.roll(trans, 4, 0)]

    def piece(n, carry):
        p = lax.bitwise_xor(first + n, depth_ref[0])
        results = [strip(p * piece_strips + j) for j in range(piece_strips)]
        for j in range(packs):
            packed = [
                jnp.where(is_first, one, pltpu.roll(two, 4, 0)) for one, two in zip(results[j], results[j + packs])
            ]
            for c in range(4):
                out_ref[n, c, :, j * LANES:(j + 1) * LANES] = packed[c]
        return carry

    lax.fori_loop(0, pieces // 2, piece, 0)


def merge(mine, other, rank, level):
    ahead = jnp.broadcast_to(lax.rem(lax.shift_right_logical(rank, level), 2), mine[3].shape) == 0
    clear = jnp.where(ahead, mine[3], other[3])
    return [
        jnp.where(ahead, m, o) + clear * jnp.where(ahead, o, m) for m, o in zip(mine[:3], other[:3])
    ] + [mine[3] * other[3]]


def channels(ref):
    return [ref[c] for c in range(4)]


def merge_kernel(depth_ref, stay_ref, got_ref, own_ref, away_ref):
    for n, out_ref in enumerate((own_ref, away_ref)):
        for c, value in enumerate(merge(channels(stay_ref.at[n]), channels(got_ref.at[n]), depth_ref[0], 0)):
            out_ref[c] = value


def finish_kernel(depth_ref, own_ref, got_ref, home_ref, beside_ref, across_ref, corner_ref, out_ref):
    rows = out_ref.shape[1]
    rank = depth_ref[0]
    frame = merge(channels(own_ref), channels(got_ref), rank, 1)
    near = merge(channels(home_ref.at[0]), channels(beside_ref.at[1]), rank, 0)
    far = merge(channels(across_ref.at[0]), channels(corner_ref.at[1]), rank, 0)
    rim = merge(near, far, rank, 1)
    for c in range(4):
        inner, packed = frame[c], rim[c]
        if c == 3:
            inner, packed = 1.0 - inner, 1.0 - packed
        wide = jnp.concatenate([packed, pltpu.roll(packed, 4, 0)], axis=1)
        sub = sublane(wide.shape)
        out_ref[c, 0:SUB, :] = jnp.where(sub < 2, wide, inner[0:SUB, :])
        out_ref[c, rows - SUB:rows, :] = jnp.where(sub >= SUB - 2, wide, inner[rows - SUB:rows, :])


def swap_near(x, axis):
    return lax.ppermute(x, axis, [(i, i ^ 1) for i in range(lax.axis_size(axis))])


def swap_far(x, axis):
    size = lax.axis_size(axis)
    return lax.ppermute(x, axis, [(i, j) for k in range(1, size - 1, 2) for i, j in ((k, k + 1), (k + 1, k))])


def by_strips(array):
    rows, cols = array.shape[-2:]
    split = array.reshape(-1, rows // SUB, SUB, cols // LANES, LANES)
    return split.transpose(0, 1, 3, 2, 4).reshape(-1, LANES)


def local(grade_field, amplitude, tf_table, brick_mask):
    slices, rows, cols = grade_field.shape
    pieces = lax.axis_size("depth")
    assert (slices, rows, pieces) == (2 * MZ, 2 * MX, 4)
    depth_rank = lax.axis_index("depth").astype(jnp.int32).reshape(1)
    lat_rank = lax.axis_index("lat").astype(jnp.int32).reshape(1)
    f32 = jnp.float32
    vmem = pl.BlockSpec(memory_space=pltpu.VMEM)
    smem = pl.BlockSpec(memory_space=pltpu.SMEM)
    hbm = pl.BlockSpec(memory_space=pltpu.MemorySpace.HBM)
    lat_halo = jax.ShapeDtypeStruct((2, slices // 4, SUB, cols), f32)
    depth_halo = jax.ShapeDtypeStruct((2, 2, rows, cols), f32)
    hbm_only = pltpu.MemorySpace.HBM
    fields = (grade_field, amplitude)
    grade_field = pltpu.with_memory_space_constraint(grade_field, hbm_only)
    amplitude = pltpu.with_memory_space_constraint(amplitude, hbm_only)
    small = pltpu.CompilerParams(vmem_limit_bytes=4 << 20)
    after = pl.BlockSpec(memory_space=pl.ANY)
    pair = pl.pallas_call(
        pair_kernel,
        out_shape=lat_halo,
        in_specs=[smem, hbm, hbm],
        out_specs=vmem,
        scratch_shapes=[pltpu.SemaphoreType.DMA((2, 4))],
        compiler_params=small,
        name="take_pair",
    )(lat_rank, grade_field, amplitude)
    cross, near, far = pl.pallas_call(
        rest_kernel,
        out_shape=(lat_halo, depth_halo, depth_halo),
        in_specs=[smem, smem, hbm, hbm, after],
        out_specs=[vmem] * 3,
        scratch_shapes=[pltpu.SemaphoreType.DMA((2, 4)), pltpu.SemaphoreType.DMA((2, 2))],
        compiler_params=small,
        name="take_rest",
    )(lat_rank, depth_rank, grade_field, amplitude, pair)
    far = pass_on(far, cross)
    near = pass_on(near, far)
    pair = swap_near(pair, "lat")
    cross = swap_far(cross, "lat")
    near = swap_near(near, "depth")
    far = swap_far(far, "depth")
    piece = jax.ShapeDtypeStruct((4, rows, cols // pieces), f32)
    half = jax.ShapeDtypeStruct((2, *piece.shape), f32)
    scale = 4.0 / (slices * pieces)
    strips = cols // LANES
    table = pltpu.VMEM((4, SUB, tf_table.shape[1]), f32)
    grade_strips, amp_strips = by_strips(fields[0]), by_strips(fields[1])
    mid, kept = pl.pallas_call(
        functools.partial(middle_kernel, scale, slices, strips),
        out_shape=(
            jax.ShapeDtypeStruct((2, strips, 4, SUB, LANES), f32),
            jax.ShapeDtypeStruct((MZ, strips, TERMS, SUB, LANES), f32),
        ),
        in_specs=[smem, vmem, vmem, vmem],
        out_specs=[vmem, vmem],
        scratch_shapes=[table, table],
        compiler_params=pltpu.CompilerParams(vmem_limit_bytes=8 << 20),
        cost_estimate=pl.CostEstimate(flops=10**10, bytes_accessed=10**8, transcendentals=0),
        name="middle",
    )(brick_mask, grade_strips, amp_strips, tf_table)
    stay, go, kept_ends = pl.pallas_call(
        functools.partial(ends_kernel, scale, pieces, slices, strips),
        out_shape=(half, half, jax.ShapeDtypeStruct((4, strips, TERMS, SUB, LANES), f32)),
        in_specs=[smem, smem] + [vmem] * 7,
        out_specs=[vmem] * 3,
        scratch_shapes=[pltpu.VMEM((2, MY // LANES, 4, SUB, LANES), f32), table, table],
        compiler_params=pltpu.CompilerParams(vmem_limit_bytes=8 << 20),
        name="ends",
    )(brick_mask, depth_rank, grade_strips, amp_strips, by_strips(near), by_strips(far), tf_table, mid, kept)

    def swap_across(x):
        return lax.ppermute(x, "depth", [(i, i ^ 2) for i in range(pieces)])

    own, away_inner = pl.pallas_call(
        merge_kernel,
        out_shape=(piece, piece),
        in_specs=[smem, vmem, vmem],
        out_specs=[vmem, vmem],
        compiler_params=small,
        name="merge",
    )(depth_rank, stay, swap_near(go, "depth"))
    got = swap_across(away_inner)
    rims = jax.ShapeDtypeStruct((2, 4, SUB, cols // pieces // 2), f32)

    def edges_of(first, *earlier):
        return pl.pallas_call(
            functools.partial(edge_kernel, pieces, first),
            out_shape=rims,
            in_specs=[smem, smem, vmem, vmem, vmem, vmem] + [after] * len(earlier),
            out_specs=vmem,
            compiler_params=small,
            name="edges",
        )(depth_rank, lat_rank, kept, kept_ends, pair, cross, *earlier)

    away = edges_of(2, away_inner)
    home = edges_of(0, away)
    across = swap_across(away)
    edges = (home, swap_near(home, "depth"), across, swap_near(across, "depth"))
    return pl.pallas_call(
        finish_kernel,
        out_shape=piece,
        in_specs=[smem] + [vmem] * 6,
        out_specs=vmem,
        compiler_params=small,
        name="finish",
    )(depth_rank, own, got, *edges)


def solution(mesh):
    placed = (P("depth", "lat", None), P("depth", "lat", None), P(), P("depth", "lat", None))
    return jax.shard_map(
        local, mesh=mesh, in_specs=placed, out_specs=P(None, "lat", "depth"), check_vma=False
    )
```

```python
import functools

import jax
import jax.numpy as jnp
from jax import lax
from jax.experimental import pallas as pl
from jax.experimental.pallas import tpu as pltpu
from jax.sharding import PartitionSpec as P

MZ = 8
MX = 8
MY = 256
LANES = 128
SUB = 8
TERMS = 9


def sublane(shape):
    return lax.broadcasted_iota(jnp.int32, shape, len(shape) - 2)


PLACES = ((6, 4, 2, 0), (0, 6, 4, 2))


def row_copies(fields, out_ref, sems, last):
    slices, rows = fields[0].shape[:2]
    span = slices // 4
    made = []
    for f, src in enumerate(fields):
        for q in range(4):
            here = src.at[pl.ds(span * q, span), pl.ds(rows - 2 if last else 0, 2), :]
            made.append(pltpu.make_async_copy(here, out_ref.at[f, :, pl.ds(PLACES[last][q], 2), :], sems.at[f, q]))
    return made


def start_and_wait(copies):
    for copy in copies:
        copy.start()
    for copy in copies:
        copy.wait()


def pair_kernel(lat_ref, grade_hbm, amp_hbm, pair_ref, sems):
    odd = lax.rem(lat_ref[0], 2)
    for last in (0, 1):
        @pl.when(odd == 1 - last)
        def _():
            start_and_wait(row_copies((grade_hbm, amp_hbm), pair_ref, sems, last))


def rest_kernel(lat_ref, depth_ref, grade_hbm, amp_hbm, after_ref, cross_ref, near_ref, far_ref, sems, depth_sems):
    del after_ref
    slices = grade_hbm.shape[0]
    fields = (grade_hbm, amp_hbm)
    odd = lax.rem(depth_ref[0], 2)
    parallel = []
    for f, src in enumerate(fields):
        for n, (dst, at) in enumerate(((near_ref, 1 - odd), (far_ref, odd))):
            here = src.at[pl.ds(at * (slices - 2), 2)]
            parallel.append(pltpu.make_async_copy(here, dst.at[f], depth_sems.at[f, n]))
    odd_lat = lax.rem(lat_ref[0], 2)
    for last in (0, 1):
        @pl.when(odd_lat == last)
        def _():
            start_and_wait(row_copies(fields, cross_ref, sems, last) + parallel)


def pass_on_kernel(*refs):
    del refs


def pass_on(x, *earlier):
    spec = pl.BlockSpec(memory_space=pl.ANY)
    return pl.pallas_call(
        pass_on_kernel,
        out_shape=jax.ShapeDtypeStruct(x.shape, x.dtype),
        in_specs=[spec] * (1 + len(earlier)),
        out_specs=spec,
        input_output_aliases={0: 0},
        compiler_params=pltpu.CompilerParams(vmem_limit_bytes=1 << 20),
        name="pass_on",
    )(x, *earlier)


def round_weight(w):
    return w.astype(jnp.bfloat16).astype(jnp.float32)


def stencil(m2, m1, p1, p2):
    return (m2 - p2) + 8.0 * (p1 - m1)


def fill_tables(scale, table_ref, low_ref, high_ref):
    bins = table_ref.shape[1]
    table = (table_ref[...].astype(jnp.float32) / 65535.0).astype(jnp.bfloat16).astype(jnp.float32)
    table = jnp.where(sublane(table.shape) == 3, table * scale, table)
    column = lax.broadcasted_iota(jnp.int32, table.shape, 1)
    following = jnp.where(column == bins - 1, 0.0, pltpu.roll(table, bins - 1, 1))
    for c in range(4):
        low_ref[c] = jnp.broadcast_to(table[c:c + 1, :], (SUB, bins))
        high_ref[c] = jnp.broadcast_to(following[c:c + 1, :], (SUB, bins))


class Field:
    def __init__(self, ref, slices, strips, s):
        self.ref, self.strips = ref, strips
        self.per_slice = ref.shape[0] // slices
        self.s = s

    def load(self, z, rt, ds=0, k=0):
        start = pl.multiple_of((self.s + ds) * SUB, SUB) + (z * self.per_slice + rt * self.strips * SUB + k)
        return self.ref[pl.ds(start, SUB), :]

    def columns(self, z, rt, mid, lane):
        left = jnp.where(self.s > 0, self.load(z, rt, -jnp.minimum(self.s, 1)), 0.0)
        right = jnp.where(self.s < self.strips - 1, self.load(z, rt, jnp.minimum(self.strips - 1 - self.s, 1)), 0.0)
        return stencil(
            pltpu.roll(jnp.where(lane >= LANES - 2, left, mid), 2, 1),
            pltpu.roll(jnp.where(lane >= LANES - 1, left, mid), 1, 1),
            pltpu.roll(jnp.where(lane < 1, right, mid), LANES - 1, 1),
            pltpu.roll(jnp.where(lane < 2, right, mid), LANES - 2, 1),
        )

    def rows(self, z, rt, mid, sub, roll):
        def shifted(k):
            if k > 0:
                inside = sub < SUB - k
                if rt == 0:
                    return jnp.where(inside, self.load(z, 0, 0, k), self.load(z, 1, 0, k - SUB))
                return jnp.where(inside, pltpu.roll(mid, SUB - k, 0) if roll else self.load(z, 1, 0, k), 0.0)
            inside = sub >= -k
            if rt == 1:
                return jnp.where(inside, self.load(z, 1, 0, k), self.load(z, 0, 0, SUB + k))
            return jnp.where(inside, pltpu.roll(mid, -k, 0) if roll else self.load(z, 0, 0, k), 0.0)

        return stencil(*(shifted(k) for k in (-2, -1, 1, 2)))


def classify(grade, bins, low_ref, high_ref):
    position = grade * (bins - 1.0)
    index = jnp.minimum(position.astype(jnp.int32), bins - 1)
    w_low = 1.0 - (position - index.astype(jnp.float32))
    w_high = round_weight(1.0 - w_low)
    w_low = round_weight(w_low)

    def gather(ref, c):
        return jnp.take_along_axis(ref[c], index, axis=1)

    return [w_low * gather(low_ref, c) + w_high * gather(high_ref, c) for c in range(4)]


def step(state, terms):
    red, green, blue, trans = state
    g_x, a_x, g_yz, a_yz, steep, *cls = terms
    edge = 1.0 - 12.0 * lax.rsqrt(a_x * a_x + a_yz)
    shade = 0.3 + steep * lax.rsqrt(g_x * g_x + g_yz)
    weight = trans * (cls[3] * edge)
    trans = trans - weight
    weight = weight * shade
    return (red + weight * cls[0], green + weight * cls[1], blue + weight * cls[2], trans)


def cell_terms(fields, z, rt, along, roll, bins, low_ref, high_ref):
    lane = lax.broadcasted_iota(jnp.int32, (SUB, LANES), 1)
    sub = sublane((SUB, LANES))
    parts = []
    for field, near in zip(fields, along):
        mid = field.load(z, rt)
        dy = field.columns(z, rt, mid, lane)
        dz = stencil(*near)
        parts.append((mid, field.rows(z, rt, mid, sub, roll), dy * dy + dz * dz, dz))
    (grade, g_x, g_yz, g_z), (_, a_x, a_yz, _) = parts
    cls = classify(grade, bins, low_ref, high_ref)
    return (g_x, a_x, g_yz + 36.0, a_yz + 144.0, 0.7 * jnp.abs(g_z), *cls)


KEPT_AT = ((0, 4), (6, 2))


def keep(kept_ref, zi, s, rt, zb, terms):
    rows = slice(0, 2) if rt == 0 else slice(SUB - 2, SUB)
    at = KEPT_AT[rt][zb]
    for n, term in enumerate(terms):
        kept_ref[zi, s, n, at:at + 2, :] = term[rows, :]


BLANK = (0.0, 0.0, 36.0, 144.0, 0.0, 0.0, 0.0, 0.0, 0.0)


def blank(kept_ref, zi, s, rt, zb):
    at = KEPT_AT[rt][zb]
    for n, value in enumerate(BLANK):
        kept_ref[zi, s, n, at:at + 2, :] = jnp.full((2, LANES), value, jnp.float32)


def middle_kernel(scale, slices, strips, mask_ref, grade_ref, amp_ref, table_ref, mid_ref, kept_ref, low_ref, high_ref):
    bins = table_ref.shape[1]
    fill_tables(scale, table_ref, low_ref, high_ref)
    per_block = MY // LANES
    zero = jnp.zeros((SUB, LANES), jnp.float32)

    def block(cb, carry):
        for rt in range(2):
            def march(halves):
                for j in range(per_block):
                    s = cb * per_block + j
                    fields = [Field(ref, slices, strips, s) for ref in (grade_ref, amp_ref)]
                    state = (zero, zero, zero, zero + 1.0)
                    for zb in halves:
                        for zi in range(2 - 2 * zb, MZ - 2 * zb):
                            z = zb * MZ + zi
                            along = [[field.load(z + k, rt) for k in (-2, -1, 1, 2)] for field in fields]
                            terms = cell_terms(fields, z, rt, along, False, bins, low_ref, high_ref)
                            keep(kept_ref, zi, s, rt, zb, terms)
                            state = step(state, terms)
                    for zb in {0, 1} - set(halves):
                        for zi in range(2 - 2 * zb, MZ - 2 * zb):
                            blank(kept_ref, zi, s, rt, zb)
                    for c in range(4):
                        mid_ref[rt, s, c] = state[c]

            front, back = mask_ref[0, rt, cb] != 0, mask_ref[1, rt, cb] != 0
            pl.when(front & back)(functools.partial(march, (0, 1)))
            pl.when(front & ~back)(functools.partial(march, (0,)))
            pl.when(~front & back)(functools.partial(march, (1,)))
            pl.when(~front & ~back)(functools.partial(march, ()))
        return carry

    lax.fori_loop(0, strips // per_block, block, 0)


def ends_kernel(scale, pieces, slices, strips, mask_ref, depth_ref, grade_ref, amp_ref, near_ref, far_ref, table_ref,
                mid_ref, middle_kept_ref, *rest):
    outs, (kept_ref, acc_ref, low_ref, high_ref) = rest[:2], rest[2:]
    bins = table_ref.shape[1]
    fill_tables(scale, table_ref, low_ref, high_ref)
    per_block = MY // LANES
    piece_strips = strips // pieces
    piece_blocks = piece_strips // per_block
    zero = jnp.zeros((SUB, LANES), jnp.float32)
    odd = jnp.broadcast_to(lax.rem(depth_ref[0], 2), (SUB, LANES)) == 1

    def block(cb, carry):
        owner = lax.bitwise_xor(cb // piece_blocks, depth_ref[0])
        full = [[mask_ref[zb, rt, cb] for rt in range(2)] for zb in range(2)]

        def march():
            for j in range(per_block):
                s = cb * per_block + j
                for n in range(TERMS):
                    for k, zi in enumerate((0, 1, MZ - 2, MZ - 1)):
                        kept_ref[k, s, n] = middle_kept_ref[zi, s, n]
            for rt in range(2):
                for j in range(per_block):
                    s = cb * per_block + j
                    fields = [Field(ref, slices, strips, s) for ref in (grade_ref, amp_ref)]
                    near, far = (Field(ref, 4, strips, s) for ref in (near_ref, far_ref))
                    state = (zero, zero, zero, zero + 1.0)
                    for zb in range(2):
                        cover = jnp.broadcast_to(full[zb][rt], (SUB, LANES)).astype(jnp.float32)
                        if zb == 1:
                            red, green, blue, trans = state
                            state = tuple(
                                value + trans * mid_ref[rt, s, c] for c, value in enumerate((red, green, blue))
                            ) + (trans * mid_ref[rt, s, 3],)
                        for zi in (0, 1) if zb == 0 else (MZ - 2, MZ - 1):
                            z = zb * MZ + zi
                            along = []
                            for f in range(2):

                                def at(z):
                                    if 0 <= z < slices:
                                        return fields[f].load(z, rt)
                                    k = 2 * f + z % slices % 2
                                    one, two = near.load(k, rt), far.load(k, rt)
                                    return jnp.where(odd, one, two) if z < 0 else jnp.where(odd, two, one)

                                along.append([at(z + k) for k in (-2, -1, 1, 2)])
                            terms = cell_terms(fields, z, rt, along, True, bins, low_ref, high_ref)
                            terms = (*terms[:-1], terms[-1] * cover)
                            keep(kept_ref, zi if zb == 0 else zi - 4, s, rt, zb, terms)
                            state = step(state, terms)
                    for c in range(4):
                        acc_ref[rt, j, c] = state[c]

        some = (full[0][0] | full[0][1] | full[1][0] | full[1][1]) != 0
        pl.when(some)(march)

        @pl.when(jnp.logical_not(some))
        def _():
            for j in range(per_block):
                for n, value in enumerate(BLANK):
                    for k in range(4):
                        kept_ref[k, cb * per_block + j, n] = jnp.full((SUB, LANES), value, jnp.float32)
            for rt in range(2):
                for j in range(per_block):
                    for c in range(4):
                        acc_ref[rt, j, c] = zero if c < 3 else zero + 1.0

        for k, out in enumerate(outs):
            @pl.when(lax.rem(owner, 2) == k)
            def _():
                for rt in range(2):
                    for c in range(4):
                        for j in range(per_block):
                            part = lax.rem(cb, piece_blocks) * MY + j * LANES
                            lanes = pl.ds(pl.multiple_of(part, LANES), LANES)
                            out[owner // 2, c, rt * SUB:(rt + 1) * SUB, lanes] = acc_ref[rt, j, c]
        return carry

    lax.fori_loop(0, strips // per_block, block, 0)


def edge_kernel(pieces, depth_ref, lat_ref, kept_ref, ends_ref, pair_ref, cross_ref, after_ref, *outs):
    del after_ref
    half = kept_ref.shape[0]
    strips = kept_ref.shape[1]
    sub = sublane((SUB, LANES))
    is_first = lax.rem((sub + 2) // 4, 2) == 0
    odd_lat = jnp.broadcast_to(lax.rem(lat_ref[0], 2), (SUB, LANES))
    from_pair = lax.rem(sub // 2, 2) != odd_lat
    piece_strips = strips // pieces
    packs = piece_strips // 2

    above = lax.rem(sub // 2, 2) == 0
    even_row = lax.rem(sub, 2) == 0

    own_factor = jnp.where(above, 1.0, -1.0)
    mate_factor = jnp.where(above == even_row, -8.0 * own_factor, 0.0)

    def outside(raw):
        mate = jnp.where(even_row, pltpu.roll(raw, SUB - 1, 0), pltpu.roll(raw, 1, 0))
        return own_factor * raw + mate_factor * mate

    def halo(f, zi, lanes):
        pair, cross = pair_ref[f, zi % 4, :, lanes], cross_ref[f, zi % 4, :, lanes]
        if zi < 4:
            return outside(jnp.where(from_pair, pair, cross))
        return outside(pltpu.roll(jnp.where(from_pair, cross, pair), 2, 0))

    def strip(s):
        lanes = pl.ds(pl.multiple_of(s * LANES, LANES), LANES)
        zero = jnp.zeros((SUB, LANES), jnp.float32)
        state = (zero, zero, zero, zero + 1.0)
        for zi in range(half):
            held, at = (kept_ref, zi) if 2 <= zi < half - 2 else (ends_ref, zi % (half - 4))
            g_x, a_x, *others = (held[at, s, n] for n in range(TERMS))
            state = step(state, (g_x + halo(0, zi, lanes), a_x + halo(1, zi, lanes), *others))
        *total, trans = state
        out = [t + trans * pltpu.roll(t, 4, 0) for t in total]
        return out + [trans * pltpu.roll(trans, 4, 0)]

    def piece(n, carry):
        p = lax.bitwise_xor(n, depth_ref[0])
        results = [strip(p * piece_strips + j) for j in range(piece_strips)]
        for j in range(packs):
            packed = [
                jnp.where(is_first, one, pltpu.roll(two, 4, 0)) for one, two in zip(results[j], results[j + packs])
            ]
            for k, out in enumerate(outs):
                @pl.when(n == k)
                def _():
                    for c in range(4):
                        out[c, :, j * LANES:(j + 1) * LANES] = packed[c]
        return carry

    lax.fori_loop(0, pieces, piece, 0)


def merge(mine, other, rank, level):
    ahead = jnp.broadcast_to(lax.rem(lax.shift_right_logical(rank, level), 2), mine[3].shape) == 0
    clear = jnp.where(ahead, mine[3], other[3])
    return [
        jnp.where(ahead, m, o) + clear * jnp.where(ahead, o, m) for m, o in zip(mine[:3], other[:3])
    ] + [mine[3] * other[3]]


def channels(ref):
    return [ref[c] for c in range(4)]


def merge_kernel(depth_ref, stay_ref, got_ref, own_ref, away_ref):
    for n, out_ref in enumerate((own_ref, away_ref)):
        for c, value in enumerate(merge(channels(stay_ref.at[n]), channels(got_ref.at[n]), depth_ref[0], 0)):
            out_ref[c] = value


def finish_kernel(depth_ref, own_ref, got_ref, home_ref, across_ref, corner_ref, beside_ref, out_ref):
    rows = out_ref.shape[1]
    rank = depth_ref[0]
    frame = merge(channels(own_ref), channels(got_ref), rank, 1)
    near = merge(channels(home_ref), channels(beside_ref), rank, 0)
    far = merge(channels(across_ref), channels(corner_ref), rank, 0)
    rim = merge(near, far, rank, 1)
    for c in range(4):
        inner, packed = frame[c], rim[c]
        if c == 3:
            inner, packed = 1.0 - inner, 1.0 - packed
        wide = jnp.concatenate([packed, pltpu.roll(packed, 4, 0)], axis=1)
        sub = sublane(wide.shape)
        out_ref[c, 0:SUB, :] = jnp.where(sub < 2, wide, inner[0:SUB, :])
        out_ref[c, rows - SUB:rows, :] = jnp.where(sub >= SUB - 2, wide, inner[rows - SUB:rows, :])


def swap_near(x, axis):
    return lax.ppermute(x, axis, [(i, i ^ 1) for i in range(lax.axis_size(axis))])


def swap_far(x, axis):
    size = lax.axis_size(axis)
    return lax.ppermute(x, axis, [(i, j) for k in range(1, size - 1, 2) for i, j in ((k, k + 1), (k + 1, k))])


def by_strips(array):
    rows, cols = array.shape[-2:]
    split = array.reshape(-1, rows // SUB, SUB, cols // LANES, LANES)
    return split.transpose(0, 1, 3, 2, 4).reshape(-1, LANES)


def local(grade_field, amplitude, tf_table, brick_mask):
    slices, rows, cols = grade_field.shape
    pieces = lax.axis_size("depth")
    assert (slices, rows, pieces) == (2 * MZ, 2 * MX, 4)
    depth_rank = lax.axis_index("depth").astype(jnp.int32).reshape(1)
    lat_rank = lax.axis_index("lat").astype(jnp.int32).reshape(1)
    f32 = jnp.float32
    vmem = pl.BlockSpec(memory_space=pltpu.VMEM)
    smem = pl.BlockSpec(memory_space=pltpu.SMEM)
    hbm = pl.BlockSpec(memory_space=pltpu.MemorySpace.HBM)
    lat_halo = jax.ShapeDtypeStruct((2, slices // 4, SUB, cols), f32)
    depth_halo = jax.ShapeDtypeStruct((2, 2, rows, cols), f32)
    hbm_only = pltpu.MemorySpace.HBM
    fields = (grade_field, amplitude)
    grade_field = pltpu.with_memory_space_constraint(grade_field, hbm_only)
    amplitude = pltpu.with_memory_space_constraint(amplitude, hbm_only)
    small = pltpu.CompilerParams(vmem_limit_bytes=4 << 20)
    after = pl.BlockSpec(memory_space=pl.ANY)
    pair = pl.pallas_call(
        pair_kernel,
        out_shape=lat_halo,
        in_specs=[smem, hbm, hbm],
        out_specs=vmem,
        scratch_shapes=[pltpu.SemaphoreType.DMA((2, 4))],
        compiler_params=small,
        name="take_pair",
    )(lat_rank, grade_field, amplitude)
    cross, near, far = pl.pallas_call(
        rest_kernel,
        out_shape=(lat_halo, depth_halo, depth_halo),
        in_specs=[smem, smem, hbm, hbm, after],
        out_specs=[vmem] * 3,
        scratch_shapes=[pltpu.SemaphoreType.DMA((2, 4)), pltpu.SemaphoreType.DMA((2, 2))],
        compiler_params=small,
        name="take_rest",
    )(lat_rank, depth_rank, grade_field, amplitude, pair)
    far = pass_on(far, cross)
    near = pass_on(near, far)
    pair = swap_near(pair, "lat")
    cross = swap_far(cross, "lat")
    near = swap_near(near, "depth")
    far = swap_far(far, "depth")
    piece = jax.ShapeDtypeStruct((4, rows, cols // pieces), f32)
    half = jax.ShapeDtypeStruct((2, *piece.shape), f32)
    scale = 4.0 / (slices * pieces)
    strips = cols // LANES
    table = pltpu.VMEM((4, SUB, tf_table.shape[1]), f32)
    grade_strips, amp_strips = by_strips(fields[0]), by_strips(fields[1])
    mid, kept = pl.pallas_call(
        functools.partial(middle_kernel, scale, slices, strips),
        out_shape=(
            jax.ShapeDtypeStruct((2, strips, 4, SUB, LANES), f32),
            jax.ShapeDtypeStruct((MZ, strips, TERMS, SUB, LANES), f32),
        ),
        in_specs=[smem, vmem, vmem, vmem],
        out_specs=[vmem, vmem],
        scratch_shapes=[table, table],
        compiler_params=pltpu.CompilerParams(vmem_limit_bytes=8 << 20),
        cost_estimate=pl.CostEstimate(flops=10**10, bytes_accessed=10**8, transcendentals=0),
        name="middle",
    )(brick_mask, grade_strips, amp_strips, tf_table)
    stay, go, kept_ends = pl.pallas_call(
        functools.partial(ends_kernel, scale, pieces, slices, strips),
        out_shape=(half, half, jax.ShapeDtypeStruct((4, strips, TERMS, SUB, LANES), f32)),
        in_specs=[smem, smem] + [vmem] * 7,
        out_specs=[vmem] * 3,
        scratch_shapes=[pltpu.VMEM((2, MY // LANES, 4, SUB, LANES), f32), table, table],
        compiler_params=pltpu.CompilerParams(vmem_limit_bytes=8 << 20),
        name="ends",
    )(brick_mask, depth_rank, grade_strips, amp_strips, by_strips(near), by_strips(far), tf_table, mid, kept)

    def swap_across(x):
        return lax.ppermute(x, "depth", [(i, i ^ 2) for i in range(pieces)])

    own, away_inner = pl.pallas_call(
        merge_kernel,
        out_shape=(piece, piece),
        in_specs=[smem, vmem, vmem],
        out_specs=[vmem, vmem],
        compiler_params=small,
        name="merge",
    )(depth_rank, stay, swap_near(go, "depth"))
    got = swap_across(away_inner)
    rim = jax.ShapeDtypeStruct((4, SUB, cols // pieces // 2), f32)
    rims = pl.pallas_call(
        functools.partial(edge_kernel, pieces),
        out_shape=(rim,) * pieces,
        in_specs=[smem, smem, vmem, vmem, vmem, vmem, after],
        out_specs=[vmem] * pieces,
        compiler_params=small,
        name="edges",
    )(depth_rank, lat_rank, kept, kept_ends, pair, cross, away_inner)
    home, beside, across, corner = rims
    beside = swap_near(beside, "depth")
    across = swap_across(across)
    corner = lax.ppermute(corner, "depth", [(i, i ^ 3) for i in range(pieces)])
    edges = (home, beside, across, corner)
    return pl.pallas_call(
        finish_kernel,
        out_shape=piece,
        in_specs=[smem] + [vmem] * 6,
        out_specs=vmem,
        compiler_params=small,
        name="finish",
    )(depth_rank, own, got, edges[0], edges[2], edges[3], edges[1])


def solution(mesh):
    placed = (P("depth", "lat", None), P("depth", "lat", None), P(), P("depth", "lat", None))
    return jax.shard_map(
        local, mesh=mesh, in_specs=placed, out_specs=P(None, "lat", "depth"), check_vma=False
    )
```

```python
import functools

import jax
import jax.numpy as jnp
from jax import lax
from jax.experimental import pallas as pl
from jax.experimental.pallas import tpu as pltpu
from jax.sharding import PartitionSpec as P

MZ = 8
MX = 8
MY = 256
LANES = 128
SUB = 8
TERMS = 9


def sublane(shape):
    return lax.broadcasted_iota(jnp.int32, shape, len(shape) - 2)


PLACES = ((6, 4, 2, 0), (0, 6, 4, 2))


def row_copies(fields, out_ref, sems, last):
    slices, rows = fields[0].shape[:2]
    span = slices // 4
    made = []
    for f, src in enumerate(fields):
        for q in range(4):
            here = src.at[pl.ds(span * q, span), pl.ds(rows - 2 if last else 0, 2), :]
            made.append(pltpu.make_async_copy(here, out_ref.at[f, :, pl.ds(PLACES[last][q], 2), :], sems.at[f, q]))
    return made


def start_and_wait(copies):
    for copy in copies:
        copy.start()
    for copy in copies:
        copy.wait()


def pair_kernel(lat_ref, grade_hbm, amp_hbm, pair_ref, sems):
    odd = lax.rem(lat_ref[0], 2)
    for last in (0, 1):
        @pl.when(odd == 1 - last)
        def _():
            start_and_wait(row_copies((grade_hbm, amp_hbm), pair_ref, sems, last))


def rest_kernel(lat_ref, depth_ref, grade_hbm, amp_hbm, after_ref, cross_ref, near_ref, far_ref, sems, depth_sems):
    del after_ref
    slices = grade_hbm.shape[0]
    fields = (grade_hbm, amp_hbm)
    odd = lax.rem(depth_ref[0], 2)
    parallel = []
    for f, src in enumerate(fields):
        for n, (dst, at) in enumerate(((near_ref, 1 - odd), (far_ref, odd))):
            here = src.at[pl.ds(at * (slices - 2), 2)]
            parallel.append(pltpu.make_async_copy(here, dst.at[f], depth_sems.at[f, n]))
    odd_lat = lax.rem(lat_ref[0], 2)
    for last in (0, 1):
        @pl.when(odd_lat == last)
        def _():
            start_and_wait(row_copies(fields, cross_ref, sems, last) + parallel)


def pass_on_kernel(*refs):
    del refs


def pass_on(x, *earlier):
    spec = pl.BlockSpec(memory_space=pl.ANY)
    return pl.pallas_call(
        pass_on_kernel,
        out_shape=jax.ShapeDtypeStruct(x.shape, x.dtype),
        in_specs=[spec] * (1 + len(earlier)),
        out_specs=spec,
        input_output_aliases={0: 0},
        compiler_params=pltpu.CompilerParams(vmem_limit_bytes=1 << 20),
        name="pass_on",
    )(x, *earlier)


def round_weight(w):
    return w.astype(jnp.bfloat16).astype(jnp.float32)


def stencil(m2, m1, p1, p2):
    return (m2 - p2) + 8.0 * (p1 - m1)


def fill_tables(scale, table_ref, low_ref, high_ref):
    bins = table_ref.shape[1]
    table = (table_ref[...].astype(jnp.float32) / 65535.0).astype(jnp.bfloat16).astype(jnp.float32)
    table = jnp.where(sublane(table.shape) == 3, table * scale, table)
    column = lax.broadcasted_iota(jnp.int32, table.shape, 1)
    following = jnp.where(column == bins - 1, 0.0, pltpu.roll(table, bins - 1, 1))
    for c in range(4):
        low_ref[c] = jnp.broadcast_to(table[c:c + 1, :], (SUB, bins))
        high_ref[c] = jnp.broadcast_to(following[c:c + 1, :], (SUB, bins))


class Field:
    def __init__(self, ref, slices, strips, s):
        self.ref, self.strips = ref, strips
        self.per_slice = ref.shape[0] // slices
        self.s = s

    def load(self, z, rt, ds=0, k=0):
        start = pl.multiple_of((self.s + ds) * SUB, SUB) + (z * self.per_slice + rt * self.strips * SUB + k)
        return self.ref[pl.ds(start, SUB), :]

    def columns(self, z, rt, mid, lane):
        left = jnp.where(self.s > 0, self.load(z, rt, -jnp.minimum(self.s, 1)), 0.0)
        right = jnp.where(self.s < self.strips - 1, self.load(z, rt, jnp.minimum(self.strips - 1 - self.s, 1)), 0.0)
        return stencil(
            pltpu.roll(jnp.where(lane >= LANES - 2, left, mid), 2, 1),
            pltpu.roll(jnp.where(lane >= LANES - 1, left, mid), 1, 1),
            pltpu.roll(jnp.where(lane < 1, right, mid), LANES - 1, 1),
            pltpu.roll(jnp.where(lane < 2, right, mid), LANES - 2, 1),
        )

    def rows(self, z, rt, mid, sub, roll):
        def shifted(k):
            if k > 0:
                inside = sub < SUB - k
                if rt == 0:
                    return jnp.where(inside, self.load(z, 0, 0, k), self.load(z, 1, 0, k - SUB))
                return jnp.where(inside, pltpu.roll(mid, SUB - k, 0) if roll else self.load(z, 1, 0, k), 0.0)
            inside = sub >= -k
            if rt == 1:
                return jnp.where(inside, self.load(z, 1, 0, k), self.load(z, 0, 0, SUB + k))
            return jnp.where(inside, pltpu.roll(mid, -k, 0) if roll else self.load(z, 0, 0, k), 0.0)

        return stencil(*(shifted(k) for k in (-2, -1, 1, 2)))


def classify(grade, bins, low_ref, high_ref):
    position = grade * (bins - 1.0)
    index = jnp.minimum(position.astype(jnp.int32), bins - 1)
    w_low = 1.0 - (position - index.astype(jnp.float32))
    w_high = round_weight(1.0 - w_low)
    w_low = round_weight(w_low)

    def gather(ref, c):
        return jnp.take_along_axis(ref[c], index, axis=1)

    return [w_low * gather(low_ref, c) + w_high * gather(high_ref, c) for c in range(4)]


def step(state, terms):
    red, green, blue, trans = state
    g_x, a_x, g_yz, a_yz, steep, *cls = terms
    edge = 1.0 - 12.0 * lax.rsqrt(a_x * a_x + a_yz)
    shade = 0.3 + steep * lax.rsqrt(g_x * g_x + g_yz)
    weight = trans * (cls[3] * edge)
    trans = trans - weight
    weight = weight * shade
    return (red + weight * cls[0], green + weight * cls[1], blue + weight * cls[2], trans)


def cell_terms(fields, z, rt, along, roll, bins, low_ref, high_ref):
    lane = lax.broadcasted_iota(jnp.int32, (SUB, LANES), 1)
    sub = sublane((SUB, LANES))
    parts = []
    for field, near in zip(fields, along):
        mid = field.load(z, rt)
        dy = field.columns(z, rt, mid, lane)
        dz = stencil(*near)
        parts.append((mid, field.rows(z, rt, mid, sub, roll), dy * dy + dz * dz, dz))
    (grade, g_x, g_yz, g_z), (_, a_x, a_yz, _) = parts
    cls = classify(grade, bins, low_ref, high_ref)
    return (g_x, a_x, g_yz + 36.0, a_yz + 144.0, 0.7 * jnp.abs(g_z), *cls)


KEPT_AT = ((0, 4), (6, 2))


def keep(kept_ref, zi, s, rt, zb, terms):
    rows = slice(0, 2) if rt == 0 else slice(SUB - 2, SUB)
    at = KEPT_AT[rt][zb]
    for n, term in enumerate(terms):
        kept_ref[zi, s, n, at:at + 2, :] = term[rows, :]


BLANK = (0.0, 0.0, 36.0, 144.0, 0.0, 0.0, 0.0, 0.0, 0.0)


def blank(kept_ref, zi, s, rt, zb):
    at = KEPT_AT[rt][zb]
    for n, value in enumerate(BLANK):
        kept_ref[zi, s, n, at:at + 2, :] = jnp.full((2, LANES), value, jnp.float32)


def middle_kernel(scale, slices, strips, mask_ref, grade_ref, amp_ref, table_ref, mid_ref, kept_ref, low_ref, high_ref):
    bins = table_ref.shape[1]
    fill_tables(scale, table_ref, low_ref, high_ref)
    per_block = MY // LANES
    zero = jnp.zeros((SUB, LANES), jnp.float32)

    def block(cb, carry):
        for rt in range(2):
            def march(halves):
                for j in range(per_block):
                    s = cb * per_block + j
                    fields = [Field(ref, slices, strips, s) for ref in (grade_ref, amp_ref)]
                    state = (zero, zero, zero, zero + 1.0)
                    for zb in halves:
                        for zi in range(2 - 2 * zb, MZ - 2 * zb):
                            z = zb * MZ + zi
                            along = [[field.load(z + k, rt) for k in (-2, -1, 1, 2)] for field in fields]
                            terms = cell_terms(fields, z, rt, along, False, bins, low_ref, high_ref)
                            keep(kept_ref, zi, s, rt, zb, terms)
                            state = step(state, terms)
                    for zb in {0, 1} - set(halves):
                        for zi in range(2 - 2 * zb, MZ - 2 * zb):
                            blank(kept_ref, zi, s, rt, zb)
                    for c in range(4):
                        mid_ref[rt, s, c] = state[c]

            front, back = mask_ref[0, rt, cb] != 0, mask_ref[1, rt, cb] != 0
            pl.when(front & back)(functools.partial(march, (0, 1)))
            pl.when(front & ~back)(functools.partial(march, (0,)))
            pl.when(~front & back)(functools.partial(march, (1,)))
            pl.when(~front & ~back)(functools.partial(march, ()))
        return carry

    lax.fori_loop(0, strips // per_block, block, 0)


def ends_kernel(scale, pieces, slices, strips, for_sibling, mask_ref, depth_ref, grade_ref, amp_ref, near_ref, far_ref,
                table_ref, mid_ref, middle_kept_ref, *rest):
    out_ref, kept_ref, acc_ref, low_ref, high_ref = rest[-5:]
    bins = table_ref.shape[1]
    fill_tables(scale, table_ref, low_ref, high_ref)
    per_block = MY // LANES
    piece_strips = strips // pieces
    piece_blocks = piece_strips // per_block
    zero = jnp.zeros((SUB, LANES), jnp.float32)
    odd = jnp.broadcast_to(lax.rem(depth_ref[0], 2), (SUB, LANES)) == 1

    own_bit = lax.rem(depth_ref[0], 2)
    first_piece = 1 - own_bit if for_sibling else own_bit

    def block(n, carry):
        piece = first_piece + 2 * (n // piece_blocks)
        cb = piece * piece_blocks + lax.rem(n, piece_blocks)
        owner = lax.bitwise_xor(piece, depth_ref[0])
        full = [[mask_ref[zb, rt, cb] for rt in range(2)] for zb in range(2)]

        def march():
            for j in range(per_block):
                s = cb * per_block + j
                for n in range(TERMS):
                    for k, zi in enumerate((0, 1, MZ - 2, MZ - 1)):
                        kept_ref[k, s, n] = middle_kept_ref[zi, s, n]
            for rt in range(2):
                for j in range(per_block):
                    s = cb * per_block + j
                    fields = [Field(ref, slices, strips, s) for ref in (grade_ref, amp_ref)]
                    near, far = (Field(ref, 4, strips, s) for ref in (near_ref, far_ref))
                    state = (zero, zero, zero, zero + 1.0)
                    for zb in range(2):
                        cover = jnp.broadcast_to(full[zb][rt], (SUB, LANES)).astype(jnp.float32)
                        if zb == 1:
                            red, green, blue, trans = state
                            state = tuple(
                                value + trans * mid_ref[rt, s, c] for c, value in enumerate((red, green, blue))
                            ) + (trans * mid_ref[rt, s, 3],)
                        for zi in (0, 1) if zb == 0 else (MZ - 2, MZ - 1):
                            z = zb * MZ + zi
                            along = []
                            for f in range(2):

                                def at(z):
                                    if 0 <= z < slices:
                                        return fields[f].load(z, rt)
                                    k = 2 * f + z % slices % 2
                                    one, two = near.load(k, rt), far.load(k, rt)
                                    return jnp.where(odd, one, two) if z < 0 else jnp.where(odd, two, one)

                                along.append([at(z + k) for k in (-2, -1, 1, 2)])
                            terms = cell_terms(fields, z, rt, along, z in (0, slices - 1), bins, low_ref, high_ref)
                            terms = (*terms[:-1], terms[-1] * cover)
                            keep(kept_ref, zi if zb == 0 else zi - 4, s, rt, zb, terms)
                            state = step(state, terms)
                    for c in range(4):
                        acc_ref[rt, j, c] = state[c]

        some = (full[0][0] | full[0][1] | full[1][0] | full[1][1]) != 0
        pl.when(some)(march)

        @pl.when(jnp.logical_not(some))
        def _():
            for j in range(per_block):
                for n, value in enumerate(BLANK):
                    for k in range(4):
                        kept_ref[k, cb * per_block + j, n] = jnp.full((SUB, LANES), value, jnp.float32)
            for rt in range(2):
                for j in range(per_block):
                    for c in range(4):
                        acc_ref[rt, j, c] = zero if c < 3 else zero + 1.0

        for rt in range(2):
            for c in range(4):
                for j in range(per_block):
                    part = lax.rem(cb, piece_blocks) * MY + j * LANES
                    lanes = pl.ds(pl.multiple_of(part, LANES), LANES)
                    out_ref[owner // 2, c, rt * SUB:(rt + 1) * SUB, lanes] = acc_ref[rt, j, c]
        return carry

    lax.fori_loop(0, pieces // 2 * piece_blocks, block, 0)


def edge_kernel(pieces, depth_ref, lat_ref, kept_ref, stay_ref, go_ref, pair_ref, cross_ref, after_ref, *outs):
    del after_ref
    half = kept_ref.shape[0]
    strips = kept_ref.shape[1]
    sub = sublane((SUB, LANES))
    is_first = lax.rem((sub + 2) // 4, 2) == 0
    odd_lat = jnp.broadcast_to(lax.rem(lat_ref[0], 2), (SUB, LANES))
    from_pair = lax.rem(sub // 2, 2) != odd_lat
    piece_strips = strips // pieces
    packs = piece_strips // 2

    above = lax.rem(sub // 2, 2) == 0
    even_row = lax.rem(sub, 2) == 0

    own_factor = jnp.where(above, 1.0, -1.0)
    mate_factor = jnp.where(above == even_row, -8.0 * own_factor, 0.0)

    def outside(raw):
        mate = jnp.where(even_row, pltpu.roll(raw, SUB - 1, 0), pltpu.roll(raw, 1, 0))
        return own_factor * raw + mate_factor * mate

    def halo(f, zi, lanes):
        pair, cross = pair_ref[f, zi % 4, :, lanes], cross_ref[f, zi % 4, :, lanes]
        if zi < 4:
            return outside(jnp.where(from_pair, pair, cross))
        return outside(pltpu.roll(jnp.where(from_pair, cross, pair), 2, 0))

    def strip(s, ends_ref):
        lanes = pl.ds(pl.multiple_of(s * LANES, LANES), LANES)
        zero = jnp.zeros((SUB, LANES), jnp.float32)
        state = (zero, zero, zero, zero + 1.0)
        for zi in range(half):
            held, at = (kept_ref, zi) if 2 <= zi < half - 2 else (ends_ref, zi % (half - 4))
            g_x, a_x, *others = (held[at, s, n] for n in range(TERMS))
            state = step(state, (g_x + halo(0, zi, lanes), a_x + halo(1, zi, lanes), *others))
        *total, trans = state
        out = [t + trans * pltpu.roll(t, 4, 0) for t in total]
        return out + [trans * pltpu.roll(trans, 4, 0)]

    for n, out in enumerate(outs):
        p = lax.bitwise_xor(n, depth_ref[0])
        results = [strip(p * piece_strips + j, go_ref if n % 2 else stay_ref) for j in range(piece_strips)]
        for j in range(packs):
            for c, (one, two) in enumerate(zip(results[j], results[j + packs])):
                out[c, :, j * LANES:(j + 1) * LANES] = jnp.where(is_first, one, pltpu.roll(two, 4, 0))


def merge(mine, other, rank, level):
    ahead = jnp.broadcast_to(lax.rem(lax.shift_right_logical(rank, level), 2), mine[3].shape) == 0
    clear = jnp.where(ahead, mine[3], other[3])
    return [
        jnp.where(ahead, m, o) + clear * jnp.where(ahead, o, m) for m, o in zip(mine[:3], other[:3])
    ] + [mine[3] * other[3]]


def channels(ref):
    return [ref[c] for c in range(4)]


def merge_kernel(depth_ref, stay_ref, got_ref, own_ref, away_ref):
    for n, out_ref in enumerate((own_ref, away_ref)):
        for c, value in enumerate(merge(channels(stay_ref.at[n]), channels(got_ref.at[n]), depth_ref[0], 0)):
            out_ref[c] = value


def finish_kernel(depth_ref, own_ref, got_ref, home_ref, across_ref, corner_ref, beside_ref, out_ref):
    rows = out_ref.shape[1]
    rank = depth_ref[0]
    frame = merge(channels(own_ref), channels(got_ref), rank, 1)
    near = merge(channels(home_ref), channels(beside_ref), rank, 0)
    far = merge(channels(across_ref), channels(corner_ref), rank, 0)
    rim = merge(near, far, rank, 1)
    for c in range(4):
        inner, packed = frame[c], rim[c]
        if c == 3:
            inner, packed = 1.0 - inner, 1.0 - packed
        wide = jnp.concatenate([packed, pltpu.roll(packed, 4, 0)], axis=1)
        sub = sublane(wide.shape)
        out_ref[c, 0:SUB, :] = jnp.where(sub < 2, wide, inner[0:SUB, :])
        out_ref[c, rows - SUB:rows, :] = jnp.where(sub >= SUB - 2, wide, inner[rows - SUB:rows, :])


def swap_near(x, axis):
    return lax.ppermute(x, axis, [(i, i ^ 1) for i in range(lax.axis_size(axis))])


def swap_far(x, axis):
    size = lax.axis_size(axis)
    return lax.ppermute(x, axis, [(i, j) for k in range(1, size - 1, 2) for i, j in ((k, k + 1), (k + 1, k))])


def by_strips(array):
    rows, cols = array.shape[-2:]
    split = array.reshape(-1, rows // SUB, SUB, cols // LANES, LANES)
    return split.transpose(0, 1, 3, 2, 4).reshape(-1, LANES)


def local(grade_field, amplitude, tf_table, brick_mask):
    slices, rows, cols = grade_field.shape
    pieces = lax.axis_size("depth")
    assert (slices, rows, pieces) == (2 * MZ, 2 * MX, 4)
    depth_rank = lax.axis_index("depth").astype(jnp.int32).reshape(1)
    lat_rank = lax.axis_index("lat").astype(jnp.int32).reshape(1)
    f32 = jnp.float32
    vmem = pl.BlockSpec(memory_space=pltpu.VMEM)
    smem = pl.BlockSpec(memory_space=pltpu.SMEM)
    hbm = pl.BlockSpec(memory_space=pltpu.MemorySpace.HBM)
    lat_halo = jax.ShapeDtypeStruct((2, slices // 4, SUB, cols), f32)
    depth_halo = jax.ShapeDtypeStruct((2, 2, rows, cols), f32)
    hbm_only = pltpu.MemorySpace.HBM
    fields = (grade_field, amplitude)
    grade_field = pltpu.with_memory_space_constraint(grade_field, hbm_only)
    amplitude = pltpu.with_memory_space_constraint(amplitude, hbm_only)
    small = pltpu.CompilerParams(vmem_limit_bytes=4 << 20)
    after = pl.BlockSpec(memory_space=pl.ANY)
    pair = pl.pallas_call(
        pair_kernel,
        out_shape=lat_halo,
        in_specs=[smem, hbm, hbm],
        out_specs=vmem,
        scratch_shapes=[pltpu.SemaphoreType.DMA((2, 4))],
        compiler_params=small,
        name="take_pair",
    )(lat_rank, grade_field, amplitude)
    cross, near, far = pl.pallas_call(
        rest_kernel,
        out_shape=(lat_halo, depth_halo, depth_halo),
        in_specs=[smem, smem, hbm, hbm, after],
        out_specs=[vmem] * 3,
        scratch_shapes=[pltpu.SemaphoreType.DMA((2, 4)), pltpu.SemaphoreType.DMA((2, 2))],
        compiler_params=small,
        name="take_rest",
    )(lat_rank, depth_rank, grade_field, amplitude, pair)
    far = pass_on(far, cross)
    near = pass_on(near, far)
    pair = swap_near(pair, "lat")
    cross = swap_far(cross, "lat")
    near = swap_near(near, "depth")
    far = swap_far(far, "depth")
    piece = jax.ShapeDtypeStruct((4, rows, cols // pieces), f32)
    half = jax.ShapeDtypeStruct((2, *piece.shape), f32)
    scale = 4.0 / (slices * pieces)
    strips = cols // LANES
    table = pltpu.VMEM((4, SUB, tf_table.shape[1]), f32)
    grade_strips, amp_strips = by_strips(fields[0]), by_strips(fields[1])
    mid, kept = pl.pallas_call(
        functools.partial(middle_kernel, scale, slices, strips),
        out_shape=(
            jax.ShapeDtypeStruct((2, strips, 4, SUB, LANES), f32),
            jax.ShapeDtypeStruct((MZ, strips, TERMS, SUB, LANES), f32),
        ),
        in_specs=[smem, vmem, vmem, vmem],
        out_specs=[vmem, vmem],
        scratch_shapes=[table, table],
        compiler_params=pltpu.CompilerParams(vmem_limit_bytes=8 << 20),
        cost_estimate=pl.CostEstimate(flops=10**10, bytes_accessed=10**8, transcendentals=0),
        name="middle",
    )(brick_mask, grade_strips, amp_strips, tf_table)

    def march_ends(for_sibling, *earlier):
        return pl.pallas_call(
            functools.partial(ends_kernel, scale, pieces, slices, strips, for_sibling),
            out_shape=(half, jax.ShapeDtypeStruct((4, strips, TERMS, SUB, LANES), f32)),
            in_specs=[smem, smem] + [vmem] * 7 + [after] * len(earlier),
            out_specs=[vmem] * 2,
            scratch_shapes=[pltpu.VMEM((2, MY // LANES, 4, SUB, LANES), f32), table, table],
            compiler_params=small,
            name="ends",
        )(brick_mask, depth_rank, grade_strips, amp_strips, by_strips(near), by_strips(far), tf_table, mid, kept, *earlier)

    go, kept_go = march_ends(True)
    stay, kept_stay = march_ends(False, go)

    def swap_across(x):
        return lax.ppermute(x, "depth", [(i, i ^ 2) for i in range(pieces)])

    own, away_inner = pl.pallas_call(
        merge_kernel,
        out_shape=(piece, piece),
        in_specs=[smem, vmem, vmem],
        out_specs=[vmem, vmem],
        compiler_params=small,
        name="merge",
    )(depth_rank, stay, swap_near(go, "depth"))
    got = swap_across(away_inner)
    rim = jax.ShapeDtypeStruct((4, SUB, cols // pieces // 2), f32)
    rims = pl.pallas_call(
        functools.partial(edge_kernel, pieces),
        out_shape=(rim,) * pieces,
        in_specs=[smem, smem] + [vmem] * 5 + [after],
        out_specs=[vmem] * pieces,
        compiler_params=small,
        name="edges",
    )(depth_rank, lat_rank, kept, kept_stay, kept_go, pair, cross, away_inner)
    home, beside, across, corner = rims
    beside = swap_near(beside, "depth")
    across = swap_across(across)
    corner = lax.ppermute(corner, "depth", [(i, i ^ 3) for i in range(pieces)])
    edges = (home, beside, across, corner)
    return pl.pallas_call(
        finish_kernel,
        out_shape=piece,
        in_specs=[smem] + [vmem] * 6,
        out_specs=vmem,
        compiler_params=small,
        name="finish",
    )(depth_rank, own, got, edges[0], edges[2], edges[3], edges[1])


def solution(mesh):
    placed = (P("depth", "lat", None), P("depth", "lat", None), P(), P("depth", "lat", None))
    return jax.shard_map(
        local, mesh=mesh, in_specs=placed, out_specs=P(None, "lat", "depth"), check_vma=False
    )
```

```python
import functools

import jax
import jax.numpy as jnp
from jax import lax
from jax.experimental import pallas as pl
from jax.experimental.pallas import tpu as pltpu
from jax.sharding import PartitionSpec as P

MZ = 8
MX = 8
MY = 256
LANES = 128
SUB = 8
TERMS = 9


def sublane(shape):
    return lax.broadcasted_iota(jnp.int32, shape, len(shape) - 2)


PLACES = ((6, 4, 2, 0), (0, 6, 4, 2))


def row_copies(fields, out_ref, sems, last):
    slices, rows = fields[0].shape[:2]
    span = slices // 4
    made = []
    for f, src in enumerate(fields):
        for q in range(4):
            here = src.at[pl.ds(span * q, span), pl.ds(rows - 2 if last else 0, 2), :]
            made.append(pltpu.make_async_copy(here, out_ref.at[f, :, pl.ds(PLACES[last][q], 2), :], sems.at[f, q]))
    return made


def start_and_wait(copies):
    for copy in copies:
        copy.start()
    for copy in copies:
        copy.wait()


def pair_kernel(lat_ref, grade_hbm, amp_hbm, pair_ref, sems):
    odd = lax.rem(lat_ref[0], 2)
    for last in (0, 1):
        @pl.when(odd == 1 - last)
        def _():
            start_and_wait(row_copies((grade_hbm, amp_hbm), pair_ref, sems, last))


def rest_kernel(lat_ref, depth_ref, grade_hbm, amp_hbm, after_ref, cross_ref, near_ref, far_ref, sems, depth_sems):
    del after_ref
    slices = grade_hbm.shape[0]
    fields = (grade_hbm, amp_hbm)
    odd = lax.rem(depth_ref[0], 2)
    parallel = []
    for f, src in enumerate(fields):
        for n, (dst, at) in enumerate(((near_ref, 1 - odd), (far_ref, odd))):
            here = src.at[pl.ds(at * (slices - 2), 2)]
            parallel.append(pltpu.make_async_copy(here, dst.at[f], depth_sems.at[f, n]))
    odd_lat = lax.rem(lat_ref[0], 2)
    for last in (0, 1):
        @pl.when(odd_lat == last)
        def _():
            start_and_wait(row_copies(fields, cross_ref, sems, last) + parallel)


def pass_on_kernel(*refs):
    del refs


def pass_on(x, *earlier):
    spec = pl.BlockSpec(memory_space=pl.ANY)
    return pl.pallas_call(
        pass_on_kernel,
        out_shape=jax.ShapeDtypeStruct(x.shape, x.dtype),
        in_specs=[spec] * (1 + len(earlier)),
        out_specs=spec,
        input_output_aliases={0: 0},
        compiler_params=pltpu.CompilerParams(vmem_limit_bytes=1 << 20),
        name="pass_on",
    )(x, *earlier)


def round_weight(w):
    return w.astype(jnp.bfloat16).astype(jnp.float32)


def stencil(m2, m1, p1, p2):
    return (m2 - p2) + 8.0 * (p1 - m1)


def fill_tables(scale, table_ref, low_ref, high_ref):
    bins = table_ref.shape[1]
    table = (table_ref[...].astype(jnp.float32) / 65535.0).astype(jnp.bfloat16).astype(jnp.float32)
    table = jnp.where(sublane(table.shape) == 3, table * scale, table)
    column = lax.broadcasted_iota(jnp.int32, table.shape, 1)
    following = jnp.where(column == bins - 1, 0.0, pltpu.roll(table, bins - 1, 1))
    for c in range(4):
        low_ref[c] = jnp.broadcast_to(table[c:c + 1, :], (SUB, bins))
        high_ref[c] = jnp.broadcast_to(following[c:c + 1, :], (SUB, bins))


class Field:
    def __init__(self, ref, slices, strips, s):
        self.ref, self.strips = ref, strips
        self.per_slice = ref.shape[0] // slices
        self.s = s

    def load(self, z, rt, ds=0, k=0):
        start = pl.multiple_of((self.s + ds) * SUB, SUB) + (z * self.per_slice + rt * self.strips * SUB + k)
        return self.ref[pl.ds(start, SUB), :]

    def columns(self, z, rt, mid, lane):
        left = jnp.where(self.s > 0, self.load(z, rt, -jnp.minimum(self.s, 1)), 0.0)
        right = jnp.where(self.s < self.strips - 1, self.load(z, rt, jnp.minimum(self.strips - 1 - self.s, 1)), 0.0)
        return stencil(
            pltpu.roll(jnp.where(lane >= LANES - 2, left, mid), 2, 1),
            pltpu.roll(jnp.where(lane >= LANES - 1, left, mid), 1, 1),
            pltpu.roll(jnp.where(lane < 1, right, mid), LANES - 1, 1),
            pltpu.roll(jnp.where(lane < 2, right, mid), LANES - 2, 1),
        )

    def rows(self, z, rt, mid, sub, roll):
        def shifted(k):
            if k > 0:
                inside = sub < SUB - k
                if rt == 0:
                    return jnp.where(inside, self.load(z, 0, 0, k), self.load(z, 1, 0, k - SUB))
                return jnp.where(inside, pltpu.roll(mid, SUB - k, 0) if roll else self.load(z, 1, 0, k), 0.0)
            inside = sub >= -k
            if rt == 1:
                return jnp.where(inside, self.load(z, 1, 0, k), self.load(z, 0, 0, SUB + k))
            return jnp.where(inside, pltpu.roll(mid, -k, 0) if roll else self.load(z, 0, 0, k), 0.0)

        return stencil(*(shifted(k) for k in (-2, -1, 1, 2)))


def classify(grade, bins, low_ref, high_ref):
    position = grade * (bins - 1.0)
    index = jnp.minimum(position.astype(jnp.int32), bins - 1)
    w_low = 1.0 - (position - index.astype(jnp.float32))
    w_high = round_weight(1.0 - w_low)
    w_low = round_weight(w_low)

    def gather(ref, c):
        return jnp.take_along_axis(ref[c], index, axis=1)

    return [w_low * gather(low_ref, c) + w_high * gather(high_ref, c) for c in range(4)]


def step(state, terms):
    red, green, blue, trans = state
    g_x, a_x, g_yz, a_yz, steep, *cls = terms
    edge = 1.0 - 12.0 * lax.rsqrt(a_x * a_x + a_yz)
    shade = 0.3 + steep * lax.rsqrt(g_x * g_x + g_yz)
    weight = trans * (cls[3] * edge)
    trans = trans - weight
    weight = weight * shade
    return (red + weight * cls[0], green + weight * cls[1], blue + weight * cls[2], trans)


def cell_terms(fields, z, rt, along, roll, bins, low_ref, high_ref):
    lane = lax.broadcasted_iota(jnp.int32, (SUB, LANES), 1)
    sub = sublane((SUB, LANES))
    parts = []
    for field, near in zip(fields, along):
        mid = field.load(z, rt)
        dy = field.columns(z, rt, mid, lane)
        dz = stencil(*near)
        parts.append((mid, field.rows(z, rt, mid, sub, roll), dy * dy + dz * dz, dz))
    (grade, g_x, g_yz, g_z), (_, a_x, a_yz, _) = parts
    cls = classify(grade, bins, low_ref, high_ref)
    return (g_x, a_x, g_yz + 36.0, a_yz + 144.0, 0.7 * jnp.abs(g_z), *cls)


KEPT_AT = ((0, 4), (6, 2))


def keep(kept_ref, zi, s, rt, zb, terms):
    rows = slice(0, 2) if rt == 0 else slice(SUB - 2, SUB)
    at = KEPT_AT[rt][zb]
    for n, term in enumerate(terms):
        kept_ref[zi, s, n, at:at + 2, :] = term[rows, :]


BLANK = (0.0, 0.0, 36.0, 144.0, 0.0, 0.0, 0.0, 0.0, 0.0)


def blank(kept_ref, zi, s, rt, zb):
    at = KEPT_AT[rt][zb]
    for n, value in enumerate(BLANK):
        kept_ref[zi, s, n, at:at + 2, :] = jnp.full((2, LANES), value, jnp.float32)


def middle_kernel(scale, slices, strips, mask_ref, grade_ref, amp_ref, table_ref, mid_ref, kept_ref, low_ref, high_ref):
    bins = table_ref.shape[1]
    fill_tables(scale, table_ref, low_ref, high_ref)
    per_block = MY // LANES
    zero = jnp.zeros((SUB, LANES), jnp.float32)

    def block(cb, carry):
        for rt in range(2):
            def march(halves):
                for j in range(per_block):
                    s = cb * per_block + j
                    fields = [Field(ref, slices, strips, s) for ref in (grade_ref, amp_ref)]
                    state = (zero, zero, zero, zero + 1.0)
                    for zb in halves:
                        for zi in range(2 - 2 * zb, MZ - 2 * zb):
                            z = zb * MZ + zi
                            along = [[field.load(z + k, rt) for k in (-2, -1, 1, 2)] for field in fields]
                            terms = cell_terms(fields, z, rt, along, False, bins, low_ref, high_ref)
                            keep(kept_ref, zi, s, rt, zb, terms)
                            state = step(state, terms)
                    for zb in {0, 1} - set(halves):
                        for zi in range(2 - 2 * zb, MZ - 2 * zb):
                            blank(kept_ref, zi, s, rt, zb)
                    for c in range(4):
                        mid_ref[rt, s, c] = state[c]

            front, back = mask_ref[0, rt, cb] != 0, mask_ref[1, rt, cb] != 0
            pl.when(front & back)(functools.partial(march, (0, 1)))
            pl.when(front & ~back)(functools.partial(march, (0,)))
            pl.when(~front & back)(functools.partial(march, (1,)))
            pl.when(~front & ~back)(functools.partial(march, ()))
        return carry

    lax.fori_loop(0, strips // per_block, block, 0)


def ends_kernel(scale, pieces, slices, strips, for_sibling, mask_ref, depth_ref, grade_ref, amp_ref, near_ref, far_ref,
                table_ref, mid_ref, middle_kept_ref, *rest):
    out_ref, kept_ref, acc_ref, low_ref, high_ref = rest[-5:]
    bins = table_ref.shape[1]
    fill_tables(scale, table_ref, low_ref, high_ref)
    per_block = MY // LANES
    piece_strips = strips // pieces
    piece_blocks = piece_strips // per_block
    zero = jnp.zeros((SUB, LANES), jnp.float32)
    odd = jnp.broadcast_to(lax.rem(depth_ref[0], 2), (SUB, LANES)) == 1

    own_bit = lax.rem(depth_ref[0], 2)
    first_piece = 1 - own_bit if for_sibling else own_bit

    def block(n, carry):
        piece = first_piece + 2 * (n // piece_blocks)
        cb = piece * piece_blocks + lax.rem(n, piece_blocks)
        owner = lax.bitwise_xor(piece, depth_ref[0])
        full = [[mask_ref[zb, rt, cb] for rt in range(2)] for zb in range(2)]

        def march():
            for j in range(per_block):
                s = cb * per_block + j
                for n in range(TERMS):
                    for k, zi in enumerate((0, 1, MZ - 2, MZ - 1)):
                        kept_ref[k, s, n] = middle_kept_ref[zi, s, n]
            for rt in range(2):
                for j in range(per_block):
                    s = cb * per_block + j
                    fields = [Field(ref, slices, strips, s) for ref in (grade_ref, amp_ref)]
                    near, far = (Field(ref, 4, strips, s) for ref in (near_ref, far_ref))
                    state = (zero, zero, zero, zero + 1.0)
                    for zb in range(2):
                        cover = jnp.broadcast_to(full[zb][rt], (SUB, LANES)).astype(jnp.float32)
                        if zb == 1:
                            red, green, blue, trans = state
                            state = tuple(
                                value + trans * mid_ref[rt, s, c] for c, value in enumerate((red, green, blue))
                            ) + (trans * mid_ref[rt, s, 3],)
                        for zi in (0, 1) if zb == 0 else (MZ - 2, MZ - 1):
                            z = zb * MZ + zi
                            along = []
                            for f in range(2):

                                def at(z):
                                    if 0 <= z < slices:
                                        return fields[f].load(z, rt)
                                    k = 2 * f + z % slices % 2
                                    one, two = near.load(k, rt), far.load(k, rt)
                                    return jnp.where(odd, one, two) if z < 0 else jnp.where(odd, two, one)

                                along.append([at(z + k) for k in (-2, -1, 1, 2)])
                            terms = cell_terms(fields, z, rt, along, z in (0, slices - 1), bins, low_ref, high_ref)
                            terms = (*terms[:-1], terms[-1] * cover)
                            keep(kept_ref, zi if zb == 0 else zi - 4, s, rt, zb, terms)
                            state = step(state, terms)
                    for c in range(4):
                        acc_ref[rt, j, c] = state[c]

        some = (full[0][0] | full[0][1] | full[1][0] | full[1][1]) != 0
        pl.when(some)(march)

        @pl.when(jnp.logical_not(some))
        def _():
            for j in range(per_block):
                for n, value in enumerate(BLANK):
                    for k in range(4):
                        kept_ref[k, cb * per_block + j, n] = jnp.full((SUB, LANES), value, jnp.float32)
            for rt in range(2):
                for j in range(per_block):
                    for c in range(4):
                        acc_ref[rt, j, c] = zero if c < 3 else zero + 1.0

        for rt in range(2):
            for c in range(4):
                for j in range(per_block):
                    part = lax.rem(cb, piece_blocks) * MY + j * LANES
                    lanes = pl.ds(pl.multiple_of(part, LANES), LANES)
                    out_ref[owner // 2, c, rt * SUB:(rt + 1) * SUB, lanes] = acc_ref[rt, j, c]
        return carry

    lax.fori_loop(0, pieces // 2 * piece_blocks, block, 0)


def edge_kernel(pieces, which, depth_ref, lat_ref, kept_ref, stay_ref, go_ref, pair_ref, cross_ref, after_ref, *outs):
    del after_ref
    half = kept_ref.shape[0]
    strips = kept_ref.shape[1]
    sub = sublane((SUB, LANES))
    is_first = lax.rem((sub + 2) // 4, 2) == 0
    odd_lat = jnp.broadcast_to(lax.rem(lat_ref[0], 2), (SUB, LANES))
    from_pair = lax.rem(sub // 2, 2) != odd_lat
    piece_strips = strips // pieces
    packs = piece_strips // 2

    above = lax.rem(sub // 2, 2) == 0
    even_row = lax.rem(sub, 2) == 0

    own_factor = jnp.where(above, 1.0, -1.0)
    mate_factor = jnp.where(above == even_row, -8.0 * own_factor, 0.0)

    def outside(raw):
        mate = jnp.where(even_row, pltpu.roll(raw, SUB - 1, 0), pltpu.roll(raw, 1, 0))
        return own_factor * raw + mate_factor * mate

    def halo(f, zi, lanes):
        pair, cross = pair_ref[f, zi % 4, :, lanes], cross_ref[f, zi % 4, :, lanes]
        if zi < 4:
            return outside(jnp.where(from_pair, pair, cross))
        return outside(pltpu.roll(jnp.where(from_pair, cross, pair), 2, 0))

    def strip(s, ends_ref):
        lanes = pl.ds(pl.multiple_of(s * LANES, LANES), LANES)
        zero = jnp.zeros((SUB, LANES), jnp.float32)
        state = (zero, zero, zero, zero + 1.0)
        for zi in range(half):
            held, at = (kept_ref, zi) if 2 <= zi < half - 2 else (ends_ref, zi % (half - 4))
            g_x, a_x, *others = (held[at, s, n] for n in range(TERMS))
            state = step(state, (g_x + halo(0, zi, lanes), a_x + halo(1, zi, lanes), *others))
        *total, trans = state
        out = [t + trans * pltpu.roll(t, 4, 0) for t in total]
        return out + [trans * pltpu.roll(trans, 4, 0)]

    for n, out in zip(which, outs):
        p = lax.bitwise_xor(n, depth_ref[0])
        results = [strip(p * piece_strips + j, go_ref if n % 2 else stay_ref) for j in range(piece_strips)]
        for j in range(packs):
            for c, (one, two) in enumerate(zip(results[j], results[j + packs])):
                out[c, :, j * LANES:(j + 1) * LANES] = jnp.where(is_first, one, pltpu.roll(two, 4, 0))


def merge(mine, other, rank, level):
    ahead = jnp.broadcast_to(lax.rem(lax.shift_right_logical(rank, level), 2), mine[3].shape) == 0
    clear = jnp.where(ahead, mine[3], other[3])
    return [
        jnp.where(ahead, m, o) + clear * jnp.where(ahead, o, m) for m, o in zip(mine[:3], other[:3])
    ] + [mine[3] * other[3]]


def channels(ref):
    return [ref[c] for c in range(4)]


def merge_kernel(depth_ref, stay_ref, got_ref, own_ref, away_ref):
    for n, out_ref in enumerate((own_ref, away_ref)):
        for c, value in enumerate(merge(channels(stay_ref.at[n]), channels(got_ref.at[n]), depth_ref[0], 0)):
            out_ref[c] = value


def finish_kernel(depth_ref, own_ref, got_ref, home_ref, across_ref, corner_ref, beside_ref, out_ref):
    rows = out_ref.shape[1]
    rank = depth_ref[0]
    frame = merge(channels(own_ref), channels(got_ref), rank, 1)
    near = merge(channels(home_ref), channels(beside_ref), rank, 0)
    far = merge(channels(across_ref), channels(corner_ref), rank, 0)
    rim = merge(near, far, rank, 1)
    for c in range(4):
        inner, packed = frame[c], rim[c]
        if c == 3:
            inner, packed = 1.0 - inner, 1.0 - packed
        wide = jnp.concatenate([packed, pltpu.roll(packed, 4, 0)], axis=1)
        sub = sublane(wide.shape)
        out_ref[c, 0:SUB, :] = jnp.where(sub < 2, wide, inner[0:SUB, :])
        out_ref[c, rows - SUB:rows, :] = jnp.where(sub >= SUB - 2, wide, inner[rows - SUB:rows, :])


def swap_near(x, axis):
    return lax.ppermute(x, axis, [(i, i ^ 1) for i in range(lax.axis_size(axis))])


def swap_far(x, axis):
    size = lax.axis_size(axis)
    return lax.ppermute(x, axis, [(i, j) for k in range(1, size - 1, 2) for i, j in ((k, k + 1), (k + 1, k))])


def by_strips(array):
    rows, cols = array.shape[-2:]
    split = array.reshape(-1, rows // SUB, SUB, cols // LANES, LANES)
    return split.transpose(0, 1, 3, 2, 4).reshape(-1, LANES)


def local(grade_field, amplitude, tf_table, brick_mask):
    slices, rows, cols = grade_field.shape
    pieces = lax.axis_size("depth")
    assert (slices, rows, pieces) == (2 * MZ, 2 * MX, 4)
    depth_rank = lax.axis_index("depth").astype(jnp.int32).reshape(1)
    lat_rank = lax.axis_index("lat").astype(jnp.int32).reshape(1)
    f32 = jnp.float32
    vmem = pl.BlockSpec(memory_space=pltpu.VMEM)
    smem = pl.BlockSpec(memory_space=pltpu.SMEM)
    hbm = pl.BlockSpec(memory_space=pltpu.MemorySpace.HBM)
    lat_halo = jax.ShapeDtypeStruct((2, slices // 4, SUB, cols), f32)
    depth_halo = jax.ShapeDtypeStruct((2, 2, rows, cols), f32)
    hbm_only = pltpu.MemorySpace.HBM
    fields = (grade_field, amplitude)
    grade_field = pltpu.with_memory_space_constraint(grade_field, hbm_only)
    amplitude = pltpu.with_memory_space_constraint(amplitude, hbm_only)
    small = pltpu.CompilerParams(vmem_limit_bytes=4 << 20)
    after = pl.BlockSpec(memory_space=pl.ANY)
    pair = pl.pallas_call(
        pair_kernel,
        out_shape=lat_halo,
        in_specs=[smem, hbm, hbm],
        out_specs=vmem,
        scratch_shapes=[pltpu.SemaphoreType.DMA((2, 4))],
        compiler_params=small,
        name="take_pair",
    )(lat_rank, grade_field, amplitude)
    cross, near, far = pl.pallas_call(
        rest_kernel,
        out_shape=(lat_halo, depth_halo, depth_halo),
        in_specs=[smem, smem, hbm, hbm, after],
        out_specs=[vmem] * 3,
        scratch_shapes=[pltpu.SemaphoreType.DMA((2, 4)), pltpu.SemaphoreType.DMA((2, 2))],
        compiler_params=small,
        name="take_rest",
    )(lat_rank, depth_rank, grade_field, amplitude, pair)
    far = pass_on(far, cross)
    near = pass_on(near, far)
    pair = swap_near(pair, "lat")
    cross = swap_far(cross, "lat")
    near = swap_near(near, "depth")
    far = swap_far(far, "depth")
    piece = jax.ShapeDtypeStruct((4, rows, cols // pieces), f32)
    half = jax.ShapeDtypeStruct((2, *piece.shape), f32)
    scale = 4.0 / (slices * pieces)
    strips = cols // LANES
    table = pltpu.VMEM((4, SUB, tf_table.shape[1]), f32)
    grade_strips, amp_strips = by_strips(fields[0]), by_strips(fields[1])
    mid, kept = pl.pallas_call(
        functools.partial(middle_kernel, scale, slices, strips),
        out_shape=(
            jax.ShapeDtypeStruct((2, strips, 4, SUB, LANES), f32),
            jax.ShapeDtypeStruct((MZ, strips, TERMS, SUB, LANES), f32),
        ),
        in_specs=[smem, vmem, vmem, vmem],
        out_specs=[vmem, vmem],
        scratch_shapes=[table, table],
        compiler_params=pltpu.CompilerParams(vmem_limit_bytes=8 << 20),
        cost_estimate=pl.CostEstimate(flops=10**10, bytes_accessed=10**8, transcendentals=0),
        name="middle",
    )(brick_mask, grade_strips, amp_strips, tf_table)

    def march_ends(for_sibling, *earlier):
        return pl.pallas_call(
            functools.partial(ends_kernel, scale, pieces, slices, strips, for_sibling),
            out_shape=(half, jax.ShapeDtypeStruct((4, strips, TERMS, SUB, LANES), f32)),
            in_specs=[smem, smem] + [vmem] * 7 + [after] * len(earlier),
            out_specs=[vmem] * 2,
            scratch_shapes=[pltpu.VMEM((2, MY // LANES, 4, SUB, LANES), f32), table, table],
            compiler_params=small,
            name="ends",
        )(brick_mask, depth_rank, grade_strips, amp_strips, by_strips(near), by_strips(far), tf_table, mid, kept, *earlier)

    go, kept_go = march_ends(True)
    stay, kept_stay = march_ends(False, go)

    def swap_across(x):
        return lax.ppermute(x, "depth", [(i, i ^ 2) for i in range(pieces)])

    own, away_inner = pl.pallas_call(
        merge_kernel,
        out_shape=(piece, piece),
        in_specs=[smem, vmem, vmem],
        out_specs=[vmem, vmem],
        compiler_params=small,
        name="merge",
    )(depth_rank, stay, swap_near(go, "depth"))
    got = swap_across(away_inner)
    rim = jax.ShapeDtypeStruct((4, SUB, cols // pieces // 2), f32)

    def edges_of(which, earlier):
        return pl.pallas_call(
            functools.partial(edge_kernel, pieces, which),
            out_shape=(rim,) * len(which),
            in_specs=[smem, smem] + [vmem] * 5 + [after],
            out_specs=[vmem] * len(which),
            compiler_params=small,
            name="edges",
        )(depth_rank, lat_rank, kept, kept_stay, kept_go, pair, cross, earlier)

    across, corner = edges_of((2, 3), away_inner)
    beside, home = edges_of((1, 0), got)
    beside = swap_near(beside, "depth")
    across = swap_across(across)
    corner = lax.ppermute(corner, "depth", [(i, i ^ 3) for i in range(pieces)])
    edges = (home, beside, across, corner)
    return pl.pallas_call(
        finish_kernel,
        out_shape=piece,
        in_specs=[smem] + [vmem] * 6,
        out_specs=vmem,
        compiler_params=small,
        name="finish",
    )(depth_rank, own, got, edges[0], edges[2], edges[3], edges[1])


def solution(mesh):
    placed = (P("depth", "lat", None), P("depth", "lat", None), P(), P("depth", "lat", None))
    return jax.shard_map(
        local, mesh=mesh, in_specs=placed, out_specs=P(None, "lat", "depth"), check_vma=False
    )
```

```python
import functools

import jax
import jax.numpy as jnp
from jax import lax
from jax.experimental import pallas as pl
from jax.experimental.pallas import tpu as pltpu
from jax.sharding import PartitionSpec as P

MZ = 8
MX = 8
MY = 256
LANES = 128
SUB = 8
TERMS = 9


def sublane(shape):
    return lax.broadcasted_iota(jnp.int32, shape, len(shape) - 2)


PLACES = ((6, 4, 2, 0), (0, 6, 4, 2))


def row_copies(fields, out_ref, sems, last):
    slices, rows = fields[0].shape[:2]
    span = slices // 4
    made = []
    for f, src in enumerate(fields):
        for q in range(4):
            here = src.at[pl.ds(span * q, span), pl.ds(rows - 2 if last else 0, 2), :]
            made.append(pltpu.make_async_copy(here, out_ref.at[f, :, pl.ds(PLACES[last][q], 2), :], sems.at[f, q]))
    return made


def start_and_wait(copies):
    for copy in copies:
        copy.start()
    for copy in copies:
        copy.wait()


def pair_kernel(lat_ref, grade_hbm, amp_hbm, pair_ref, sems):
    odd = lax.rem(lat_ref[0], 2)
    for last in (0, 1):
        @pl.when(odd == 1 - last)
        def _():
            start_and_wait(row_copies((grade_hbm, amp_hbm), pair_ref, sems, last))


def rest_kernel(lat_ref, depth_ref, grade_hbm, amp_hbm, after_ref, cross_ref, near_ref, far_ref, sems, depth_sems):
    del after_ref
    slices = grade_hbm.shape[0]
    fields = (grade_hbm, amp_hbm)
    odd = lax.rem(depth_ref[0], 2)
    parallel = []
    for f, src in enumerate(fields):
        for n, (dst, at) in enumerate(((near_ref, 1 - odd), (far_ref, odd))):
            here = src.at[pl.ds(at * (slices - 2), 2)]
            parallel.append(pltpu.make_async_copy(here, dst.at[f], depth_sems.at[f, n]))
    odd_lat = lax.rem(lat_ref[0], 2)
    for last in (0, 1):
        @pl.when(odd_lat == last)
        def _():
            start_and_wait(row_copies(fields, cross_ref, sems, last) + parallel)


def pass_on_kernel(*refs):
    del refs


def pass_on(x, *earlier):
    spec = pl.BlockSpec(memory_space=pl.ANY)
    return pl.pallas_call(
        pass_on_kernel,
        out_shape=jax.ShapeDtypeStruct(x.shape, x.dtype),
        in_specs=[spec] * (1 + len(earlier)),
        out_specs=spec,
        input_output_aliases={0: 0},
        compiler_params=pltpu.CompilerParams(vmem_limit_bytes=1 << 20),
        name="pass_on",
    )(x, *earlier)


def round_weight(w):
    return w.astype(jnp.bfloat16).astype(jnp.float32)


def stencil(m2, m1, p1, p2):
    return (m2 - p2) + 8.0 * (p1 - m1)


def fill_tables(scale, table_ref, low_ref, high_ref):
    bins = table_ref.shape[1]
    table = (table_ref[...].astype(jnp.float32) / 65535.0).astype(jnp.bfloat16).astype(jnp.float32)
    table = jnp.where(sublane(table.shape) == 3, table * scale, table)
    column = lax.broadcasted_iota(jnp.int32, table.shape, 1)
    following = jnp.where(column == bins - 1, 0.0, pltpu.roll(table, bins - 1, 1))
    for c in range(4):
        low_ref[c] = jnp.broadcast_to(table[c:c + 1, :], (SUB, bins))
        high_ref[c] = jnp.broadcast_to(following[c:c + 1, :], (SUB, bins))


class Field:
    def __init__(self, ref, slices, strips, s):
        self.ref, self.strips = ref, strips
        self.per_slice = ref.shape[0] // slices
        self.s = s

    def load(self, z, rt, ds=0, k=0):
        start = pl.multiple_of((self.s + ds) * SUB, SUB) + (z * self.per_slice + rt * self.strips * SUB + k)
        return self.ref[pl.ds(start, SUB), :]

    def columns(self, z, rt, mid, lane):
        left = jnp.where(self.s > 0, self.load(z, rt, -jnp.minimum(self.s, 1)), 0.0)
        right = jnp.where(self.s < self.strips - 1, self.load(z, rt, jnp.minimum(self.strips - 1 - self.s, 1)), 0.0)
        return stencil(
            pltpu.roll(jnp.where(lane >= LANES - 2, left, mid), 2, 1),
            pltpu.roll(jnp.where(lane >= LANES - 1, left, mid), 1, 1),
            pltpu.roll(jnp.where(lane < 1, right, mid), LANES - 1, 1),
            pltpu.roll(jnp.where(lane < 2, right, mid), LANES - 2, 1),
        )

    def rows(self, z, rt, mid, sub, roll):
        def shifted(k):
            if k > 0:
                inside = sub < SUB - k
                if rt == 0:
                    return jnp.where(inside, self.load(z, 0, 0, k), self.load(z, 1, 0, k - SUB))
                return jnp.where(inside, pltpu.roll(mid, SUB - k, 0) if roll else self.load(z, 1, 0, k), 0.0)
            inside = sub >= -k
            if rt == 1:
                return jnp.where(inside, self.load(z, 1, 0, k), self.load(z, 0, 0, SUB + k))
            return jnp.where(inside, pltpu.roll(mid, -k, 0) if roll else self.load(z, 0, 0, k), 0.0)

        return stencil(*(shifted(k) for k in (-2, -1, 1, 2)))


def classify(grade, bins, low_ref, high_ref):
    position = grade * (bins - 1.0)
    index = jnp.minimum(position.astype(jnp.int32), bins - 1)
    w_low = 1.0 - (position - index.astype(jnp.float32))
    w_high = round_weight(1.0 - w_low)
    w_low = round_weight(w_low)

    def gather(ref, c):
        return jnp.take_along_axis(ref[c], index, axis=1)

    return [w_low * gather(low_ref, c) + w_high * gather(high_ref, c) for c in range(4)]


def step(state, terms):
    red, green, blue, trans = state
    g_x, a_x, g_yz, a_yz, steep, *cls = terms
    edge = 1.0 - 12.0 * lax.rsqrt(a_x * a_x + a_yz)
    shade = 0.3 + steep * lax.rsqrt(g_x * g_x + g_yz)
    weight = trans * (cls[3] * edge)
    trans = trans - weight
    weight = weight * shade
    return (red + weight * cls[0], green + weight * cls[1], blue + weight * cls[2], trans)


def cell_terms(fields, z, rt, along, roll, bins, low_ref, high_ref):
    lane = lax.broadcasted_iota(jnp.int32, (SUB, LANES), 1)
    sub = sublane((SUB, LANES))
    parts = []
    for field, near in zip(fields, along):
        mid = field.load(z, rt)
        dy = field.columns(z, rt, mid, lane)
        dz = stencil(*near)
        parts.append((mid, field.rows(z, rt, mid, sub, roll), dy * dy + dz * dz, dz))
    (grade, g_x, g_yz, g_z), (_, a_x, a_yz, _) = parts
    cls = classify(grade, bins, low_ref, high_ref)
    return (g_x, a_x, g_yz + 36.0, a_yz + 144.0, 0.7 * jnp.abs(g_z), *cls)


KEPT_AT = ((0, 4), (6, 2))


def keep(kept_ref, zi, s, rt, zb, terms):
    rows = slice(0, 2) if rt == 0 else slice(SUB - 2, SUB)
    at = KEPT_AT[rt][zb]
    for n, term in enumerate(terms):
        kept_ref[zi, s, n, at:at + 2, :] = term[rows, :]


BLANK = (0.0, 0.0, 36.0, 144.0, 0.0, 0.0, 0.0, 0.0, 0.0)


def blank(kept_ref, zi, s, rt, zb):
    at = KEPT_AT[rt][zb]
    for n, value in enumerate(BLANK):
        kept_ref[zi, s, n, at:at + 2, :] = jnp.full((2, LANES), value, jnp.float32)


def middle_kernel(scale, slices, strips, mask_ref, grade_ref, amp_ref, table_ref, mid_ref, kept_ref, low_ref, high_ref):
    bins = table_ref.shape[1]
    fill_tables(scale, table_ref, low_ref, high_ref)
    per_block = MY // LANES
    zero = jnp.zeros((SUB, LANES), jnp.float32)

    def block(cb, carry):
        for rt in range(2):
            def march(halves):
                for j in range(per_block):
                    s = cb * per_block + j
                    fields = [Field(ref, slices, strips, s) for ref in (grade_ref, amp_ref)]
                    state = (zero, zero, zero, zero + 1.0)
                    for zb in halves:
                        for zi in range(2 - 2 * zb, MZ - 2 * zb):
                            z = zb * MZ + zi
                            along = [[field.load(z + k, rt) for k in (-2, -1, 1, 2)] for field in fields]
                            terms = cell_terms(fields, z, rt, along, False, bins, low_ref, high_ref)
                            keep(kept_ref, zi, s, rt, zb, terms)
                            state = step(state, terms)
                    for zb in {0, 1} - set(halves):
                        for zi in range(2 - 2 * zb, MZ - 2 * zb):
                            blank(kept_ref, zi, s, rt, zb)
                    for c in range(4):
                        mid_ref[rt, s, c] = state[c]

            front, back = mask_ref[0, rt, cb] != 0, mask_ref[1, rt, cb] != 0
            pl.when(front & back)(functools.partial(march, (0, 1)))
            pl.when(front & ~back)(functools.partial(march, (0,)))
            pl.when(~front & back)(functools.partial(march, (1,)))
            pl.when(~front & ~back)(functools.partial(march, ()))
        return carry

    lax.fori_loop(0, strips // per_block, block, 0)


def ends_kernel(scale, pieces, slices, strips, for_sibling, mask_ref, depth_ref, grade_ref, amp_ref, near_ref, far_ref,
                table_ref, mid_ref, middle_kept_ref, *rest):
    out_ref, kept_ref, acc_ref, low_ref, high_ref = rest[-5:]
    bins = table_ref.shape[1]
    fill_tables(scale, table_ref, low_ref, high_ref)
    per_block = MY // LANES
    piece_strips = strips // pieces
    piece_blocks = piece_strips // per_block
    zero = jnp.zeros((SUB, LANES), jnp.float32)
    odd = jnp.broadcast_to(lax.rem(depth_ref[0], 2), (SUB, LANES)) == 1

    own_bit = lax.rem(depth_ref[0], 2)
    first_piece = 1 - own_bit if for_sibling else own_bit

    def block(n, carry):
        piece = first_piece + 2 * (n // piece_blocks)
        cb = piece * piece_blocks + lax.rem(n, piece_blocks)
        owner = lax.bitwise_xor(piece, depth_ref[0])
        full = [[mask_ref[zb, rt, cb] for rt in range(2)] for zb in range(2)]

        def march():
            for j in range(per_block):
                s = cb * per_block + j
                for n in range(TERMS):
                    for k, zi in enumerate((0, 1, MZ - 2, MZ - 1)):
                        kept_ref[k, s, n] = middle_kept_ref[zi, s, n]
            for rt in range(2):
                for j in range(per_block):
                    s = cb * per_block + j
                    fields = [Field(ref, slices, strips, s) for ref in (grade_ref, amp_ref)]
                    near, far = (Field(ref, 4, strips, s) for ref in (near_ref, far_ref))
                    state = (zero, zero, zero, zero + 1.0)
                    for zb in range(2):
                        cover = jnp.broadcast_to(full[zb][rt], (SUB, LANES)).astype(jnp.float32)
                        if zb == 1:
                            red, green, blue, trans = state
                            state = tuple(
                                value + trans * mid_ref[rt, s, c] for c, value in enumerate((red, green, blue))
                            ) + (trans * mid_ref[rt, s, 3],)
                        for zi in (0, 1) if zb == 0 else (MZ - 2, MZ - 1):
                            z = zb * MZ + zi
                            along = []
                            for f in range(2):

                                def at(z):
                                    if 0 <= z < slices:
                                        return fields[f].load(z, rt)
                                    k = 2 * f + z % slices % 2
                                    one, two = near.load(k, rt), far.load(k, rt)
                                    return jnp.where(odd, one, two) if z < 0 else jnp.where(odd, two, one)

                                along.append([at(z + k) for k in (-2, -1, 1, 2)])
                            terms = cell_terms(fields, z, rt, along, z in (0, slices - 1), bins, low_ref, high_ref)
                            terms = (*terms[:-1], terms[-1] * cover)
                            keep(kept_ref, zi if zb == 0 else zi - 4, s, rt, zb, terms)
                            state = step(state, terms)
                    for c in range(4):
                        acc_ref[rt, j, c] = state[c]

        some = (full[0][0] | full[0][1] | full[1][0] | full[1][1]) != 0
        pl.when(some)(march)

        @pl.when(jnp.logical_not(some))
        def _():
            for j in range(per_block):
                for n, value in enumerate(BLANK):
                    for k in range(4):
                        kept_ref[k, cb * per_block + j, n] = jnp.full((SUB, LANES), value, jnp.float32)
            for rt in range(2):
                for j in range(per_block):
                    for c in range(4):
                        acc_ref[rt, j, c] = zero if c < 3 else zero + 1.0

        for rt in range(2):
            for c in range(4):
                for j in range(per_block):
                    part = lax.rem(cb, piece_blocks) * MY + j * LANES
                    lanes = pl.ds(pl.multiple_of(part, LANES), LANES)
                    out_ref[owner // 2, c, rt * SUB:(rt + 1) * SUB, lanes] = acc_ref[rt, j, c]
        return carry

    lax.fori_loop(0, pieces // 2 * piece_blocks, block, 0)


def edge_kernel(pieces, which, depth_ref, lat_ref, kept_ref, stay_ref, go_ref, pair_ref, cross_ref, after_ref, *outs):
    del after_ref
    half = kept_ref.shape[0]
    strips = kept_ref.shape[1]
    sub = sublane((SUB, LANES))
    is_first = lax.rem((sub + 2) // 4, 2) == 0
    odd_lat = jnp.broadcast_to(lax.rem(lat_ref[0], 2), (SUB, LANES))
    from_pair = lax.rem(sub // 2, 2) != odd_lat
    piece_strips = strips // pieces
    packs = piece_strips // 2

    above = lax.rem(sub // 2, 2) == 0
    even_row = lax.rem(sub, 2) == 0

    own_factor = jnp.where(above, 1.0, -1.0)
    mate_factor = jnp.where(above == even_row, -8.0 * own_factor, 0.0)

    def outside(raw):
        mate = jnp.where(even_row, pltpu.roll(raw, SUB - 1, 0), pltpu.roll(raw, 1, 0))
        return own_factor * raw + mate_factor * mate

    def halo(f, zi, lanes):
        pair, cross = pair_ref[f, zi % 4, :, lanes], cross_ref[f, zi % 4, :, lanes]
        if zi < 4:
            return outside(jnp.where(from_pair, pair, cross))
        return outside(pltpu.roll(jnp.where(from_pair, cross, pair), 2, 0))

    def strip(s, ends_ref):
        lanes = pl.ds(pl.multiple_of(s * LANES, LANES), LANES)
        zero = jnp.zeros((SUB, LANES), jnp.float32)
        state = (zero, zero, zero, zero + 1.0)
        for zi in range(half):
            held, at = (kept_ref, zi) if 2 <= zi < half - 2 else (ends_ref, zi % (half - 4))
            g_x, a_x, *others = (held[at, s, n] for n in range(TERMS))
            state = step(state, (g_x + halo(0, zi, lanes), a_x + halo(1, zi, lanes), *others))
        *total, trans = state
        out = [t + trans * pltpu.roll(t, 4, 0) for t in total]
        return out + [trans * pltpu.roll(trans, 4, 0)]

    for n, out in zip(which, outs):
        p = lax.bitwise_xor(n, depth_ref[0])
        results = [strip(p * piece_strips + j, go_ref if n % 2 else stay_ref) for j in range(piece_strips)]
        for j in range(packs):
            for c, (one, two) in enumerate(zip(results[j], results[j + packs])):
                out[c, :, j * LANES:(j + 1) * LANES] = jnp.where(is_first, one, pltpu.roll(two, 4, 0))


def merge(mine, other, rank, level):
    ahead = jnp.broadcast_to(lax.rem(lax.shift_right_logical(rank, level), 2), mine[3].shape) == 0
    clear = jnp.where(ahead, mine[3], other[3])
    return [
        jnp.where(ahead, m, o) + clear * jnp.where(ahead, o, m) for m, o in zip(mine[:3], other[:3])
    ] + [mine[3] * other[3]]


def channels(ref):
    return [ref[c] for c in range(4)]


def merge_kernel(depth_ref, stay_ref, got_ref, own_ref, away_ref):
    for n, out_ref in enumerate((own_ref, away_ref)):
        for c, value in enumerate(merge(channels(stay_ref.at[n]), channels(got_ref.at[n]), depth_ref[0], 0)):
            out_ref[c] = value


def finish_kernel(depth_ref, own_ref, got_ref, home_ref, across_ref, corner_ref, beside_ref, out_ref):
    rows = out_ref.shape[1]
    rank = depth_ref[0]
    frame = merge(channels(own_ref), channels(got_ref), rank, 1)
    near = merge(channels(home_ref), channels(beside_ref), rank, 0)
    far = merge(channels(across_ref), channels(corner_ref), rank, 0)
    rim = merge(near, far, rank, 1)
    for c in range(4):
        inner, packed = frame[c], rim[c]
        if c == 3:
            inner, packed = 1.0 - inner, 1.0 - packed
        wide = jnp.concatenate([packed, pltpu.roll(packed, 4, 0)], axis=1)
        sub = sublane(wide.shape)
        out_ref[c, 0:SUB, :] = jnp.where(sub < 2, wide, inner[0:SUB, :])
        out_ref[c, rows - SUB:rows, :] = jnp.where(sub >= SUB - 2, wide, inner[rows - SUB:rows, :])


def swap_near(x, axis):
    return lax.ppermute(x, axis, [(i, i ^ 1) for i in range(lax.axis_size(axis))])


def swap_far(x, axis):
    size = lax.axis_size(axis)
    return lax.ppermute(x, axis, [(i, j) for k in range(1, size - 1, 2) for i, j in ((k, k + 1), (k + 1, k))])


def by_strips(array):
    rows, cols = array.shape[-2:]
    split = array.reshape(-1, rows // SUB, SUB, cols // LANES, LANES)
    return split.transpose(0, 1, 3, 2, 4).reshape(-1, LANES)


def local(grade_field, amplitude, tf_table, brick_mask):
    slices, rows, cols = grade_field.shape
    pieces = lax.axis_size("depth")
    assert (slices, rows, pieces) == (2 * MZ, 2 * MX, 4)
    depth_rank = lax.axis_index("depth").astype(jnp.int32).reshape(1)
    lat_rank = lax.axis_index("lat").astype(jnp.int32).reshape(1)
    f32 = jnp.float32
    vmem = pl.BlockSpec(memory_space=pltpu.VMEM)
    smem = pl.BlockSpec(memory_space=pltpu.SMEM)
    hbm = pl.BlockSpec(memory_space=pltpu.MemorySpace.HBM)
    lat_halo = jax.ShapeDtypeStruct((2, slices // 4, SUB, cols), f32)
    depth_halo = jax.ShapeDtypeStruct((2, 2, rows, cols), f32)
    hbm_only = pltpu.MemorySpace.HBM
    fields = (grade_field, amplitude)
    grade_field = pltpu.with_memory_space_constraint(grade_field, hbm_only)
    amplitude = pltpu.with_memory_space_constraint(amplitude, hbm_only)
    small = pltpu.CompilerParams(vmem_limit_bytes=4 << 20)
    after = pl.BlockSpec(memory_space=pl.ANY)
    pair = pl.pallas_call(
        pair_kernel,
        out_shape=lat_halo,
        in_specs=[smem, hbm, hbm],
        out_specs=vmem,
        scratch_shapes=[pltpu.SemaphoreType.DMA((2, 4))],
        compiler_params=small,
        name="take_pair",
    )(lat_rank, grade_field, amplitude)
    cross, near, far = pl.pallas_call(
        rest_kernel,
        out_shape=(lat_halo, depth_halo, depth_halo),
        in_specs=[smem, smem, hbm, hbm, after],
        out_specs=[vmem] * 3,
        scratch_shapes=[pltpu.SemaphoreType.DMA((2, 4)), pltpu.SemaphoreType.DMA((2, 2))],
        compiler_params=small,
        name="take_rest",
    )(lat_rank, depth_rank, grade_field, amplitude, pair)
    far = pass_on(far, cross)
    near = pass_on(near, far)
    pair = swap_near(pair, "lat")
    cross = swap_far(cross, "lat")
    near = swap_near(near, "depth")
    far = swap_far(far, "depth")
    piece = jax.ShapeDtypeStruct((4, rows, cols // pieces), f32)
    half = jax.ShapeDtypeStruct((2, *piece.shape), f32)
    scale = 4.0 / (slices * pieces)
    strips = cols // LANES
    table = pltpu.VMEM((4, SUB, tf_table.shape[1]), f32)
    grade_strips, amp_strips = by_strips(fields[0]), by_strips(fields[1])
    mid, kept = pl.pallas_call(
        functools.partial(middle_kernel, scale, slices, strips),
        out_shape=(
            jax.ShapeDtypeStruct((2, strips, 4, SUB, LANES), f32),
            jax.ShapeDtypeStruct((MZ, strips, TERMS, SUB, LANES), f32),
        ),
        in_specs=[smem, vmem, vmem, vmem],
        out_specs=[vmem, vmem],
        scratch_shapes=[table, table],
        compiler_params=pltpu.CompilerParams(vmem_limit_bytes=8 << 20),
        cost_estimate=pl.CostEstimate(flops=10**10, bytes_accessed=10**8, transcendentals=0),
        name="middle",
    )(brick_mask, grade_strips, amp_strips, tf_table)

    def march_ends(for_sibling, *earlier):
        return pl.pallas_call(
            functools.partial(ends_kernel, scale, pieces, slices, strips, for_sibling),
            out_shape=(half, jax.ShapeDtypeStruct((4, strips, TERMS, SUB, LANES), f32)),
            in_specs=[smem, smem] + [vmem] * 7 + [after] * len(earlier),
            out_specs=[vmem] * 2,
            scratch_shapes=[pltpu.VMEM((2, MY // LANES, 4, SUB, LANES), f32), table, table],
            compiler_params=small,
            name="ends",
        )(brick_mask, depth_rank, grade_strips, amp_strips, by_strips(near), by_strips(far), tf_table, mid, kept, *earlier)

    go, kept_go = march_ends(True)
    stay, kept_stay = march_ends(False, go)

    def swap_across(x):
        return lax.ppermute(x, "depth", [(i, i ^ 2) for i in range(pieces)])

    own, away_inner = pl.pallas_call(
        merge_kernel,
        out_shape=(piece, piece),
        in_specs=[smem, vmem, vmem],
        out_specs=[vmem, vmem],
        compiler_params=small,
        name="merge",
    )(depth_rank, stay, swap_near(go, "depth"))
    got = swap_across(away_inner)
    rim = jax.ShapeDtypeStruct((4, SUB, cols // pieces // 2), f32)

    def edges_of(which, earlier):
        return pl.pallas_call(
            functools.partial(edge_kernel, pieces, which),
            out_shape=(rim,) * len(which),
            in_specs=[smem, smem] + [vmem] * 5 + [after],
            out_specs=[vmem] * len(which),
            compiler_params=small,
            name="edges",
        )(depth_rank, lat_rank, kept, kept_stay, kept_go, pair, cross, earlier)

    across, corner, beside = edges_of((2, 3, 1), away_inner)
    (home,) = edges_of((0,), beside)
    beside = swap_near(beside, "depth")
    across = swap_across(across)
    corner = lax.ppermute(corner, "depth", [(i, i ^ 3) for i in range(pieces)])
    edges = (home, beside, across, corner)
    return pl.pallas_call(
        finish_kernel,
        out_shape=piece,
        in_specs=[smem] + [vmem] * 6,
        out_specs=vmem,
        compiler_params=small,
        name="finish",
    )(depth_rank, own, got, edges[0], edges[2], edges[3], edges[1])


def solution(mesh):
    placed = (P("depth", "lat", None), P("depth", "lat", None), P(), P("depth", "lat", None))
    return jax.shard_map(
        local, mesh=mesh, in_specs=placed, out_specs=P(None, "lat", "depth"), check_vma=False
    )
```

```python
import functools

import jax
import jax.numpy as jnp
from jax import lax
from jax.experimental import pallas as pl
from jax.experimental.pallas import tpu as pltpu
from jax.sharding import PartitionSpec as P

MZ = 8
MX = 8
MY = 256
LANES = 128
SUB = 8
TERMS = 9


def sublane(shape):
    return lax.broadcasted_iota(jnp.int32, shape, len(shape) - 2)


PLACES = ((6, 4, 2, 0), (0, 6, 4, 2))


def row_copies(fields, out_ref, sems, last):
    slices, rows = fields[0].shape[:2]
    span = slices // 4
    made = []
    for f, src in enumerate(fields):
        for q in range(4):
            here = src.at[pl.ds(span * q, span), pl.ds(rows - 2 if last else 0, 2), :]
            made.append(pltpu.make_async_copy(here, out_ref.at[f, :, pl.ds(PLACES[last][q], 2), :], sems.at[f, q]))
    return made


def start_and_wait(copies):
    for copy in copies:
        copy.start()
    for copy in copies:
        copy.wait()


def pair_kernel(lat_ref, grade_hbm, amp_hbm, pair_ref, sems):
    odd = lax.rem(lat_ref[0], 2)
    for last in (0, 1):
        @pl.when(odd == 1 - last)
        def _():
            start_and_wait(row_copies((grade_hbm, amp_hbm), pair_ref, sems, last))


def rest_kernel(lat_ref, depth_ref, grade_hbm, amp_hbm, after_ref, cross_ref, near_ref, far_ref, sems, depth_sems):
    del after_ref
    slices = grade_hbm.shape[0]
    fields = (grade_hbm, amp_hbm)
    odd = lax.rem(depth_ref[0], 2)
    parallel = []
    for f, src in enumerate(fields):
        for n, (dst, at) in enumerate(((near_ref, 1 - odd), (far_ref, odd))):
            here = src.at[pl.ds(at * (slices - 2), 2)]
            parallel.append(pltpu.make_async_copy(here, dst.at[f], depth_sems.at[f, n]))
    odd_lat = lax.rem(lat_ref[0], 2)
    for last in (0, 1):
        @pl.when(odd_lat == last)
        def _():
            start_and_wait(row_copies(fields, cross_ref, sems, last) + parallel)


def pass_on_kernel(*refs):
    del refs


def pass_on(x, *earlier):
    spec = pl.BlockSpec(memory_space=pl.ANY)
    return pl.pallas_call(
        pass_on_kernel,
        out_shape=jax.ShapeDtypeStruct(x.shape, x.dtype),
        in_specs=[spec] * (1 + len(earlier)),
        out_specs=spec,
        input_output_aliases={0: 0},
        compiler_params=pltpu.CompilerParams(vmem_limit_bytes=1 << 20),
        name="pass_on",
    )(x, *earlier)


def round_weight(w):
    return w.astype(jnp.bfloat16).astype(jnp.float32)


def stencil(m2, m1, p1, p2):
    return (m2 - p2) + 8.0 * (p1 - m1)


def fill_tables(scale, table_ref, low_ref, high_ref):
    bins = table_ref.shape[1]
    table = (table_ref[...].astype(jnp.float32) / 65535.0).astype(jnp.bfloat16).astype(jnp.float32)
    table = jnp.where(sublane(table.shape) == 3, table * scale, table)
    column = lax.broadcasted_iota(jnp.int32, table.shape, 1)
    following = jnp.where(column == bins - 1, 0.0, pltpu.roll(table, bins - 1, 1))
    for c in range(4):
        low_ref[c] = jnp.broadcast_to(table[c:c + 1, :], (SUB, bins))
        high_ref[c] = jnp.broadcast_to(following[c:c + 1, :], (SUB, bins))


class Field:
    def __init__(self, ref, slices, strips, s):
        self.ref, self.strips = ref, strips
        self.per_slice = ref.shape[0] // slices
        self.s = s

    def load(self, z, rt, ds=0, k=0):
        start = pl.multiple_of((self.s + ds) * SUB, SUB) + (z * self.per_slice + rt * self.strips * SUB + k)
        return self.ref[pl.ds(start, SUB), :]

    def columns(self, z, rt, mid, lane):
        left = jnp.where(self.s > 0, self.load(z, rt, -jnp.minimum(self.s, 1)), 0.0)
        right = jnp.where(self.s < self.strips - 1, self.load(z, rt, jnp.minimum(self.strips - 1 - self.s, 1)), 0.0)
        return stencil(
            pltpu.roll(jnp.where(lane >= LANES - 2, left, mid), 2, 1),
            pltpu.roll(jnp.where(lane >= LANES - 1, left, mid), 1, 1),
            pltpu.roll(jnp.where(lane < 1, right, mid), LANES - 1, 1),
            pltpu.roll(jnp.where(lane < 2, right, mid), LANES - 2, 1),
        )

    def rows(self, z, rt, mid, sub, roll):
        def shifted(k):
            if k > 0:
                inside = sub < SUB - k
                if rt == 0:
                    return jnp.where(inside, self.load(z, 0, 0, k), self.load(z, 1, 0, k - SUB))
                return jnp.where(inside, pltpu.roll(mid, SUB - k, 0) if roll else self.load(z, 1, 0, k), 0.0)
            inside = sub >= -k
            if rt == 1:
                return jnp.where(inside, self.load(z, 1, 0, k), self.load(z, 0, 0, SUB + k))
            return jnp.where(inside, pltpu.roll(mid, -k, 0) if roll else self.load(z, 0, 0, k), 0.0)

        return stencil(*(shifted(k) for k in (-2, -1, 1, 2)))


def classify(grade, bins, low_ref, high_ref):
    position = grade * (bins - 1.0)
    index = jnp.minimum(position.astype(jnp.int32), bins - 1)
    w_low = 1.0 - (position - index.astype(jnp.float32))
    w_high = round_weight(1.0 - w_low)
    w_low = round_weight(w_low)

    def gather(ref, c):
        return jnp.take_along_axis(ref[c], index, axis=1)

    return [w_low * gather(low_ref, c) + w_high * gather(high_ref, c) for c in range(4)]


def step(state, terms):
    red, green, blue, trans = state
    g_x, a_x, g_yz, a_yz, steep, *cls = terms
    edge = 1.0 - 12.0 * lax.rsqrt(a_x * a_x + a_yz)
    shade = 0.3 + steep * lax.rsqrt(g_x * g_x + g_yz)
    weight = trans * (cls[3] * edge)
    trans = trans - weight
    weight = weight * shade
    return (red + weight * cls[0], green + weight * cls[1], blue + weight * cls[2], trans)


def cell_terms(fields, z, rt, along, roll, bins, low_ref, high_ref):
    lane = lax.broadcasted_iota(jnp.int32, (SUB, LANES), 1)
    sub = sublane((SUB, LANES))
    parts = []
    for field, near in zip(fields, along):
        mid = field.load(z, rt)
        dy = field.columns(z, rt, mid, lane)
        dz = stencil(*near)
        parts.append((mid, field.rows(z, rt, mid, sub, roll), dy * dy + dz * dz, dz))
    (grade, g_x, g_yz, g_z), (_, a_x, a_yz, _) = parts
    cls = classify(grade, bins, low_ref, high_ref)
    return (g_x, a_x, g_yz + 36.0, a_yz + 144.0, 0.7 * jnp.abs(g_z), *cls)


KEPT_AT = ((0, 4), (6, 2))


def keep(kept_ref, zi, s, rt, zb, terms):
    rows = slice(0, 2) if rt == 0 else slice(SUB - 2, SUB)
    at = KEPT_AT[rt][zb]
    for n, term in enumerate(terms):
        kept_ref[zi, s, n, at:at + 2, :] = term[rows, :]


BLANK = (0.0, 0.0, 36.0, 144.0, 0.0, 0.0, 0.0, 0.0, 0.0)


def blank(kept_ref, zi, s, rt, zb):
    at = KEPT_AT[rt][zb]
    for n, value in enumerate(BLANK):
        kept_ref[zi, s, n, at:at + 2, :] = jnp.full((2, LANES), value, jnp.float32)


def middle_kernel(scale, slices, strips, mask_ref, grade_ref, amp_ref, table_ref, mid_ref, kept_ref, low_ref, high_ref):
    bins = table_ref.shape[1]
    fill_tables(scale, table_ref, low_ref, high_ref)
    per_block = MY // LANES
    zero = jnp.zeros((SUB, LANES), jnp.float32)

    def block(cb, carry):
        for rt in range(2):
            def march(halves):
                tiles = [cb * per_block + j for j in range(per_block)]
                fields = [[Field(ref, slices, strips, s) for ref in (grade_ref, amp_ref)] for s in tiles]
                states = [(zero, zero, zero, zero + 1.0)] * per_block
                for zb in halves:
                    for zi in range(2 - 2 * zb, MZ - 2 * zb):
                        z = zb * MZ + zi
                        for j, s in enumerate(tiles):
                            along = [[field.load(z + k, rt) for k in (-2, -1, 1, 2)] for field in fields[j]]
                            terms = cell_terms(fields[j], z, rt, along, False, bins, low_ref, high_ref)
                            keep(kept_ref, zi, s, rt, zb, terms)
                            states[j] = step(states[j], terms)
                for j, s in enumerate(tiles):
                    for zb in {0, 1} - set(halves):
                        for zi in range(2 - 2 * zb, MZ - 2 * zb):
                            blank(kept_ref, zi, s, rt, zb)
                    for c in range(4):
                        mid_ref[rt, s, c] = states[j][c]

            front, back = mask_ref[0, rt, cb] != 0, mask_ref[1, rt, cb] != 0
            pl.when(front & back)(functools.partial(march, (0, 1)))
            pl.when(front & ~back)(functools.partial(march, (0,)))
            pl.when(~front & back)(functools.partial(march, (1,)))
            pl.when(~front & ~back)(functools.partial(march, ()))
        return carry

    lax.fori_loop(0, strips // per_block, block, 0)


def ends_kernel(scale, pieces, slices, strips, for_sibling, mask_ref, depth_ref, grade_ref, amp_ref, near_ref, far_ref,
                table_ref, mid_ref, middle_kept_ref, *rest):
    out_ref, kept_ref, acc_ref, low_ref, high_ref = rest[-5:]
    bins = table_ref.shape[1]
    fill_tables(scale, table_ref, low_ref, high_ref)
    per_block = MY // LANES
    piece_strips = strips // pieces
    piece_blocks = piece_strips // per_block
    zero = jnp.zeros((SUB, LANES), jnp.float32)
    odd = jnp.broadcast_to(lax.rem(depth_ref[0], 2), (SUB, LANES)) == 1

    own_bit = lax.rem(depth_ref[0], 2)
    first_piece = 1 - own_bit if for_sibling else own_bit

    def block(n, carry):
        piece = first_piece + 2 * (n // piece_blocks)
        cb = piece * piece_blocks + lax.rem(n, piece_blocks)
        owner = lax.bitwise_xor(piece, depth_ref[0])
        full = [[mask_ref[zb, rt, cb] for rt in range(2)] for zb in range(2)]

        def march():
            for j in range(per_block):
                s = cb * per_block + j
                for n in range(TERMS):
                    for k, zi in enumerate((0, 1, MZ - 2, MZ - 1)):
                        kept_ref[k, s, n] = middle_kept_ref[zi, s, n]
            for rt in range(2):
                for j in range(per_block):
                    s = cb * per_block + j
                    fields = [Field(ref, slices, strips, s) for ref in (grade_ref, amp_ref)]
                    near, far = (Field(ref, 4, strips, s) for ref in (near_ref, far_ref))
                    state = (zero, zero, zero, zero + 1.0)
                    for zb in range(2):
                        cover = jnp.broadcast_to(full[zb][rt], (SUB, LANES)).astype(jnp.float32)
                        if zb == 1:
                            red, green, blue, trans = state
                            state = tuple(
                                value + trans * mid_ref[rt, s, c] for c, value in enumerate((red, green, blue))
                            ) + (trans * mid_ref[rt, s, 3],)
                        for zi in (0, 1) if zb == 0 else (MZ - 2, MZ - 1):
                            z = zb * MZ + zi
                            along = []
                            for f in range(2):

                                def at(z):
                                    if 0 <= z < slices:
                                        return fields[f].load(z, rt)
                                    k = 2 * f + z % slices % 2
                                    one, two = near.load(k, rt), far.load(k, rt)
                                    return jnp.where(odd, one, two) if z < 0 else jnp.where(odd, two, one)

                                along.append([at(z + k) for k in (-2, -1, 1, 2)])
                            terms = cell_terms(fields, z, rt, along, z in (0, slices - 1), bins, low_ref, high_ref)
                            terms = (*terms[:-1], terms[-1] * cover)
                            keep(kept_ref, zi if zb == 0 else zi - 4, s, rt, zb, terms)
                            state = step(state, terms)
                    for c in range(4):
                        acc_ref[rt, j, c] = state[c]

        some = (full[0][0] | full[0][1] | full[1][0] | full[1][1]) != 0
        pl.when(some)(march)

        @pl.when(jnp.logical_not(some))
        def _():
            for j in range(per_block):
                for n, value in enumerate(BLANK):
                    for k in range(4):
                        kept_ref[k, cb * per_block + j, n] = jnp.full((SUB, LANES), value, jnp.float32)
            for rt in range(2):
                for j in range(per_block):
                    for c in range(4):
                        acc_ref[rt, j, c] = zero if c < 3 else zero + 1.0

        for rt in range(2):
            for c in range(4):
                for j in range(per_block):
                    part = lax.rem(cb, piece_blocks) * MY + j * LANES
                    lanes = pl.ds(pl.multiple_of(part, LANES), LANES)
                    out_ref[owner // 2, c, rt * SUB:(rt + 1) * SUB, lanes] = acc_ref[rt, j, c]
        return carry

    lax.fori_loop(0, pieces // 2 * piece_blocks, block, 0)


def edge_kernel(pieces, which, depth_ref, lat_ref, kept_ref, stay_ref, go_ref, pair_ref, cross_ref, after_ref, *outs):
    del after_ref
    half = kept_ref.shape[0]
    strips = kept_ref.shape[1]
    sub = sublane((SUB, LANES))
    is_first = lax.rem((sub + 2) // 4, 2) == 0
    odd_lat = jnp.broadcast_to(lax.rem(lat_ref[0], 2), (SUB, LANES))
    from_pair = lax.rem(sub // 2, 2) != odd_lat
    piece_strips = strips // pieces
    packs = piece_strips // 2

    above = lax.rem(sub // 2, 2) == 0
    even_row = lax.rem(sub, 2) == 0

    own_factor = jnp.where(above, 1.0, -1.0)
    mate_factor = jnp.where(above == even_row, -8.0 * own_factor, 0.0)

    def outside(raw):
        mate = jnp.where(even_row, pltpu.roll(raw, SUB - 1, 0), pltpu.roll(raw, 1, 0))
        return own_factor * raw + mate_factor * mate

    def halo(f, zi, lanes):
        pair, cross = pair_ref[f, zi % 4, :, lanes], cross_ref[f, zi % 4, :, lanes]
        if zi < 4:
            return outside(jnp.where(from_pair, pair, cross))
        return outside(pltpu.roll(jnp.where(from_pair, cross, pair), 2, 0))

    def strip(s, ends_ref):
        lanes = pl.ds(pl.multiple_of(s * LANES, LANES), LANES)
        zero = jnp.zeros((SUB, LANES), jnp.float32)
        state = (zero, zero, zero, zero + 1.0)
        for zi in range(half):
            held, at = (kept_ref, zi) if 2 <= zi < half - 2 else (ends_ref, zi % (half - 4))
            g_x, a_x, *others = (held[at, s, n] for n in range(TERMS))
            state = step(state, (g_x + halo(0, zi, lanes), a_x + halo(1, zi, lanes), *others))
        *total, trans = state
        out = [t + trans * pltpu.roll(t, 4, 0) for t in total]
        return out + [trans * pltpu.roll(trans, 4, 0)]

    for n, out in zip(which, outs):
        p = lax.bitwise_xor(n, depth_ref[0])
        results = [strip(p * piece_strips + j, go_ref if n % 2 else stay_ref) for j in range(piece_strips)]
        for j in range(packs):
            for c, (one, two) in enumerate(zip(results[j], results[j + packs])):
                out[c, :, j * LANES:(j + 1) * LANES] = jnp.where(is_first, one, pltpu.roll(two, 4, 0))


def merge(mine, other, rank, level):
    ahead = jnp.broadcast_to(lax.rem(lax.shift_right_logical(rank, level), 2), mine[3].shape) == 0
    clear = jnp.where(ahead, mine[3], other[3])
    return [
        jnp.where(ahead, m, o) + clear * jnp.where(ahead, o, m) for m, o in zip(mine[:3], other[:3])
    ] + [mine[3] * other[3]]


def channels(ref):
    return [ref[c] for c in range(4)]


def merge_kernel(depth_ref, stay_ref, got_ref, own_ref, away_ref):
    for n, out_ref in enumerate((own_ref, away_ref)):
        for c, value in enumerate(merge(channels(stay_ref.at[n]), channels(got_ref.at[n]), depth_ref[0], 0)):
            out_ref[c] = value


def finish_kernel(depth_ref, own_ref, got_ref, home_ref, across_ref, corner_ref, beside_ref, out_ref):
    rows = out_ref.shape[1]
    rank = depth_ref[0]
    frame = merge(channels(own_ref), channels(got_ref), rank, 1)
    near = merge(channels(home_ref), channels(beside_ref), rank, 0)
    far = merge(channels(across_ref), channels(corner_ref), rank, 0)
    rim = merge(near, far, rank, 1)
    for c in range(4):
        inner, packed = frame[c], rim[c]
        if c == 3:
            inner, packed = 1.0 - inner, 1.0 - packed
        wide = jnp.concatenate([packed, pltpu.roll(packed, 4, 0)], axis=1)
        sub = sublane(wide.shape)
        out_ref[c, 0:SUB, :] = jnp.where(sub < 2, wide, inner[0:SUB, :])
        out_ref[c, rows - SUB:rows, :] = jnp.where(sub >= SUB - 2, wide, inner[rows - SUB:rows, :])


def swap_near(x, axis):
    return lax.ppermute(x, axis, [(i, i ^ 1) for i in range(lax.axis_size(axis))])


def swap_far(x, axis):
    size = lax.axis_size(axis)
    return lax.ppermute(x, axis, [(i, j) for k in range(1, size - 1, 2) for i, j in ((k, k + 1), (k + 1, k))])


def by_strips(array):
    rows, cols = array.shape[-2:]
    split = array.reshape(-1, rows // SUB, SUB, cols // LANES, LANES)
    return split.transpose(0, 1, 3, 2, 4).reshape(-1, LANES)


def local(grade_field, amplitude, tf_table, brick_mask):
    slices, rows, cols = grade_field.shape
    pieces = lax.axis_size("depth")
    assert (slices, rows, pieces) == (2 * MZ, 2 * MX, 4)
    depth_rank = lax.axis_index("depth").astype(jnp.int32).reshape(1)
    lat_rank = lax.axis_index("lat").astype(jnp.int32).reshape(1)
    f32 = jnp.float32
    vmem = pl.BlockSpec(memory_space=pltpu.VMEM)
    smem = pl.BlockSpec(memory_space=pltpu.SMEM)
    hbm = pl.BlockSpec(memory_space=pltpu.MemorySpace.HBM)
    lat_halo = jax.ShapeDtypeStruct((2, slices // 4, SUB, cols), f32)
    depth_halo = jax.ShapeDtypeStruct((2, 2, rows, cols), f32)
    hbm_only = pltpu.MemorySpace.HBM
    fields = (grade_field, amplitude)
    grade_field = pltpu.with_memory_space_constraint(grade_field, hbm_only)
    amplitude = pltpu.with_memory_space_constraint(amplitude, hbm_only)
    small = pltpu.CompilerParams(vmem_limit_bytes=4 << 20)
    after = pl.BlockSpec(memory_space=pl.ANY)
    pair = pl.pallas_call(
        pair_kernel,
        out_shape=lat_halo,
        in_specs=[smem, hbm, hbm],
        out_specs=vmem,
        scratch_shapes=[pltpu.SemaphoreType.DMA((2, 4))],
        compiler_params=small,
        name="take_pair",
    )(lat_rank, grade_field, amplitude)
    cross, near, far = pl.pallas_call(
        rest_kernel,
        out_shape=(lat_halo, depth_halo, depth_halo),
        in_specs=[smem, smem, hbm, hbm, after],
        out_specs=[vmem] * 3,
        scratch_shapes=[pltpu.SemaphoreType.DMA((2, 4)), pltpu.SemaphoreType.DMA((2, 2))],
        compiler_params=small,
        name="take_rest",
    )(lat_rank, depth_rank, grade_field, amplitude, pair)
    far = pass_on(far, cross)
    near = pass_on(near, far)
    pair = swap_near(pair, "lat")
    cross = swap_far(cross, "lat")
    near = swap_near(near, "depth")
    far = swap_far(far, "depth")
    piece = jax.ShapeDtypeStruct((4, rows, cols // pieces), f32)
    half = jax.ShapeDtypeStruct((2, *piece.shape), f32)
    scale = 4.0 / (slices * pieces)
    strips = cols // LANES
    table = pltpu.VMEM((4, SUB, tf_table.shape[1]), f32)
    grade_strips, amp_strips = by_strips(fields[0]), by_strips(fields[1])
    mid, kept = pl.pallas_call(
        functools.partial(middle_kernel, scale, slices, strips),
        out_shape=(
            jax.ShapeDtypeStruct((2, strips, 4, SUB, LANES), f32),
            jax.ShapeDtypeStruct((MZ, strips, TERMS, SUB, LANES), f32),
        ),
        in_specs=[smem, vmem, vmem, vmem],
        out_specs=[vmem, vmem],
        scratch_shapes=[table, table],
        compiler_params=pltpu.CompilerParams(vmem_limit_bytes=8 << 20),
        cost_estimate=pl.CostEstimate(flops=10**10, bytes_accessed=10**8, transcendentals=0),
        name="middle",
    )(brick_mask, grade_strips, amp_strips, tf_table)

    def march_ends(for_sibling, *earlier):
        return pl.pallas_call(
            functools.partial(ends_kernel, scale, pieces, slices, strips, for_sibling),
            out_shape=(half, jax.ShapeDtypeStruct((4, strips, TERMS, SUB, LANES), f32)),
            in_specs=[smem, smem] + [vmem] * 7 + [after] * len(earlier),
            out_specs=[vmem] * 2,
            scratch_shapes=[pltpu.VMEM((2, MY // LANES, 4, SUB, LANES), f32), table, table],
            compiler_params=small,
            name="ends",
        )(brick_mask, depth_rank, grade_strips, amp_strips, by_strips(near), by_strips(far), tf_table, mid, kept, *earlier)

    go, kept_go = march_ends(True)
    stay, kept_stay = march_ends(False, go)

    def swap_across(x):
        return lax.ppermute(x, "depth", [(i, i ^ 2) for i in range(pieces)])

    own, away_inner = pl.pallas_call(
        merge_kernel,
        out_shape=(piece, piece),
        in_specs=[smem, vmem, vmem],
        out_specs=[vmem, vmem],
        compiler_params=small,
        name="merge",
    )(depth_rank, stay, swap_near(go, "depth"))
    got = swap_across(away_inner)
    rim = jax.ShapeDtypeStruct((4, SUB, cols // pieces // 2), f32)

    def edges_of(which, earlier):
        return pl.pallas_call(
            functools.partial(edge_kernel, pieces, which),
            out_shape=(rim,) * len(which),
            in_specs=[smem, smem] + [vmem] * 5 + [after],
            out_specs=[vmem] * len(which),
            compiler_params=small,
            name="edges",
        )(depth_rank, lat_rank, kept, kept_stay, kept_go, pair, cross, earlier)

    across, corner, beside = edges_of((2, 3, 1), away_inner)
    (home,) = edges_of((0,), beside)
    beside = swap_near(beside, "depth")
    across = swap_across(across)
    corner = lax.ppermute(corner, "depth", [(i, i ^ 3) for i in range(pieces)])
    edges = (home, beside, across, corner)
    return pl.pallas_call(
        finish_kernel,
        out_shape=piece,
        in_specs=[smem] + [vmem] * 6,
        out_specs=vmem,
        compiler_params=small,
        name="finish",
    )(depth_rank, own, got, edges[0], edges[2], edges[3], edges[1])


def solution(mesh):
    placed = (P("depth", "lat", None), P("depth", "lat", None), P(), P("depth", "lat", None))
    return jax.shard_map(
        local, mesh=mesh, in_specs=placed, out_specs=P(None, "lat", "depth"), check_vma=False
    )
```

```python
import functools

import jax
import jax.numpy as jnp
from jax import lax
from jax.experimental import pallas as pl
from jax.experimental.pallas import tpu as pltpu
from jax.sharding import PartitionSpec as P

MZ = 8
MX = 8
MY = 256
LANES = 128
SUB = 8
TERMS = 9


def sublane(shape):
    return lax.broadcasted_iota(jnp.int32, shape, len(shape) - 2)


PLACES = ((6, 4, 2, 0), (0, 6, 4, 2))


def row_copies(fields, out_ref, sems, last):
    slices, rows = fields[0].shape[:2]
    span = slices // 4
    made = []
    for f, src in enumerate(fields):
        for q in range(4):
            here = src.at[pl.ds(span * q, span), pl.ds(rows - 2 if last else 0, 2), :]
            made.append(pltpu.make_async_copy(here, out_ref.at[f, :, pl.ds(PLACES[last][q], 2), :], sems.at[f, q]))
    return made


def start_and_wait(copies):
    for copy in copies:
        copy.start()
    for copy in copies:
        copy.wait()


def pair_kernel(lat_ref, grade_hbm, amp_hbm, pair_ref, sems):
    odd = lax.rem(lat_ref[0], 2)
    for last in (0, 1):
        @pl.when(odd == 1 - last)
        def _():
            start_and_wait(row_copies((grade_hbm, amp_hbm), pair_ref, sems, last))


def rest_kernel(lat_ref, depth_ref, grade_hbm, amp_hbm, after_ref, cross_ref, near_ref, far_ref, sems, depth_sems):
    del after_ref
    slices = grade_hbm.shape[0]
    fields = (grade_hbm, amp_hbm)
    odd = lax.rem(depth_ref[0], 2)
    parallel = []
    for f, src in enumerate(fields):
        for n, (dst, at) in enumerate(((near_ref, 1 - odd), (far_ref, odd))):
            here = src.at[pl.ds(at * (slices - 2), 2)]
            parallel.append(pltpu.make_async_copy(here, dst.at[f], depth_sems.at[f, n]))
    odd_lat = lax.rem(lat_ref[0], 2)
    for last in (0, 1):
        @pl.when(odd_lat == last)
        def _():
            start_and_wait(row_copies(fields, cross_ref, sems, last) + parallel)


def pass_on_kernel(*refs):
    del refs


def pass_on(x, *earlier):
    spec = pl.BlockSpec(memory_space=pl.ANY)
    return pl.pallas_call(
        pass_on_kernel,
        out_shape=jax.ShapeDtypeStruct(x.shape, x.dtype),
        in_specs=[spec] * (1 + len(earlier)),
        out_specs=spec,
        input_output_aliases={0: 0},
        compiler_params=pltpu.CompilerParams(vmem_limit_bytes=1 << 20),
        name="pass_on",
    )(x, *earlier)


def round_weight(w):
    return w.astype(jnp.bfloat16).astype(jnp.float32)


def stencil(m2, m1, p1, p2):
    return (m2 - p2) + 8.0 * (p1 - m1)


def fill_tables(scale, table_ref, low_ref, high_ref):
    bins = table_ref.shape[1]
    table = (table_ref[...].astype(jnp.float32) / 65535.0).astype(jnp.bfloat16).astype(jnp.float32)
    table = jnp.where(sublane(table.shape) == 3, table * scale, table)
    column = lax.broadcasted_iota(jnp.int32, table.shape, 1)
    following = jnp.where(column == bins - 1, 0.0, pltpu.roll(table, bins - 1, 1))
    for c in range(4):
        low_ref[c] = jnp.broadcast_to(table[c:c + 1, :], (SUB, bins))
        high_ref[c] = jnp.broadcast_to(following[c:c + 1, :], (SUB, bins))


class Field:
    def __init__(self, ref, slices, strips, s):
        self.ref, self.strips = ref, strips
        self.per_slice = ref.shape[0] // slices
        self.s = s

    def load(self, z, rt, ds=0, k=0):
        start = pl.multiple_of((self.s + ds) * SUB, SUB) + (z * self.per_slice + rt * self.strips * SUB + k)
        return self.ref[pl.ds(start, SUB), :]

    def columns(self, z, rt, mid, lane):
        left = jnp.where(self.s > 0, self.load(z, rt, -jnp.minimum(self.s, 1)), 0.0)
        right = jnp.where(self.s < self.strips - 1, self.load(z, rt, jnp.minimum(self.strips - 1 - self.s, 1)), 0.0)
        return stencil(
            pltpu.roll(jnp.where(lane >= LANES - 2, left, mid), 2, 1),
            pltpu.roll(jnp.where(lane >= LANES - 1, left, mid), 1, 1),
            pltpu.roll(jnp.where(lane < 1, right, mid), LANES - 1, 1),
            pltpu.roll(jnp.where(lane < 2, right, mid), LANES - 2, 1),
        )

    def rows(self, z, rt, mid, sub, roll):
        def shifted(k):
            if k > 0:
                inside = sub < SUB - k
                if rt == 0:
                    return jnp.where(inside, self.load(z, 0, 0, k), self.load(z, 1, 0, k - SUB))
                return jnp.where(inside, pltpu.roll(mid, SUB - k, 0) if roll else self.load(z, 1, 0, k), 0.0)
            inside = sub >= -k
            if rt == 1:
                return jnp.where(inside, self.load(z, 1, 0, k), self.load(z, 0, 0, SUB + k))
            return jnp.where(inside, pltpu.roll(mid, -k, 0) if roll else self.load(z, 0, 0, k), 0.0)

        return stencil(*(shifted(k) for k in (-2, -1, 1, 2)))


def classify(grade, bins, low_ref, high_ref):
    position = grade * (bins - 1.0)
    index = jnp.minimum(position.astype(jnp.int32), bins - 1)
    w_low = 1.0 - (position - index.astype(jnp.float32))
    w_high = round_weight(1.0 - w_low)
    w_low = round_weight(w_low)

    def gather(ref, c):
        return jnp.take_along_axis(ref[c], index, axis=1)

    return [w_low * gather(low_ref, c) + w_high * gather(high_ref, c) for c in range(4)]


def step(state, terms):
    red, green, blue, trans = state
    g_x, a_x, g_yz, a_yz, steep, *cls = terms
    edge = 1.0 - 12.0 * lax.rsqrt(a_x * a_x + a_yz)
    shade = 0.3 + steep * lax.rsqrt(g_x * g_x + g_yz)
    weight = trans * (cls[3] * edge)
    trans = trans - weight
    weight = weight * shade
    return (red + weight * cls[0], green + weight * cls[1], blue + weight * cls[2], trans)


def cell_terms(fields, z, rt, along, roll, bins, low_ref, high_ref):
    lane = lax.broadcasted_iota(jnp.int32, (SUB, LANES), 1)
    sub = sublane((SUB, LANES))
    parts = []
    for field, near in zip(fields, along):
        mid = field.load(z, rt)
        dy = field.columns(z, rt, mid, lane)
        dz = stencil(*near)
        parts.append((mid, field.rows(z, rt, mid, sub, roll), dy * dy + dz * dz, dz))
    (grade, g_x, g_yz, g_z), (_, a_x, a_yz, _) = parts
    cls = classify(grade, bins, low_ref, high_ref)
    return (g_x, a_x, g_yz + 36.0, a_yz + 144.0, 0.7 * jnp.abs(g_z), *cls)


KEPT_AT = ((0, 4), (6, 2))


def keep(kept_ref, zi, s, rt, zb, terms):
    rows = slice(0, 2) if rt == 0 else slice(SUB - 2, SUB)
    at = KEPT_AT[rt][zb]
    for n, term in enumerate(terms):
        kept_ref[zi, s, n, at:at + 2, :] = term[rows, :]


BLANK = (0.0, 0.0, 36.0, 144.0, 0.0, 0.0, 0.0, 0.0, 0.0)


def blank(kept_ref, zi, s, rt, zb):
    at = KEPT_AT[rt][zb]
    for n, value in enumerate(BLANK):
        kept_ref[zi, s, n, at:at + 2, :] = jnp.full((2, LANES), value, jnp.float32)


def middle_kernel(scale, slices, strips, mask_ref, grade_ref, amp_ref, table_ref, mid_ref, kept_ref, low_ref, high_ref):
    bins = table_ref.shape[1]
    fill_tables(scale, table_ref, low_ref, high_ref)
    per_block = MY // LANES
    zero = jnp.zeros((SUB, LANES), jnp.float32)

    def block(cb, carry):
        for rt in range(2):
            def march(halves):
                tiles = [cb * per_block + j for j in range(per_block)]
                fields = [[Field(ref, slices, strips, s) for ref in (grade_ref, amp_ref)] for s in tiles]
                states = [(zero, zero, zero, zero + 1.0)] * per_block
                for zb in halves:
                    for zi in range(2 - 2 * zb, MZ - 2 * zb):
                        z = zb * MZ + zi
                        for j, s in enumerate(tiles):
                            along = [[field.load(z + k, rt) for k in (-2, -1, 1, 2)] for field in fields[j]]
                            terms = cell_terms(fields[j], z, rt, along, False, bins, low_ref, high_ref)
                            keep(kept_ref, zi, s, rt, zb, terms)
                            states[j] = step(states[j], terms)
                for j, s in enumerate(tiles):
                    for zb in {0, 1} - set(halves):
                        for zi in range(2 - 2 * zb, MZ - 2 * zb):
                            blank(kept_ref, zi, s, rt, zb)
                    for c in range(4):
                        mid_ref[rt, s, c] = states[j][c]

            front, back = mask_ref[0, rt, cb] != 0, mask_ref[1, rt, cb] != 0
            pl.when(front & back)(functools.partial(march, (0, 1)))
            pl.when(front & ~back)(functools.partial(march, (0,)))
            pl.when(~front & back)(functools.partial(march, (1,)))
            pl.when(~front & ~back)(functools.partial(march, ()))
        return carry

    lax.fori_loop(0, strips // per_block, block, 0)


def ends_kernel(scale, pieces, slices, strips, for_sibling, mask_ref, depth_ref, grade_ref, amp_ref, near_ref, far_ref,
                table_ref, mid_ref, middle_kept_ref, *rest):
    out_ref, kept_ref, acc_ref, low_ref, high_ref = rest[-5:]
    bins = table_ref.shape[1]
    fill_tables(scale, table_ref, low_ref, high_ref)
    per_block = MY // LANES
    piece_strips = strips // pieces
    piece_blocks = piece_strips // per_block
    zero = jnp.zeros((SUB, LANES), jnp.float32)
    odd = jnp.broadcast_to(lax.rem(depth_ref[0], 2), (SUB, LANES)) == 1

    own_bit = lax.rem(depth_ref[0], 2)
    first_piece = 1 - own_bit if for_sibling else own_bit

    def block(n, carry):
        piece = first_piece + 2 * (n // piece_blocks)
        cb = piece * piece_blocks + lax.rem(n, piece_blocks)
        owner = lax.bitwise_xor(piece, depth_ref[0])
        full = [[mask_ref[zb, rt, cb] for rt in range(2)] for zb in range(2)]

        def march():
            for j in range(per_block):
                s = cb * per_block + j
                for n in range(TERMS):
                    for k, zi in enumerate((0, 1, MZ - 2, MZ - 1)):
                        kept_ref[k, s, n] = middle_kept_ref[zi, s, n]
            for rt in range(2):
                for j in range(per_block):
                    s = cb * per_block + j
                    fields = [Field(ref, slices, strips, s) for ref in (grade_ref, amp_ref)]
                    near, far = (Field(ref, 4, strips, s) for ref in (near_ref, far_ref))
                    state = (zero, zero, zero, zero + 1.0)
                    for zb in range(2):
                        cover = jnp.broadcast_to(full[zb][rt], (SUB, LANES)).astype(jnp.float32)
                        if zb == 1:
                            red, green, blue, trans = state
                            state = tuple(
                                value + trans * mid_ref[rt, s, c] for c, value in enumerate((red, green, blue))
                            ) + (trans * mid_ref[rt, s, 3],)
                        for zi in (0, 1) if zb == 0 else (MZ - 2, MZ - 1):
                            z = zb * MZ + zi
                            along = []
                            for f in range(2):

                                def at(z):
                                    if 0 <= z < slices:
                                        return fields[f].load(z, rt)
                                    k = 2 * f + z % slices % 2
                                    one, two = near.load(k, rt), far.load(k, rt)
                                    return jnp.where(odd, one, two) if z < 0 else jnp.where(odd, two, one)

                                along.append([at(z + k) for k in (-2, -1, 1, 2)])
                            terms = cell_terms(fields, z, rt, along, z in (0, slices - 1), bins, low_ref, high_ref)
                            terms = (*terms[:-1], terms[-1] * cover)
                            keep(kept_ref, zi if zb == 0 else zi - 4, s, rt, zb, terms)
                            state = step(state, terms)
                    for c in range(4):
                        acc_ref[rt, j, c] = state[c]

        some = (full[0][0] | full[0][1] | full[1][0] | full[1][1]) != 0
        pl.when(some)(march)

        @pl.when(jnp.logical_not(some))
        def _():
            for j in range(per_block):
                for n, value in enumerate(BLANK):
                    for k in range(4):
                        kept_ref[k, cb * per_block + j, n] = jnp.full((SUB, LANES), value, jnp.float32)
            for rt in range(2):
                for j in range(per_block):
                    for c in range(4):
                        acc_ref[rt, j, c] = zero if c < 3 else zero + 1.0

        for rt in range(2):
            for c in range(4):
                for j in range(per_block):
                    part = lax.rem(cb, piece_blocks) * MY + j * LANES
                    lanes = pl.ds(pl.multiple_of(part, LANES), LANES)
                    out_ref[owner // 2, c, rt * SUB:(rt + 1) * SUB, lanes] = acc_ref[rt, j, c]
        return carry

    lax.fori_loop(0, pieces // 2 * piece_blocks, block, 0)


def edge_kernel(pieces, which, depth_ref, lat_ref, kept_ref, stay_ref, go_ref, pair_ref, cross_ref, after_ref, *outs):
    del after_ref
    half = kept_ref.shape[0]
    strips = kept_ref.shape[1]
    sub = sublane((SUB, LANES))
    is_first = lax.rem((sub + 2) // 4, 2) == 0
    odd_lat = jnp.broadcast_to(lax.rem(lat_ref[0], 2), (SUB, LANES))
    from_pair = lax.rem(sub // 2, 2) != odd_lat
    piece_strips = strips // pieces
    packs = piece_strips // 2

    above = lax.rem(sub // 2, 2) == 0
    even_row = lax.rem(sub, 2) == 0

    own_factor = jnp.where(above, 1.0, -1.0)
    mate_factor = jnp.where(above == even_row, -8.0 * own_factor, 0.0)

    def outside(raw):
        mate = jnp.where(even_row, pltpu.roll(raw, SUB - 1, 0), pltpu.roll(raw, 1, 0))
        return own_factor * raw + mate_factor * mate

    def halo(f, zi, lanes):
        pair, cross = pair_ref[f, zi % 4, :, lanes], cross_ref[f, zi % 4, :, lanes]
        if zi < 4:
            return outside(jnp.where(from_pair, pair, cross))
        return outside(pltpu.roll(jnp.where(from_pair, cross, pair), 2, 0))

    def strip(s, ends_ref):
        lanes = pl.ds(pl.multiple_of(s * LANES, LANES), LANES)
        zero = jnp.zeros((SUB, LANES), jnp.float32)
        state = (zero, zero, zero, zero + 1.0)
        for zi in range(half):
            held, at = (kept_ref, zi) if 2 <= zi < half - 2 else (ends_ref, zi % (half - 4))
            g_x, a_x, *others = (held[at, s, n] for n in range(TERMS))
            state = step(state, (g_x + halo(0, zi, lanes), a_x + halo(1, zi, lanes), *others))
        *total, trans = state
        out = [t + trans * pltpu.roll(t, 4, 0) for t in total]
        return out + [trans * pltpu.roll(trans, 4, 0)]

    for n, out in zip(which, outs):
        p = lax.bitwise_xor(n, depth_ref[0])
        results = [strip(p * piece_strips + j, go_ref if n % 2 else stay_ref) for j in range(piece_strips)]
        for j in range(packs):
            for c, (one, two) in enumerate(zip(results[j], results[j + packs])):
                out[c, :, j * LANES:(j + 1) * LANES] = jnp.where(is_first, one, pltpu.roll(two, 4, 0))


def merge(mine, other, rank, level):
    ahead = jnp.broadcast_to(lax.rem(lax.shift_right_logical(rank, level), 2), mine[3].shape) == 0
    clear = jnp.where(ahead, mine[3], other[3])
    return [
        jnp.where(ahead, m, o) + clear * jnp.where(ahead, o, m) for m, o in zip(mine[:3], other[:3])
    ] + [mine[3] * other[3]]


def channels(ref):
    return [ref[c] for c in range(4)]


def merge_kernel(depth_ref, stay_ref, got_ref, own_ref, away_ref):
    for n, out_ref in enumerate((own_ref, away_ref)):
        for c, value in enumerate(merge(channels(stay_ref.at[n]), channels(got_ref.at[n]), depth_ref[0], 0)):
            out_ref[c] = value


def finish_kernel(depth_ref, own_ref, got_ref, home_ref, corner_ref, across_ref, beside_ref, out_ref):
    rows = out_ref.shape[1]
    rank = depth_ref[0]
    frame = merge(channels(own_ref), channels(got_ref), rank, 1)
    near = merge(channels(home_ref), channels(beside_ref), rank, 0)
    far = merge(channels(across_ref), channels(corner_ref), rank, 0)
    rim = merge(near, far, rank, 1)
    for c in range(4):
        inner, packed = frame[c], rim[c]
        if c == 3:
            inner, packed = 1.0 - inner, 1.0 - packed
        wide = jnp.concatenate([packed, pltpu.roll(packed, 4, 0)], axis=1)
        sub = sublane(wide.shape)
        out_ref[c, 0:SUB, :] = jnp.where(sub < 2, wide, inner[0:SUB, :])
        out_ref[c, rows - SUB:rows, :] = jnp.where(sub >= SUB - 2, wide, inner[rows - SUB:rows, :])


def swap_near(x, axis):
    return lax.ppermute(x, axis, [(i, i ^ 1) for i in range(lax.axis_size(axis))])


def swap_far(x, axis):
    size = lax.axis_size(axis)
    return lax.ppermute(x, axis, [(i, j) for k in range(1, size - 1, 2) for i, j in ((k, k + 1), (k + 1, k))])


def by_strips(array):
    rows, cols = array.shape[-2:]
    split = array.reshape(-1, rows // SUB, SUB, cols // LANES, LANES)
    return split.transpose(0, 1, 3, 2, 4).reshape(-1, LANES)


def local(grade_field, amplitude, tf_table, brick_mask):
    slices, rows, cols = grade_field.shape
    pieces = lax.axis_size("depth")
    assert (slices, rows, pieces) == (2 * MZ, 2 * MX, 4)
    depth_rank = lax.axis_index("depth").astype(jnp.int32).reshape(1)
    lat_rank = lax.axis_index("lat").astype(jnp.int32).reshape(1)
    f32 = jnp.float32
    vmem = pl.BlockSpec(memory_space=pltpu.VMEM)
    smem = pl.BlockSpec(memory_space=pltpu.SMEM)
    hbm = pl.BlockSpec(memory_space=pltpu.MemorySpace.HBM)
    lat_halo = jax.ShapeDtypeStruct((2, slices // 4, SUB, cols), f32)
    depth_halo = jax.ShapeDtypeStruct((2, 2, rows, cols), f32)
    hbm_only = pltpu.MemorySpace.HBM
    fields = (grade_field, amplitude)
    grade_field = pltpu.with_memory_space_constraint(grade_field, hbm_only)
    amplitude = pltpu.with_memory_space_constraint(amplitude, hbm_only)
    small = pltpu.CompilerParams(vmem_limit_bytes=4 << 20)
    after = pl.BlockSpec(memory_space=pl.ANY)
    pair = pl.pallas_call(
        pair_kernel,
        out_shape=lat_halo,
        in_specs=[smem, hbm, hbm],
        out_specs=vmem,
        scratch_shapes=[pltpu.SemaphoreType.DMA((2, 4))],
        compiler_params=small,
        name="take_pair",
    )(lat_rank, grade_field, amplitude)
    cross, near, far = pl.pallas_call(
        rest_kernel,
        out_shape=(lat_halo, depth_halo, depth_halo),
        in_specs=[smem, smem, hbm, hbm, after],
        out_specs=[vmem] * 3,
        scratch_shapes=[pltpu.SemaphoreType.DMA((2, 4)), pltpu.SemaphoreType.DMA((2, 2))],
        compiler_params=small,
        name="take_rest",
    )(lat_rank, depth_rank, grade_field, amplitude, pair)
    far = pass_on(far, cross)
    near = pass_on(near, far)
    pair = swap_near(pair, "lat")
    cross = swap_far(cross, "lat")
    near = swap_near(near, "depth")
    far = swap_far(far, "depth")
    piece = jax.ShapeDtypeStruct((4, rows, cols // pieces), f32)
    half = jax.ShapeDtypeStruct((2, *piece.shape), f32)
    scale = 4.0 / (slices * pieces)
    strips = cols // LANES
    table = pltpu.VMEM((4, SUB, tf_table.shape[1]), f32)
    grade_strips, amp_strips = by_strips(fields[0]), by_strips(fields[1])
    mid, kept = pl.pallas_call(
        functools.partial(middle_kernel, scale, slices, strips),
        out_shape=(
            jax.ShapeDtypeStruct((2, strips, 4, SUB, LANES), f32),
            jax.ShapeDtypeStruct((MZ, strips, TERMS, SUB, LANES), f32),
        ),
        in_specs=[smem, vmem, vmem, vmem],
        out_specs=[vmem, vmem],
        scratch_shapes=[table, table],
        compiler_params=pltpu.CompilerParams(vmem_limit_bytes=8 << 20),
        cost_estimate=pl.CostEstimate(flops=10**10, bytes_accessed=10**8, transcendentals=0),
        name="middle",
    )(brick_mask, grade_strips, amp_strips, tf_table)

    def march_ends(for_sibling, *earlier):
        return pl.pallas_call(
            functools.partial(ends_kernel, scale, pieces, slices, strips, for_sibling),
            out_shape=(half, jax.ShapeDtypeStruct((4, strips, TERMS, SUB, LANES), f32)),
            in_specs=[smem, smem] + [vmem] * 7 + [after] * len(earlier),
            out_specs=[vmem] * 2,
            scratch_shapes=[pltpu.VMEM((2, MY // LANES, 4, SUB, LANES), f32), table, table],
            compiler_params=small,
            name="ends",
        )(brick_mask, depth_rank, grade_strips, amp_strips, by_strips(near), by_strips(far), tf_table, mid, kept, *earlier)

    go, kept_go = march_ends(True)
    stay, kept_stay = march_ends(False, go)

    def swap_across(x):
        return lax.ppermute(x, "depth", [(i, i ^ 2) for i in range(pieces)])

    own, away_inner = pl.pallas_call(
        merge_kernel,
        out_shape=(piece, piece),
        in_specs=[smem, vmem, vmem],
        out_specs=[vmem, vmem],
        compiler_params=small,
        name="merge",
    )(depth_rank, stay, swap_near(go, "depth"))
    got = swap_across(away_inner)
    rim = jax.ShapeDtypeStruct((4, SUB, cols // pieces // 2), f32)

    def edges_of(which, earlier):
        return pl.pallas_call(
            functools.partial(edge_kernel, pieces, which),
            out_shape=(rim,) * len(which),
            in_specs=[smem, smem] + [vmem] * 5 + [after],
            out_specs=[vmem] * len(which),
            compiler_params=small,
            name="edges",
        )(depth_rank, lat_rank, kept, kept_stay, kept_go, pair, cross, earlier)

    across, corner, beside = edges_of((2, 3, 1), away_inner)
    (home,) = edges_of((0,), beside)
    beside = swap_near(beside, "depth")
    across = swap_across(across)
    corner = lax.ppermute(corner, "depth", [(i, i ^ 3) for i in range(pieces)])
    edges = (home, beside, across, corner)
    return pl.pallas_call(
        finish_kernel,
        out_shape=piece,
        in_specs=[smem] + [vmem] * 6,
        out_specs=vmem,
        compiler_params=small,
        name="finish",
    )(depth_rank, own, got, edges[0], edges[3], edges[2], edges[1])


def solution(mesh):
    placed = (P("depth", "lat", None), P("depth", "lat", None), P(), P("depth", "lat", None))
    return jax.shard_map(
        local, mesh=mesh, in_specs=placed, out_specs=P(None, "lat", "depth"), check_vma=False
    )
```
